256 devices in a mesh: hour: 16 (over y, x_lo, core), lat: 2 (over x_hi), lon: 8 (over z).
Axes of the slice: x: 4 (x_hi: 2, x_lo: 2; x = x_hi * 2 + x_lo), y: 4, z: 8, core: 2. Of those that a mesh axis runs over, the one named last changes fastest.
Arguments:
- precip: float32 [16, 1024, 4096], P('hour', 'lat', 'lon'), may hold values from 0.05 to 5
- scaling: float32 [16, 1024, 4096], P('hour', 'lat', 'lon'), may hold values from 0.5 to 2
- hour_weight: float32 [16], P('hour'), may hold values from 0.03 to 0.3
- cotangent: float32 [16, 1024, 4096], P('hour', 'lat', 'lon'), may hold values from -6 to 6
Outputs:
- grad_precip: float32 [16, 1024, 4096], P('hour', 'lat', 'lon')
- grad_scaling: float32 [16, 1024, 4096], P('hour', 'lat', 'lon')
The draws below stay inside these ranges and needn't reach their ends.
All inputs are finite; a program needn't handle non-finite values.
Results may differ from the reference program's by a relative error of at most 0.00012.
Values sent between devices are 32-bit elements; how exact they have to be, the bound alone decides.
No kernel may reach another device: no remote copies, remote signals or barrier semaphores. Data moves between devices by JAX's collectives and lax.ppermute only.
A program may use at most 64 MiB of HBM per device.

```python
import math
import jax
import jax.numpy as jnp
from jax import lax

RADIUS = 8
HOURS = 16
NLAT = 1024
NLON = 4096


def steps_of(own_key, dims, shards, low, high):
    def one(axis_at, parts):
        steps = jax.random.uniform(jax.random.fold_in(jax.random.fold_in(own_key, 6), axis_at), (parts,), jnp.float32, low / len(shards), high / len(shards))
        return jnp.repeat(jnp.exp(steps), dims[axis_at] // parts).reshape((-1,) + (1,) * (len(dims) - axis_at - 1))

    level = one(*shards[0])
    for cut in shards[1:]:
        level = level * one(*cut)
    return level


def noise(rng, extent, spread, bound, pieces=(), dtype=jnp.bfloat16):
    entries = jax.random.normal(rng, extent, jnp.float32) * spread
    if len(pieces) > 0:
        entries = steps_of(rng, extent, pieces, -0.22, 0.18) * entries
    return jnp.clip(entries, min=-bound, max=bound).astype(dtype)


def setup_inputs(seed: int = 0) -> dict:
    key_list = jax.random.split(jax.random.key(seed), 5)
    precip = jnp.clip(jnp.exp(math.log(5.0) - 4.6051702 * jax.random.uniform(key_list[0], (HOURS, NLAT, NLON), jnp.float32) ** steps_of(key_list[0], (HOURS, NLAT, NLON), ((0, 16), (1, 2), (2, 8)), -0.2, 0.2)), 0.05, 5.0)
    scaling = jnp.clip(jnp.exp(math.log(2.0) - 1.3862944 * jax.random.uniform(key_list[1], (HOURS, NLAT, NLON), jnp.float32) ** steps_of(key_list[1], (HOURS, NLAT, NLON), ((0, 16), (1, 2), (2, 8)), -0.2, 0.2)), 0.5, 2.0)
    hour_weight = jnp.clip(jnp.exp(math.log(0.3) - 2.3025852 * jax.random.uniform(key_list[2], (HOURS,), jnp.float32) ** steps_of(key_list[2], (HOURS,), ((0, 16),), -0.2, 0.2)), 0.03, 0.3)
    cotangent = noise(key_list[3], (HOURS, NLAT, NLON), 1.0, 6.0, ((0, 16), (1, 2), (2, 8)), jnp.float32)
    return dict(precip=precip, scaling=scaling, hour_weight=hour_weight, cotangent=cotangent)


PHI = 0.8
SPREAD = 50.0


def kernel_taps():
    offsets = jnp.arange(-RADIUS, RADIUS + 1).astype(jnp.float32)
    values = jnp.exp(-offsets * offsets / SPREAD)
    return values / jnp.sum(values)


def smooth(field):
    taps = kernel_taps()
    rows = field.shape[0]
    padded = jnp.pad(field, ((RADIUS, RADIUS), (0, 0)))
    across = taps[0] * padded[0:rows]
    for step in range(1, 2 * RADIUS + 1):
        across = across + taps[step] * padded[step:step + rows]
    result = taps[0] * jnp.roll(across, RADIUS, axis=1)
    for step in range(1, 2 * RADIUS + 1):
        result = result + taps[step] * jnp.roll(across, RADIUS - step, axis=1)
    return result


def forward_hour(precip_hour, scaling_hour):
    first = smooth(scaling_hour)
    lifted = jnp.power(precip_hour / first, PHI)
    second = smooth(lifted)
    return first, lifted, second


def reference(precip, scaling, hour_weight, cotangent):
    def log_part(pair):
        return jnp.log(forward_hour(pair[0], pair[1])[2])

    logb = lax.map(log_part, (precip, scaling))
    logq = jnp.sum(hour_weight[:, None, None] * logb, axis=0)
    terms = PHI * cotangent * jnp.exp(PHI * (logq[None] - logb))
    dlogq = jnp.sum(terms, axis=0)

    def back_hour(items):
        precip_hour, scaling_hour, term, weight = items
        first, lifted, second = forward_hour(precip_hour, scaling_hour)
        dsecond = (weight * dlogq - term) / second
        dlifted = smooth(dsecond)
        carried = PHI * dlifted * lifted
        return carried / precip_hour, smooth(-carried / first)

    grad_precip, grad_scaling = lax.map(back_hour, (precip, scaling, terms, hour_weight))
    return grad_precip, grad_scaling
```

```python
import numpy as np
import jax
import jax.numpy as jnp
from jax import lax
from jax.experimental import pallas as pl
from jax.experimental.pallas import tpu as pltpu
from jax.sharding import Mesh
from jax.sharding import PartitionSpec as P

RADIUS = 8
HOUR = ("hour_0", "hour_1", "hour_2")
PLANE = ("lat", "lon")
PHI = 0.8
SPREAD = 50.0

ROWS = 512
COLS = 512
WIDE = 640
EDGE = 128
TALL = ROWS + 2 * RADIUS
TALLER = ROWS + 4 * RADIUS
BLOCK = TALL // 3
PIECES = 16
PIECE = ROWS // PIECES
STRIP = 3 * RADIUS
F32 = jnp.float32
BF16 = jnp.bfloat16


def taps_of(spacing):
    offsets = np.arange(-RADIUS, RADIUS + 1).astype(np.float64)
    total = np.sum(np.exp(-offsets * offsets / SPREAD))
    return np.where(np.abs(spacing) <= RADIUS, np.exp(-spacing * spacing / SPREAD) / total, 0.0)


def halves(matrix):
    matrix = matrix.astype(np.float32)
    high = matrix.astype(jnp.bfloat16)
    low = (matrix - high.astype(np.float32)).astype(jnp.bfloat16)
    return jnp.asarray(high), jnp.asarray(low)


def row_band(size):
    outer = np.arange(size)[:, None]
    inner = np.arange(size + 2 * RADIUS)[None, :]
    return halves(taps_of((inner - outer - RADIUS).astype(np.float64)))


def col_band():
    outer = np.arange(WIDE)[:, None]
    inner = np.arange(WIDE)[None, :]
    spacing = (inner - outer + WIDE // 2) % WIDE - WIDE // 2
    return halves(taps_of(spacing.astype(np.float64)))


def split(x):
    high = x.astype(BF16)
    return high, (x - high.astype(F32)).astype(BF16)


def dot(a, b):
    return jnp.dot(a, b, preferred_element_type=F32)


def rows_pass(x, high, low):
    xh, xl = split(x)
    return dot(high[...], xh) + (dot(low[...], xh) + dot(high[...], xl))


def cols_piece(rh, rl, ch, cl, spans, out):
    total = None
    for lo, hi in spans:
        part = dot(rh[:, lo:hi], ch[lo:hi, out]) + (
            dot(rl[:, lo:hi], ch[lo:hi, out]) + dot(rh[:, lo:hi], cl[lo:hi, out])
        )
        total = part if total is None else total + part
    return total


def cols_pass(r, ch, cl, halo):
    rh, rl = split(r)
    pieces = [
        cols_piece(rh, rl, ch, cl, ((0, 384), (512, 640)), slice(0, 256)),
        cols_piece(rh, rl, ch, cl, ((128, 640),), slice(256, 512)),
    ]
    if halo:
        pieces.append(cols_piece(rh, rl, ch, cl, ((384, 640), (0, 128)), slice(512, 640)))
    return jnp.concatenate(pieces, axis=1)


def valid_part(start, count, lat):
    row = lax.broadcasted_iota(jnp.int32, (count, WIDE), 0) + start
    lane = lax.broadcasted_iota(jnp.int32, (count, WIDE), 1)
    inside = (row >= jnp.where(lat == 0, RADIUS, 0)) & (
        row < jnp.where(lat == 0, TALL, TALL - RADIUS)
    )
    return inside & ((lane < COLS + RADIUS) | (lane >= WIDE - RADIUS))


def fill_edges(ext, reach, lat, rows_in, left, right, left_corner, right_corner, side):
    zeros = jnp.zeros((reach, COLS), F32)
    lane = lax.broadcasted_iota(jnp.int32, (reach, EDGE), 1)
    corner = jnp.where(
        lane < reach, right_corner, jnp.where(lane >= EDGE - reach, left_corner, 0.0)
    )
    ext[0:reach, 0:COLS] = jnp.where(lat == 1, rows_in, zeros)
    ext[0:reach, COLS:WIDE] = jnp.where(lat == 1, corner, 0.0)
    ext[reach + ROWS : 2 * reach + ROWS, 0:COLS] = jnp.where(lat == 0, rows_in, zeros)
    ext[reach + ROWS : 2 * reach + ROWS, COLS:WIDE] = jnp.where(lat == 0, corner, 0.0)
    side[...] = jnp.zeros((EDGE, ROWS), F32)
    side[0:reach, :] = right
    side[EDGE - reach : EDGE, :] = left
    ext[reach : reach + ROWS, COLS:WIDE] = jnp.transpose(side[...])


def edges_kernel(lat_ref, scaling, precip, to_lat, to_right, to_left, corner_right, corner_left):
    lat = lat_ref[0]
    wide, narrow = 2 * RADIUS, RADIUS
    strip = jnp.concatenate(
        [
            jnp.where(lat == 0, scaling[ROWS - wide : ROWS, :], scaling[0:wide, :]),
            jnp.where(lat == 0, precip[ROWS - narrow : ROWS, :], precip[0:narrow, :]),
        ],
        axis=0,
    )
    to_lat[...] = strip
    corner_right[...] = strip[:, COLS - EDGE : COLS]
    corner_left[...] = strip[:, 0:EDGE]
    to_right[0:wide, :] = jnp.transpose(scaling[:, COLS - EDGE : COLS])[EDGE - wide : EDGE]
    to_right[wide:STRIP, :] = jnp.transpose(precip[:, COLS - EDGE : COLS])[EDGE - narrow : EDGE]
    to_left[0:wide, :] = jnp.transpose(scaling[:, 0:EDGE])[0:wide]
    to_left[wide:STRIP, :] = jnp.transpose(precip[:, 0:EDGE])[0:narrow]


def pack_kernel(weight, upstream, packed):
    for p in range(PIECES):
        for j in range(COLS // EDGE):
            packed[p, PIECE * j : PIECE * (j + 1), :] = upstream[
                PIECE * p : PIECE * (p + 1), EDGE * j : EDGE * (j + 1)
            ]
        packed[p, EDGE : EDGE + 8, :] = jnp.full((8, EDGE), weight[0], F32)


def forward_kernel(
    lat_ref, scaling, precip, lat_in, from_left, from_right, corner_l, corner_r,
    rh3, rl3, rh4, rl4, ch, cl, first, lifted, second, sx, px, side,
):
    lat = lat_ref[0]
    wide, narrow = 2 * RADIUS, RADIUS
    sx[wide : wide + ROWS, 0:COLS] = scaling[...]
    px[narrow : narrow + ROWS, 0:COLS] = precip[...]
    fill_edges(
        sx, wide, lat, lat_in[0:wide], from_left[0:wide], from_right[0:wide],
        corner_l[0:wide], corner_r[0:wide], side,
    )
    fill_edges(
        px, narrow, lat, lat_in[wide:STRIP], from_left[wide:STRIP], from_right[wide:STRIP],
        corner_l[wide:STRIP], corner_r[wide:STRIP], side,
    )
    for i in range(3):
        at = BLOCK * i
        r = rows_pass(sx[at : at + BLOCK + 2 * RADIUS, :], rh3, rl3)
        a = cols_pass(r, ch, cl, True)
        first[at : at + BLOCK, :] = a
        ratio = px[at : at + BLOCK, :] / a
        lifted[at : at + BLOCK, :] = jnp.where(
            valid_part(at, BLOCK, lat), jnp.exp(PHI * jnp.log(ratio)), 0.0
        )
    for i in range(4):
        at = EDGE * i
        r = rows_pass(lifted[at : at + EDGE + 2 * RADIUS, :], rh4, rl4)
        b = cols_pass(r, ch, cl, False)
        for q in range(EDGE // PIECE):
            for j in range(COLS // EDGE):
                second[i * (EDGE // PIECE) + q, PIECE * j : PIECE * (j + 1), :] = b[
                    PIECE * q : PIECE * (q + 1), EDGE * j : EDGE * (j + 1)
                ]


def hours_kernel(second, upstream, out):
    def one(at, carry):
        rows = pl.ds(pl.multiple_of(at * 8, 8), 8)
        logs = [jnp.log(second[h, rows, :]) for h in range(PIECES)]
        weights = [upstream[h, EDGE : EDGE + 8, :] for h in range(PIECES)]
        logq = weights[0] * logs[0]
        for h in range(1, PIECES):
            logq = logq + weights[h] * logs[h]
        terms = [
            PHI * upstream[h, rows, :] * jnp.exp(PHI * (logq - logs[h])) for h in range(PIECES)
        ]
        dlogq = terms[0]
        for h in range(1, PIECES):
            dlogq = dlogq + terms[h]
        for h in range(PIECES):
            out[h, rows, :] = (weights[h] * dlogq - terms[h]) / second[h, rows, :]
        return carry

    lax.fori_loop(0, EDGE // 8, one, 0)


def tile_column(pieces, j):
    return jnp.concatenate(
        [pieces[p, PIECE * j : PIECE * (j + 1), :] for p in range(PIECES)], axis=0
    )


def back_edges_kernel(lat_ref, pieces, to_lat, to_right, to_left, corner_right, corner_left):
    lat = lat_ref[0]
    wide = 2 * RADIUS
    last = COLS // EDGE - 1
    for j in range(last + 1):
        part = jnp.where(
            lat == 0,
            pieces[PIECES - 1, PIECE * (j + 1) - wide : PIECE * (j + 1), :],
            pieces[0, PIECE * j : PIECE * j + wide, :],
        )
        to_lat[:, EDGE * j : EDGE * (j + 1)] = part
        if j == 0:
            corner_left[...] = part
        if j == last:
            corner_right[...] = part
    to_right[...] = jnp.transpose(tile_column(pieces, last))[EDGE - wide : EDGE]
    to_left[...] = jnp.transpose(tile_column(pieces, 0))[0:wide]


def backward_kernel(
    lat_ref, pieces, precip, first, lifted, lat_in, from_left, from_right, corner_l, corner_r,
    rh3, rl3, rh4, rl4, ch, cl, grad_precip, grad_scaling, dx, vx, side,
):
    lat = lat_ref[0]
    wide = 2 * RADIUS
    for p in range(PIECES):
        for j in range(COLS // EDGE):
            dx[wide + PIECE * p : wide + PIECE * (p + 1), EDGE * j : EDGE * (j + 1)] = pieces[
                p, PIECE * j : PIECE * (j + 1), :
            ]
    fill_edges(
        dx, wide, lat, lat_in[...], from_left[...], from_right[...], corner_l[...], corner_r[...],
        side,
    )
    for i in range(3):
        at = BLOCK * i
        r = rows_pass(dx[at : at + BLOCK + 2 * RADIUS, :], rh3, rl3)
        du = cols_pass(r, ch, cl, True)
        c = PHI * du * lifted[at : at + BLOCK, :]
        vx[at : at + BLOCK, :] = jnp.where(
            valid_part(at, BLOCK, lat), -c / first[at : at + BLOCK, :], 0.0
        )
        lo = max(at, RADIUS)
        hi = min(at + BLOCK, RADIUS + ROWS)
        grad_precip[lo - RADIUS : hi - RADIUS, :] = (
            c[lo - at : hi - at, 0:COLS] / precip[lo - RADIUS : hi - RADIUS, :]
        )
    for i in range(4):
        at = EDGE * i
        r = rows_pass(vx[at : at + EDGE + 2 * RADIUS, :], rh4, rl4)
        grad_scaling[at : at + EDGE, :] = cols_pass(r, ch, cl, False)


def in_vmem(*shapes):
    return [pltpu.VMEM(shape, F32) for shape in shapes]


def call(kernel, args, outs, scratch=(), scalars=1, flops=0, name=None):
    size = sum(4 * a.size for a in args) + sum(4 * int(np.prod(o)) for o in outs)
    return pl.pallas_call(
        kernel,
        out_shape=[jax.ShapeDtypeStruct(o, F32) for o in outs],
        in_specs=[pl.BlockSpec(memory_space=pltpu.SMEM)] * scalars
        + [pl.BlockSpec(memory_space=pltpu.VMEM)] * (len(args) - scalars),
        out_specs=[pl.BlockSpec(memory_space=pltpu.VMEM)] * len(outs),
        scratch_shapes=in_vmem(*scratch),
        cost_estimate=pl.CostEstimate(flops=flops, bytes_accessed=size, transcendentals=0),
        compiler_params=pltpu.CompilerParams(vmem_limit_bytes=40 << 20),
        name=name,
    )(*args)


def moved(strip, dlat, dlon):
    lats, lons = lax.axis_size("lat"), lax.axis_size("lon")
    pairs = [
        (i * lons + j, (i + dlat) % lats * lons + (j + dlon) % lons)
        for i in range(lats)
        for j in range(lons)
    ]
    return lax.ppermute(strip, PLANE, pairs)


def exchanged(to_lat, to_right, to_left, corner_right, corner_left):
    return (
        moved(to_lat, 1, 0),
        moved(to_right, 0, 1),
        moved(to_left, 0, -1),
        moved(corner_right, 1, 1),
        moved(corner_left, 1, -1),
    )


def hours_swapped(pieces):
    return lax.all_to_all(pieces, HOUR, 0, 0, tiled=True)


def per_device(precip, scaling, hour_weight, cotangent):
    rainfall = precip[0]
    incoming = scaling[0]
    upstream = cotangent[0]
    lat = lax.axis_index("lat").astype(jnp.int32).reshape(1)
    bands = (*row_band(BLOCK), *row_band(EDGE), *col_band())
    strip, corner = (STRIP, COLS), (STRIP, EDGE)
    edges = call(
        edges_kernel, (lat, incoming, rainfall), (strip, strip, strip, corner, corner), name="edges"
    )
    (packed,) = call(
        pack_kernel, (hour_weight, upstream), ((PIECES, EDGE + 8, EDGE),), name="pack"
    )
    halo = exchanged(*edges)
    everyone = hours_swapped(packed)
    first, lifted, second = call(
        forward_kernel,
        (lat, incoming, rainfall, *halo, *bands),
        ((TALL, WIDE), (TALL, WIDE), (PIECES, EDGE, EDGE)),
        scratch=((TALLER, WIDE), (TALL, WIDE), (EDGE, ROWS)),
        flops=4 * 10**9,
        name="forward",
    )
    (dsecond,) = call(
        hours_kernel, (hours_swapped(second), everyone), ((PIECES, EDGE, EDGE),), scalars=0,
        name="hours",
    )
    pieces = hours_swapped(dsecond)
    strip, corner = (2 * RADIUS, COLS), (2 * RADIUS, EDGE)
    halo = exchanged(
        *call(
            back_edges_kernel, (lat, pieces), (strip, strip, strip, corner, corner),
            name="back_edges",
        )
    )
    grad_precip, grad_scaling = call(
        backward_kernel,
        (lat, pieces, rainfall, first, lifted, *halo, *bands),
        ((ROWS, COLS), (ROWS, COLS)),
        scratch=((TALLER, WIDE), (TALL, WIDE), (EDGE, ROWS)),
        flops=4 * 10**9,
        name="backward",
    )
    return (grad_precip[None], grad_scaling[None])


def solution(mesh):
    split_mesh = Mesh(
        mesh.devices.reshape(4, 2, 2, mesh.shape["lat"], mesh.shape["lon"]),
        ("hour_0", "hour_1", "hour_2", "lat", "lon"),
    )
    return jax.shard_map(
        per_device,
        mesh=split_mesh,
        in_specs=(P(HOUR, "lat", "lon"), P(HOUR, "lat", "lon"), P(HOUR), P(HOUR, "lat", "lon")),
        out_specs=(P(HOUR, "lat", "lon"), P(HOUR, "lat", "lon")),
        check_vma=False,
    )
```

```python
import numpy as np
import jax
import jax.numpy as jnp
from jax import lax
from jax.experimental import pallas as pl
from jax.experimental.pallas import tpu as pltpu
from jax.sharding import Mesh
from jax.sharding import PartitionSpec as P

RADIUS = 8
HOUR = ("hour_0", "hour_1", "hour_2")
PHI = 0.8
SPREAD = 50.0

ROWS = 512
COLS = 512
WIDE = 640
EDGE = 128
TALL = ROWS + 2 * RADIUS
TALLER = ROWS + 4 * RADIUS
BLOCK = TALL // 3
PIECES = 16
PIECE = ROWS // PIECES
STRIP = 3 * RADIUS
F32 = jnp.float32
BF16 = jnp.bfloat16


def taps_of(spacing):
    offsets = np.arange(-RADIUS, RADIUS + 1).astype(np.float64)
    total = np.sum(np.exp(-offsets * offsets / SPREAD))
    return np.where(np.abs(spacing) <= RADIUS, np.exp(-spacing * spacing / SPREAD) / total, 0.0)


def halves(matrix):
    matrix = matrix.astype(np.float32)
    high = matrix.astype(jnp.bfloat16)
    low = (matrix - high.astype(np.float32)).astype(jnp.bfloat16)
    return jnp.asarray(high), jnp.asarray(low)


def row_band(size):
    outer = np.arange(size)[:, None]
    inner = np.arange(size + 2 * RADIUS)[None, :]
    return halves(taps_of((inner - outer - RADIUS).astype(np.float64)))


def col_band():
    outer = np.arange(WIDE)[:, None]
    inner = np.arange(WIDE)[None, :]
    spacing = (inner - outer + WIDE // 2) % WIDE - WIDE // 2
    return halves(taps_of(spacing.astype(np.float64)))


def split(x):
    high = x.astype(BF16)
    return high, (x - high.astype(F32)).astype(BF16)


def dot(a, b):
    return jnp.dot(a, b, preferred_element_type=F32)


def rows_pass(x, high, low):
    xh, xl = split(x)
    return dot(high[...], xh) + (dot(low[...], xh) + dot(high[...], xl))


def cols_piece(rh, rl, ch, cl, spans, out):
    total = None
    for lo, hi in spans:
        part = dot(rh[:, lo:hi], ch[lo:hi, out]) + (
            dot(rl[:, lo:hi], ch[lo:hi, out]) + dot(rh[:, lo:hi], cl[lo:hi, out])
        )
        total = part if total is None else total + part
    return total


def cols_pass(r, ch, cl, halo):
    rh, rl = split(r)
    pieces = [
        cols_piece(rh, rl, ch, cl, ((0, 384), (512, 640)), slice(0, 256)),
        cols_piece(rh, rl, ch, cl, ((128, 640),), slice(256, 512)),
    ]
    if halo:
        pieces.append(cols_piece(rh, rl, ch, cl, ((384, 640), (0, 128)), slice(512, 640)))
    return jnp.concatenate(pieces, axis=1)


def valid_part(start, count, lat):
    row = lax.broadcasted_iota(jnp.int32, (count, WIDE), 0) + start
    lane = lax.broadcasted_iota(jnp.int32, (count, WIDE), 1)
    inside = (row >= jnp.where(lat == 0, RADIUS, 0)) & (
        row < jnp.where(lat == 0, TALL, TALL - RADIUS)
    )
    return inside & ((lane < COLS + RADIUS) | (lane >= WIDE - RADIUS))


def fill_edges(ext, reach, place, rows_in, even, odd, side):
    lat, parity = place[0], place[1]
    side[...] = jnp.zeros((EDGE, WIDE), F32)
    side[0:reach, :] = jnp.where(parity == 0, even, odd)
    side[EDGE - reach : EDGE, :] = jnp.where(parity == 0, odd, even)
    flat = jnp.transpose(side[...])
    corner = flat[ROWS : ROWS + reach]
    ext[reach : reach + ROWS, COLS:WIDE] = flat[0:ROWS]
    ext[0:reach, 0:COLS] = jnp.where(lat == 1, rows_in, 0.0)
    ext[0:reach, COLS:WIDE] = jnp.where(lat == 1, corner, 0.0)
    ext[reach + ROWS : 2 * reach + ROWS, 0:COLS] = jnp.where(lat == 0, rows_in, 0.0)
    ext[reach + ROWS : 2 * reach + ROWS, COLS:WIDE] = jnp.where(lat == 0, corner, 0.0)


def column_strips(reach, first_block, last_block, rows_in, parity):
    spare = jnp.zeros((EDGE - reach, EDGE), F32)
    left = jnp.transpose(jnp.concatenate([first_block, rows_in[:, 0:EDGE], spare], axis=0))
    right = jnp.transpose(
        jnp.concatenate([last_block, rows_in[:, COLS - EDGE : COLS], spare], axis=0)
    )
    left, right = left[0:reach], right[EDGE - reach : EDGE]
    return jnp.where(parity == 0, right, left), jnp.where(parity == 0, left, right)


def lat_kernel(place, scaling, precip, to_lat):
    lat = place[0]
    wide, narrow = 2 * RADIUS, RADIUS
    to_lat[0:wide, :] = jnp.where(lat == 0, scaling[ROWS - wide : ROWS, :], scaling[0:wide, :])
    to_lat[wide:STRIP, :] = jnp.where(
        lat == 0, precip[ROWS - narrow : ROWS, :], precip[0:narrow, :]
    )


def lon_kernel(place, scaling, precip, lat_in, to_even, to_odd):
    wide, narrow = 2 * RADIUS, RADIUS
    to_even[0:wide, :], to_odd[0:wide, :] = column_strips(
        wide, scaling[:, 0:EDGE], scaling[:, COLS - EDGE : COLS], lat_in[0:wide, :], place[1]
    )
    to_even[wide:STRIP, :], to_odd[wide:STRIP, :] = column_strips(
        narrow, precip[:, 0:EDGE], precip[:, COLS - EDGE : COLS], lat_in[wide:STRIP, :], place[1]
    )


def pack_kernel(weight, upstream, packed):
    for p in range(PIECES):
        for j in range(COLS // EDGE):
            packed[p, PIECE * j : PIECE * (j + 1), :] = upstream[
                PIECE * p : PIECE * (p + 1), EDGE * j : EDGE * (j + 1)
            ]
        packed[p, EDGE : EDGE + 8, :] = jnp.full((8, EDGE), weight[0], F32)


def forward_kernel(
    place, scaling, precip, lat_in, even, odd, rh3, rl3, rh4, rl4, ch, cl,
    first, lifted, second, sx, px, side,
):
    lat = place[0]
    wide, narrow = 2 * RADIUS, RADIUS
    sx[wide : wide + ROWS, 0:COLS] = scaling[...]
    px[narrow : narrow + ROWS, 0:COLS] = precip[...]
    fill_edges(sx, wide, place, lat_in[0:wide, :], even[0:wide, :], odd[0:wide, :], side)
    fill_edges(
        px, narrow, place, lat_in[wide:STRIP, :], even[wide:STRIP, :], odd[wide:STRIP, :], side
    )
    for i in range(3):
        at = BLOCK * i
        r = rows_pass(sx[at : at + BLOCK + 2 * RADIUS, :], rh3, rl3)
        a = cols_pass(r, ch, cl, True)
        first[at : at + BLOCK, :] = a
        ratio = px[at : at + BLOCK, :] / a
        lifted[at : at + BLOCK, :] = jnp.where(
            valid_part(at, BLOCK, lat), jnp.exp(PHI * jnp.log(ratio)), 0.0
        )
    for i in range(4):
        at = EDGE * i
        r = rows_pass(lifted[at : at + EDGE + 2 * RADIUS, :], rh4, rl4)
        b = cols_pass(r, ch, cl, False)
        for q in range(EDGE // PIECE):
            for j in range(COLS // EDGE):
                second[i * (EDGE // PIECE) + q, PIECE * j : PIECE * (j + 1), :] = b[
                    PIECE * q : PIECE * (q + 1), EDGE * j : EDGE * (j + 1)
                ]


def hours_kernel(second, upstream, out):
    def one(at, carry):
        rows = pl.ds(pl.multiple_of(at * 8, 8), 8)
        logs = [jnp.log(second[h, rows, :]) for h in range(PIECES)]
        weights = [upstream[h, EDGE : EDGE + 8, :] for h in range(PIECES)]
        logq = weights[0] * logs[0]
        for h in range(1, PIECES):
            logq = logq + weights[h] * logs[h]
        terms = [
            PHI * upstream[h, rows, :] * jnp.exp(PHI * (logq - logs[h])) for h in range(PIECES)
        ]
        dlogq = terms[0]
        for h in range(1, PIECES):
            dlogq = dlogq + terms[h]
        for h in range(PIECES):
            out[h, rows, :] = (weights[h] * dlogq - terms[h]) / second[h, rows, :]
        return carry

    lax.fori_loop(0, EDGE // 8, one, 0)


def tile_column(pieces, j):
    return jnp.concatenate(
        [pieces[p, PIECE * j : PIECE * (j + 1), :] for p in range(PIECES)], axis=0
    )


def back_lat_kernel(place, pieces, to_lat):
    wide = 2 * RADIUS
    for j in range(COLS // EDGE):
        to_lat[:, EDGE * j : EDGE * (j + 1)] = jnp.where(
            place[0] == 0,
            pieces[PIECES - 1, PIECE * (j + 1) - wide : PIECE * (j + 1), :],
            pieces[0, PIECE * j : PIECE * j + wide, :],
        )


def back_lon_kernel(place, pieces, lat_in, to_even, to_odd):
    to_even[...], to_odd[...] = column_strips(
        2 * RADIUS, tile_column(pieces, 0), tile_column(pieces, COLS // EDGE - 1), lat_in[...],
        place[1],
    )


def backward_kernel(
    place, pieces, precip, first, lifted, lat_in, even, odd, rh3, rl3, rh4, rl4, ch, cl,
    grad_precip, grad_scaling, dx, vx, side,
):
    lat = place[0]
    wide = 2 * RADIUS
    for p in range(PIECES):
        for j in range(COLS // EDGE):
            dx[wide + PIECE * p : wide + PIECE * (p + 1), EDGE * j : EDGE * (j + 1)] = pieces[
                p, PIECE * j : PIECE * (j + 1), :
            ]
    fill_edges(dx, wide, place, lat_in[...], even[...], odd[...], side)
    for i in range(3):
        at = BLOCK * i
        r = rows_pass(dx[at : at + BLOCK + 2 * RADIUS, :], rh3, rl3)
        du = cols_pass(r, ch, cl, True)
        c = PHI * du * lifted[at : at + BLOCK, :]
        vx[at : at + BLOCK, :] = jnp.where(
            valid_part(at, BLOCK, lat), -c / first[at : at + BLOCK, :], 0.0
        )
        lo = max(at, RADIUS)
        hi = min(at + BLOCK, RADIUS + ROWS)
        grad_precip[lo - RADIUS : hi - RADIUS, :] = (
            c[lo - at : hi - at, 0:COLS] / precip[lo - RADIUS : hi - RADIUS, :]
        )
    for i in range(4):
        at = EDGE * i
        r = rows_pass(vx[at : at + EDGE + 2 * RADIUS, :], rh4, rl4)
        grad_scaling[at : at + EDGE, :] = cols_pass(r, ch, cl, False)


def in_vmem(*shapes):
    return [pltpu.VMEM(shape, F32) for shape in shapes]


def call(kernel, args, outs, scratch=(), scalars=1, flops=0, name=None):
    size = sum(4 * a.size for a in args) + sum(4 * int(np.prod(o)) for o in outs)
    return pl.pallas_call(
        kernel,
        out_shape=[jax.ShapeDtypeStruct(o, F32) for o in outs],
        in_specs=[pl.BlockSpec(memory_space=pltpu.SMEM)] * scalars
        + [pl.BlockSpec(memory_space=pltpu.VMEM)] * (len(args) - scalars),
        out_specs=[pl.BlockSpec(memory_space=pltpu.VMEM)] * len(outs),
        scratch_shapes=in_vmem(*scratch),
        cost_estimate=pl.CostEstimate(flops=flops, bytes_accessed=size, transcendentals=0),
        compiler_params=pltpu.CompilerParams(vmem_limit_bytes=40 << 20),
        name=name,
    )(*args)


def lat_swapped(strip):
    return lax.ppermute(strip, "lat", [(0, 1), (1, 0)])


def lon_swapped(to_even, to_odd):
    count = lax.axis_size("lon")
    even = [(i, i ^ 1) for i in range(count)]
    odd = [(i, (((i - 1) % count ^ 1) + 1) % count) for i in range(count)]
    return lax.ppermute(to_even, "lon", even), lax.ppermute(to_odd, "lon", odd)


def hours_swapped(pieces):
    return lax.all_to_all(pieces, HOUR, 0, 0, tiled=True)


def per_device(precip, scaling, hour_weight, cotangent):
    rainfall = precip[0]
    incoming = scaling[0]
    upstream = cotangent[0]
    place = jnp.stack([lax.axis_index("lat"), lax.axis_index("lon") & 1]).astype(jnp.int32)
    bands = (*row_band(BLOCK), *row_band(EDGE), *col_band())
    (packed,) = call(
        pack_kernel, (hour_weight, upstream), ((PIECES, EDGE + 8, EDGE),), name="pack"
    )
    everyone = hours_swapped(packed)
    (to_lat,) = call(lat_kernel, (place, incoming, rainfall), ((STRIP, COLS),), name="lat_edges")
    lat_in = lat_swapped(to_lat)
    even, odd = lon_swapped(
        *call(
            lon_kernel, (place, incoming, rainfall, lat_in), ((STRIP, WIDE), (STRIP, WIDE)),
            name="lon_edges",
        )
    )
    first, lifted, second = call(
        forward_kernel,
        (place, incoming, rainfall, lat_in, even, odd, *bands),
        ((TALL, WIDE), (TALL, WIDE), (PIECES, EDGE, EDGE)),
        scratch=((TALLER, WIDE), (TALL, WIDE), (EDGE, WIDE)),
        flops=4 * 10**9,
        name="forward",
    )
    second, everyone = lax.optimization_barrier((second, everyone))
    (dsecond,) = call(
        hours_kernel, (hours_swapped(second), everyone), ((PIECES, EDGE, EDGE),), scalars=0,
        name="hours",
    )
    pieces = hours_swapped(dsecond)
    (to_lat,) = call(back_lat_kernel, (place, pieces), ((2 * RADIUS, COLS),), name="back_lat_edges")
    lat_in = lat_swapped(to_lat)
    even, odd = lon_swapped(
        *call(
            back_lon_kernel, (place, pieces, lat_in), ((2 * RADIUS, WIDE), (2 * RADIUS, WIDE)),
            name="back_lon_edges",
        )
    )
    grad_precip, grad_scaling = call(
        backward_kernel,
        (place, pieces, rainfall, first, lifted, lat_in, even, odd, *bands),
        ((ROWS, COLS), (ROWS, COLS)),
        scratch=((TALLER, WIDE), (TALL, WIDE), (EDGE, WIDE)),
        flops=4 * 10**9,
        name="backward",
    )
    return (grad_precip[None], grad_scaling[None])


def solution(mesh):
    split_mesh = Mesh(
        mesh.devices.reshape(4, 2, 2, mesh.shape["lat"], mesh.shape["lon"]),
        ("hour_0", "hour_1", "hour_2", "lat", "lon"),
    )
    return jax.shard_map(
        per_device,
        mesh=split_mesh,
        in_specs=(P(HOUR, "lat", "lon"), P(HOUR, "lat", "lon"), P(HOUR), P(HOUR, "lat", "lon")),
        out_specs=(P(HOUR, "lat", "lon"), P(HOUR, "lat", "lon")),
        check_vma=False,
    )
```

```python
import numpy as np
import jax
import jax.numpy as jnp
from jax import lax
from jax.experimental import pallas as pl
from jax.experimental.pallas import tpu as pltpu
from jax.sharding import Mesh
from jax.sharding import PartitionSpec as P

RADIUS = 8
HOUR = ("hour_0", "hour_1", "hour_2")
PHI = 0.8
SPREAD = 50.0

ROWS = 512
COLS = 512
WIDE = 640
EDGE = 128
TALL = ROWS + 2 * RADIUS
TALLER = ROWS + 4 * RADIUS
BLOCK = TALL // 3
PIECES = 16
PIECE = ROWS // PIECES
STRIP = 3 * RADIUS
F32 = jnp.float32
BF16 = jnp.bfloat16


def taps_of(spacing):
    offsets = np.arange(-RADIUS, RADIUS + 1).astype(np.float64)
    total = np.sum(np.exp(-offsets * offsets / SPREAD))
    return np.where(np.abs(spacing) <= RADIUS, np.exp(-spacing * spacing / SPREAD) / total, 0.0)


def halves(matrix):
    matrix = matrix.astype(np.float32)
    high = matrix.astype(jnp.bfloat16)
    low = (matrix - high.astype(np.float32)).astype(jnp.bfloat16)
    return jnp.asarray(high), jnp.asarray(low)


def row_band(size):
    outer = np.arange(size)[:, None]
    inner = np.arange(size + 2 * RADIUS)[None, :]
    return halves(taps_of((inner - outer - RADIUS).astype(np.float64)))


def col_band():
    outer = np.arange(WIDE)[:, None]
    inner = np.arange(WIDE)[None, :]
    spacing = (inner - outer + WIDE // 2) % WIDE - WIDE // 2
    return halves(taps_of(spacing.astype(np.float64)))


def split(x):
    high = x.astype(BF16)
    return high, (x - high.astype(F32)).astype(BF16)


def dot(a, b):
    return jnp.dot(a, b, preferred_element_type=F32)


def rows_pass(x, high, low):
    xh, xl = split(x)
    return dot(high[...], xh) + (dot(low[...], xh) + dot(high[...], xl))


def cols_piece(rh, rl, ch, cl, spans, out):
    total = None
    for lo, hi in spans:
        part = dot(rh[:, lo:hi], ch[lo:hi, out]) + (
            dot(rl[:, lo:hi], ch[lo:hi, out]) + dot(rh[:, lo:hi], cl[lo:hi, out])
        )
        total = part if total is None else total + part
    return total


def cols_pass(r, ch, cl, halo):
    rh, rl = split(r)
    pieces = [
        cols_piece(rh, rl, ch, cl, ((0, 384), (512, 640)), slice(0, 256)),
        cols_piece(rh, rl, ch, cl, ((128, 640),), slice(256, 512)),
    ]
    if halo:
        pieces.append(cols_piece(rh, rl, ch, cl, ((384, 640), (0, 128)), slice(512, 640)))
    return jnp.concatenate(pieces, axis=1)


def valid_part(start, count, lat):
    row = lax.broadcasted_iota(jnp.int32, (count, WIDE), 0) + start
    lane = lax.broadcasted_iota(jnp.int32, (count, WIDE), 1)
    inside = (row >= jnp.where(lat == 0, RADIUS, 0)) & (
        row < jnp.where(lat == 0, TALL, TALL - RADIUS)
    )
    return inside & ((lane < COLS + RADIUS) | (lane >= WIDE - RADIUS))


def fill_edges(ext, reach, place, rows_in, even, odd, side):
    lat, parity = place[0], place[1]
    side[...] = jnp.zeros((EDGE, WIDE), F32)
    side[0:reach, :] = jnp.where(parity == 0, even, odd)
    side[EDGE - reach : EDGE, :] = jnp.where(parity == 0, odd, even)
    flat = jnp.transpose(side[...])
    corner = flat[ROWS : ROWS + reach]
    ext[reach : reach + ROWS, COLS:WIDE] = flat[0:ROWS]
    ext[0:reach, 0:COLS] = jnp.where(lat == 1, rows_in, 0.0)
    ext[0:reach, COLS:WIDE] = jnp.where(lat == 1, corner, 0.0)
    ext[reach + ROWS : 2 * reach + ROWS, 0:COLS] = jnp.where(lat == 0, rows_in, 0.0)
    ext[reach + ROWS : 2 * reach + ROWS, COLS:WIDE] = jnp.where(lat == 0, corner, 0.0)


def column_strips(reach, first_block, last_block, rows_in, parity):
    spare = jnp.zeros((EDGE - reach, EDGE), F32)
    left = jnp.transpose(jnp.concatenate([first_block, rows_in[:, 0:EDGE], spare], axis=0))
    right = jnp.transpose(
        jnp.concatenate([last_block, rows_in[:, COLS - EDGE : COLS], spare], axis=0)
    )
    left, right = left[0:reach], right[EDGE - reach : EDGE]
    return jnp.where(parity == 0, right, left), jnp.where(parity == 0, left, right)


def lat_kernel(place, scaling, precip, to_lat, ends, sems):
    lat = place[0]
    wide, narrow = 2 * RADIUS, RADIUS
    copies = [
        pltpu.make_async_copy(src, dst, sems.at[k])
        for k, (src, dst) in enumerate(
            (
                (scaling.at[0:wide, :], ends.at[0, 0:wide, :]),
                (scaling.at[ROWS - wide : ROWS, :], ends.at[1, 0:wide, :]),
                (precip.at[0:narrow, :], ends.at[0, wide:STRIP, :]),
                (precip.at[ROWS - narrow : ROWS, :], ends.at[1, wide:STRIP, :]),
            )
        )
    ]
    for copy in copies:
        copy.start()
    for copy in copies:
        copy.wait()
    to_lat[...] = jnp.where(lat == 0, ends[1], ends[0])


def in_hbm(x):
    return pltpu.with_memory_space_constraint(x, pltpu.HBM)


def lat_strip(place, scaling, precip):
    return pl.pallas_call(
        lat_kernel,
        out_shape=jax.ShapeDtypeStruct((STRIP, COLS), F32),
        in_specs=[pl.BlockSpec(memory_space=pltpu.SMEM)]
        + [pl.BlockSpec(memory_space=pltpu.HBM)] * 2,
        out_specs=pl.BlockSpec(memory_space=pltpu.VMEM),
        scratch_shapes=[pltpu.VMEM((2, STRIP, COLS), F32), pltpu.SemaphoreType.DMA((4,))],
        compiler_params=pltpu.CompilerParams(vmem_limit_bytes=2 << 20),
        name="lat_edges",
    )(place, in_hbm(scaling), in_hbm(precip))


def lon_kernel(place, scaling, precip, lat_in, to_even, to_odd):
    wide, narrow = 2 * RADIUS, RADIUS
    to_even[0:wide, :], to_odd[0:wide, :] = column_strips(
        wide, scaling[:, 0:EDGE], scaling[:, COLS - EDGE : COLS], lat_in[0:wide, :], place[1]
    )
    to_even[wide:STRIP, :], to_odd[wide:STRIP, :] = column_strips(
        narrow, precip[:, 0:EDGE], precip[:, COLS - EDGE : COLS], lat_in[wide:STRIP, :], place[1]
    )


def pack_kernel(weight, upstream, packed):
    for p in range(PIECES):
        for j in range(COLS // EDGE):
            packed[p, PIECE * j : PIECE * (j + 1), :] = upstream[
                PIECE * p : PIECE * (p + 1), EDGE * j : EDGE * (j + 1)
            ]
        packed[p, EDGE : EDGE + 8, :] = jnp.full((8, EDGE), weight[0], F32)


def forward_kernel(
    place, scaling, precip, lat_in, even, odd, rh3, rl3, rh4, rl4, ch, cl,
    first_out, lifted_out, second_out, sx, px, side, first, lifted, second, sems,
):
    lat = place[0]
    wide, narrow = 2 * RADIUS, RADIUS
    sx[wide : wide + ROWS, 0:COLS] = scaling[...]
    px[narrow : narrow + ROWS, 0:COLS] = precip[...]
    fill_edges(sx, wide, place, lat_in[0:wide, :], even[0:wide, :], odd[0:wide, :], side)
    fill_edges(
        px, narrow, place, lat_in[wide:STRIP, :], even[wide:STRIP, :], odd[wide:STRIP, :], side
    )
    copies = []

    def sent(src, dst):
        copies.append(pltpu.make_async_copy(src, dst, sems.at[len(copies)]))
        copies[-1].start()

    for i in range(3):
        at = BLOCK * i
        r = rows_pass(sx[at : at + BLOCK + 2 * RADIUS, :], rh3, rl3)
        a = cols_pass(r, ch, cl, True)
        first[at : at + BLOCK, :] = a
        ratio = px[at : at + BLOCK, :] / a
        lifted[at : at + BLOCK, :] = jnp.where(
            valid_part(at, BLOCK, lat), jnp.exp(PHI * jnp.log(ratio)), 0.0
        )
        sent(first.at[at : at + BLOCK, :], first_out.at[at : at + BLOCK, :])
        sent(lifted.at[at : at + BLOCK, :], lifted_out.at[at : at + BLOCK, :])
    for i in range(4):
        at = EDGE * i
        r = rows_pass(lifted[at : at + EDGE + 2 * RADIUS, :], rh4, rl4)
        b = cols_pass(r, ch, cl, False)
        for q in range(EDGE // PIECE):
            for j in range(COLS // EDGE):
                second[i * (EDGE // PIECE) + q, PIECE * j : PIECE * (j + 1), :] = b[
                    PIECE * q : PIECE * (q + 1), EDGE * j : EDGE * (j + 1)
                ]
        done = slice(i * (EDGE // PIECE), (i + 1) * (EDGE // PIECE))
        sent(second.at[done], second_out.at[done])
    for copy in copies:
        copy.wait()


def hours_kernel(second, upstream, out):
    def one(at, carry):
        rows = pl.ds(pl.multiple_of(at * 8, 8), 8)
        logs = [jnp.log(second[h, rows, :]) for h in range(PIECES)]
        weights = [upstream[h, EDGE : EDGE + 8, :] for h in range(PIECES)]
        logq = weights[0] * logs[0]
        for h in range(1, PIECES):
            logq = logq + weights[h] * logs[h]
        terms = [
            PHI * upstream[h, rows, :] * jnp.exp(PHI * (logq - logs[h])) for h in range(PIECES)
        ]
        dlogq = terms[0]
        for h in range(1, PIECES):
            dlogq = dlogq + terms[h]
        for h in range(PIECES):
            out[h, rows, :] = (weights[h] * dlogq - terms[h]) / second[h, rows, :]
        return carry

    lax.fori_loop(0, EDGE // 8, one, 0)


def tile_column(pieces, j):
    return jnp.concatenate(
        [pieces[p, PIECE * j : PIECE * (j + 1), :] for p in range(PIECES)], axis=0
    )


def back_lat_kernel(place, pieces, to_lat):
    wide = 2 * RADIUS
    for j in range(COLS // EDGE):
        to_lat[:, EDGE * j : EDGE * (j + 1)] = jnp.where(
            place[0] == 0,
            pieces[PIECES - 1, PIECE * (j + 1) - wide : PIECE * (j + 1), :],
            pieces[0, PIECE * j : PIECE * j + wide, :],
        )


def back_lon_kernel(place, pieces, lat_in, to_even, to_odd):
    to_even[...], to_odd[...] = column_strips(
        2 * RADIUS, tile_column(pieces, 0), tile_column(pieces, COLS // EDGE - 1), lat_in[...],
        place[1],
    )


def backward_kernel(
    place, pieces, precip, first, lifted, lat_in, even, odd, rh3, rl3, rh4, rl4, ch, cl,
    grad_precip, grad_scaling, dx, vx, side,
):
    lat = place[0]
    wide = 2 * RADIUS
    for p in range(PIECES):
        for j in range(COLS // EDGE):
            dx[wide + PIECE * p : wide + PIECE * (p + 1), EDGE * j : EDGE * (j + 1)] = pieces[
                p, PIECE * j : PIECE * (j + 1), :
            ]
    fill_edges(dx, wide, place, lat_in[...], even[...], odd[...], side)
    for i in range(3):
        at = BLOCK * i
        r = rows_pass(dx[at : at + BLOCK + 2 * RADIUS, :], rh3, rl3)
        du = cols_pass(r, ch, cl, True)
        c = PHI * du * lifted[at : at + BLOCK, :]
        vx[at : at + BLOCK, :] = jnp.where(
            valid_part(at, BLOCK, lat), -c / first[at : at + BLOCK, :], 0.0
        )
        lo = max(at, RADIUS)
        hi = min(at + BLOCK, RADIUS + ROWS)
        grad_precip[lo - RADIUS : hi - RADIUS, :] = (
            c[lo - at : hi - at, 0:COLS] / precip[lo - RADIUS : hi - RADIUS, :]
        )
    for i in range(4):
        at = EDGE * i
        r = rows_pass(vx[at : at + EDGE + 2 * RADIUS, :], rh4, rl4)
        grad_scaling[at : at + EDGE, :] = cols_pass(r, ch, cl, False)


def in_vmem(*shapes):
    return [pltpu.VMEM(shape, F32) for shape in shapes]


def call(
    kernel, args, outs, scratch=(), scalars=1, flops=0, room=4 << 20, name=None, copies=0
):
    size = sum(4 * a.size for a in args) + sum(4 * int(np.prod(o)) for o in outs)
    where = pltpu.HBM if copies else pltpu.VMEM
    return pl.pallas_call(
        kernel,
        out_shape=[pltpu.HBM(o, F32) if copies else jax.ShapeDtypeStruct(o, F32) for o in outs],
        in_specs=[pl.BlockSpec(memory_space=pltpu.SMEM)] * scalars
        + [pl.BlockSpec(memory_space=pltpu.VMEM)] * (len(args) - scalars),
        out_specs=[pl.BlockSpec(memory_space=where)] * len(outs),
        scratch_shapes=in_vmem(*scratch)
        + ([pltpu.SemaphoreType.DMA((copies,))] if copies else []),
        cost_estimate=pl.CostEstimate(flops=flops, bytes_accessed=size, transcendentals=0),
        compiler_params=pltpu.CompilerParams(vmem_limit_bytes=room),
        name=name,
    )(*args)


def lat_swapped(strip):
    return lax.ppermute(strip, "lat", [(0, 1), (1, 0)])


def lon_swapped(to_even, to_odd):
    count = lax.axis_size("lon")
    even = [(i, i ^ 1) for i in range(count)]
    odd = [(i, (((i - 1) % count ^ 1) + 1) % count) for i in range(count)]
    return lax.ppermute(to_even, "lon", even), lax.ppermute(to_odd, "lon", odd)


def hours_swapped(pieces):
    return lax.all_to_all(pieces, HOUR, 0, 0, tiled=True)


def per_device(precip, scaling, hour_weight, cotangent):
    rainfall = precip[0]
    incoming = scaling[0]
    upstream = cotangent[0]
    place = jnp.stack([lax.axis_index("lat"), lax.axis_index("lon") & 1]).astype(jnp.int32)
    bands = (*row_band(BLOCK), *row_band(EDGE), *col_band())
    (packed,) = call(
        pack_kernel, (hour_weight, upstream), ((PIECES, EDGE + 8, EDGE),), name="pack"
    )
    lat_in = lat_swapped(lat_strip(place, incoming, rainfall))
    packed, _ = lax.optimization_barrier((packed, lat_in))
    everyone = hours_swapped(packed)
    even, odd = lon_swapped(
        *call(
            lon_kernel, (place, incoming, rainfall, lat_in), ((STRIP, WIDE), (STRIP, WIDE)),
            name="lon_edges",
        )
    )
    first, lifted, second = call(
        forward_kernel,
        (place, incoming, rainfall, lat_in, even, odd, *bands),
        ((TALL, WIDE), (TALL, WIDE), (PIECES, EDGE, EDGE)),
        scratch=(
            (TALLER, WIDE), (TALL, WIDE), (EDGE, WIDE),
            (TALL, WIDE), (TALL, WIDE), (PIECES, EDGE, EDGE),
        ),
        flops=4 * 10**9,
        room=14 << 20,
        name="forward",
        copies=10,
    )
    second, everyone = lax.optimization_barrier((second, everyone))
    (dsecond,) = call(
        hours_kernel, (hours_swapped(second), everyone), ((PIECES, EDGE, EDGE),), scalars=0,
        name="hours",
    )
    pieces = hours_swapped(dsecond)
    (to_lat,) = call(back_lat_kernel, (place, pieces), ((2 * RADIUS, COLS),), name="back_lat_edges")
    lat_in = lat_swapped(to_lat)
    even, odd = lon_swapped(
        *call(
            back_lon_kernel, (place, pieces, lat_in), ((2 * RADIUS, WIDE), (2 * RADIUS, WIDE)),
            name="back_lon_edges",
        )
    )
    grad_precip, grad_scaling = call(
        backward_kernel,
        (place, pieces, rainfall, first, lifted, lat_in, even, odd, *bands),
        ((ROWS, COLS), (ROWS, COLS)),
        scratch=((TALLER, WIDE), (TALL, WIDE), (EDGE, WIDE)),
        flops=4 * 10**9,
        room=14 << 20,
        name="backward",
    )
    return (grad_precip[None], grad_scaling[None])


def solution(mesh):
    split_mesh = Mesh(
        mesh.devices.reshape(4, 2, 2, mesh.shape["lat"], mesh.shape["lon"]),
        ("hour_0", "hour_1", "hour_2", "lat", "lon"),
    )
    return jax.shard_map(
        per_device,
        mesh=split_mesh,
        in_specs=(P(HOUR, "lat", "lon"), P(HOUR, "lat", "lon"), P(HOUR), P(HOUR, "lat", "lon")),
        out_specs=(P(HOUR, "lat", "lon"), P(HOUR, "lat", "lon")),
        check_vma=False,
    )
```

```python
import numpy as np
import jax
import jax.numpy as jnp
from jax import lax
from jax.experimental import pallas as pl
from jax.experimental.pallas import tpu as pltpu
from jax.sharding import Mesh
from jax.sharding import PartitionSpec as P

RADIUS = 8
HOUR = ("hour_0", "hour_1", "hour_2")
PHI = 0.8
SPREAD = 50.0

ROWS = 512
COLS = 512
WIDE = 640
EDGE = 128
TALL = ROWS + 2 * RADIUS
TALLER = ROWS + 4 * RADIUS
BLOCK = TALL // 3
PIECES = 16
PIECE = ROWS // PIECES
STRIP = 3 * RADIUS
F32 = jnp.float32
BF16 = jnp.bfloat16


def taps_of(spacing):
    offsets = np.arange(-RADIUS, RADIUS + 1).astype(np.float64)
    total = np.sum(np.exp(-offsets * offsets / SPREAD))
    return np.where(np.abs(spacing) <= RADIUS, np.exp(-spacing * spacing / SPREAD) / total, 0.0)


def halves(matrix):
    matrix = matrix.astype(np.float32)
    high = matrix.astype(jnp.bfloat16)
    low = (matrix - high.astype(np.float32)).astype(jnp.bfloat16)
    return jnp.asarray(high), jnp.asarray(low)


def row_band(size):
    outer = np.arange(size)[:, None]
    inner = np.arange(size + 2 * RADIUS)[None, :]
    return halves(taps_of((inner - outer - RADIUS).astype(np.float64)))


def edge_band(shift):
    outer = np.arange(2 * RADIUS)[:, None]
    inner = np.arange(2 * RADIUS)[None, :]
    return halves(taps_of((inner - outer + shift).astype(np.float64)))


def col_band():
    outer = np.arange(WIDE)[:, None]
    inner = np.arange(WIDE)[None, :]
    spacing = (inner - outer + WIDE // 2) % WIDE - WIDE // 2
    return halves(taps_of(spacing.astype(np.float64)))


def split(x):
    high = x.astype(BF16)
    return high, (x - high.astype(F32)).astype(BF16)


def dot(a, b):
    return jnp.dot(a, b, preferred_element_type=F32)


def rows_pass(x, high, low):
    xh, xl = split(x)
    return dot(high[...], xh) + (dot(low[...], xh) + dot(high[...], xl))


def cols_piece(rh, rl, ch, cl, spans, out):
    total = None
    for lo, hi in spans:
        part = dot(rh[:, lo:hi], ch[lo:hi, out]) + (
            dot(rl[:, lo:hi], ch[lo:hi, out]) + dot(rh[:, lo:hi], cl[lo:hi, out])
        )
        total = part if total is None else total + part
    return total


def cols_pass(r, ch, cl, halo):
    rh, rl = split(r)
    pieces = [
        cols_piece(rh, rl, ch, cl, ((0, 384), (512, 640)), slice(0, 256)),
        cols_piece(rh, rl, ch, cl, ((128, 640),), slice(256, 512)),
    ]
    if halo:
        pieces.append(cols_piece(rh, rl, ch, cl, ((384, 640), (0, 128)), slice(512, 640)))
    return jnp.concatenate(pieces, axis=1)


def valid_part(start, count, lat):
    row = lax.broadcasted_iota(jnp.int32, (count, WIDE), 0) + start
    lane = lax.broadcasted_iota(jnp.int32, (count, WIDE), 1)
    inside = (row >= jnp.where(lat == 0, RADIUS, 0)) & (
        row < jnp.where(lat == 0, TALL, TALL - RADIUS)
    )
    return inside & ((lane < COLS + RADIUS) | (lane >= WIDE - RADIUS))


def fill_edges(ext, reach, place, rows_in, even, odd, side):
    lat, parity = place[0], place[1]
    side[...] = jnp.zeros((EDGE, WIDE), F32)
    side[0:reach, :] = jnp.where(parity == 0, even, odd)
    side[EDGE - reach : EDGE, :] = jnp.where(parity == 0, odd, even)
    flat = jnp.transpose(side[...])
    corner = flat[ROWS : ROWS + reach]
    ext[reach : reach + ROWS, COLS:WIDE] = flat[0:ROWS]
    ext[0:reach, 0:COLS] = jnp.where(lat == 1, rows_in, 0.0)
    ext[0:reach, COLS:WIDE] = jnp.where(lat == 1, corner, 0.0)
    ext[reach + ROWS : 2 * reach + ROWS, 0:COLS] = jnp.where(lat == 0, rows_in, 0.0)
    ext[reach + ROWS : 2 * reach + ROWS, COLS:WIDE] = jnp.where(lat == 0, corner, 0.0)


def column_strips(reach, first_block, last_block, rows_in, parity):
    spare = jnp.zeros((EDGE - reach, EDGE), F32)
    left = jnp.transpose(jnp.concatenate([first_block, rows_in[:, 0:EDGE], spare], axis=0))
    right = jnp.transpose(
        jnp.concatenate([last_block, rows_in[:, COLS - EDGE : COLS], spare], axis=0)
    )
    left, right = left[0:reach], right[EDGE - reach : EDGE]
    return jnp.where(parity == 0, right, left), jnp.where(parity == 0, left, right)


def lat_kernel(place, scaling, precip, to_lat, ends, sems):
    lat = place[0]
    wide, narrow = 2 * RADIUS, RADIUS
    copies = [
        pltpu.make_async_copy(src, dst, sems.at[k])
        for k, (src, dst) in enumerate(
            (
                (scaling.at[0:wide, :], ends.at[0, 0:wide, :]),
                (scaling.at[ROWS - wide : ROWS, :], ends.at[1, 0:wide, :]),
                (precip.at[0:narrow, :], ends.at[0, wide:STRIP, :]),
                (precip.at[ROWS - narrow : ROWS, :], ends.at[1, wide:STRIP, :]),
            )
        )
    ]
    for copy in copies:
        copy.start()
    for copy in copies:
        copy.wait()
    to_lat[...] = jnp.where(lat == 0, ends[1], ends[0])


def in_hbm(x):
    return pltpu.with_memory_space_constraint(x, pltpu.HBM)


def lat_strip(place, scaling, precip):
    return pl.pallas_call(
        lat_kernel,
        out_shape=jax.ShapeDtypeStruct((STRIP, COLS), F32),
        in_specs=[pl.BlockSpec(memory_space=pltpu.SMEM)]
        + [pl.BlockSpec(memory_space=pltpu.HBM)] * 2,
        out_specs=pl.BlockSpec(memory_space=pltpu.VMEM),
        scratch_shapes=[pltpu.VMEM((2, STRIP, COLS), F32), pltpu.SemaphoreType.DMA((4,))],
        compiler_params=pltpu.CompilerParams(vmem_limit_bytes=2 << 20),
        name="lat_edges",
    )(place, in_hbm(scaling), in_hbm(precip))


def lon_kernel(place, scaling, precip, lat_in, to_even, to_odd):
    wide, narrow = 2 * RADIUS, RADIUS
    to_even[0:wide, :], to_odd[0:wide, :] = column_strips(
        wide, scaling[:, 0:EDGE], scaling[:, COLS - EDGE : COLS], lat_in[0:wide, :], place[1]
    )
    to_even[wide:STRIP, :], to_odd[wide:STRIP, :] = column_strips(
        narrow, precip[:, 0:EDGE], precip[:, COLS - EDGE : COLS], lat_in[wide:STRIP, :], place[1]
    )


def pack_kernel(weight, upstream, packed):
    for p in range(PIECES):
        for j in range(COLS // EDGE):
            packed[p, PIECE * j : PIECE * (j + 1), :] = upstream[
                PIECE * p : PIECE * (p + 1), EDGE * j : EDGE * (j + 1)
            ]
        packed[p, EDGE : EDGE + 8, :] = jnp.full((8, EDGE), weight[0], F32)


def forward_kernel(
    place, scaling, precip, lat_in, even, odd, rh3, rl3, rh4, rl4, ch, cl,
    slope_out, share_out, second_out, sx, px, side, slope, share, lifted, second, sems,
):
    lat = place[0]
    wide, narrow = 2 * RADIUS, RADIUS
    sx[wide : wide + ROWS, 0:COLS] = scaling[...]
    px[narrow : narrow + ROWS, 0:COLS] = precip[...]
    fill_edges(sx, wide, place, lat_in[0:wide, :], even[0:wide, :], odd[0:wide, :], side)
    fill_edges(
        px, narrow, place, lat_in[wide:STRIP, :], even[wide:STRIP, :], odd[wide:STRIP, :], side
    )
    copies = []

    def sent(src, dst):
        copies.append(pltpu.make_async_copy(src, dst, sems.at[len(copies)]))
        copies[-1].start()

    for i in range(3):
        at = BLOCK * i
        r = rows_pass(sx[at : at + BLOCK + 2 * RADIUS, :], rh3, rl3)
        a = cols_pass(r, ch, cl, True)
        rain = px[at : at + BLOCK, :]
        inside = valid_part(at, BLOCK, lat)
        u = jnp.where(inside, jnp.exp(PHI * jnp.log(rain / a)), 0.0)
        lifted[at : at + BLOCK, :] = u
        slope[at : at + BLOCK, :] = jnp.where(inside, -PHI * u / a, 0.0)
        lo, hi = max(at, RADIUS), min(at + BLOCK, RADIUS + ROWS)
        here = slice(lo - RADIUS, hi - RADIUS)
        share[here, :] = PHI * u[lo - at : hi - at, 0:COLS] / rain[lo - at : hi - at, 0:COLS]
        sent(slope.at[at : at + BLOCK, :], slope_out.at[at : at + BLOCK, :])
        sent(share.at[here, :], share_out.at[here, :])
    for i in range(4):
        at = EDGE * i
        r = rows_pass(lifted[at : at + EDGE + 2 * RADIUS, :], rh4, rl4)
        b = cols_pass(r, ch, cl, False)
        for q in range(EDGE // PIECE):
            for j in range(COLS // EDGE):
                second[i * (EDGE // PIECE) + q, PIECE * j : PIECE * (j + 1), :] = b[
                    PIECE * q : PIECE * (q + 1), EDGE * j : EDGE * (j + 1)
                ]
        done = slice(i * (EDGE // PIECE), (i + 1) * (EDGE // PIECE))
        sent(second.at[done], second_out.at[done])
    for copy in copies:
        copy.wait()


def hours_kernel(second, upstream, out):
    def one(at, carry):
        rows = pl.ds(pl.multiple_of(at * 8, 8), 8)
        logs = [jnp.log(second[h, rows, :]) for h in range(PIECES)]
        weights = [upstream[h, EDGE : EDGE + 8, :] for h in range(PIECES)]
        logq = weights[0] * logs[0]
        for h in range(1, PIECES):
            logq = logq + weights[h] * logs[h]
        terms = [
            PHI * upstream[h, rows, :] * jnp.exp(PHI * (logq - logs[h])) for h in range(PIECES)
        ]
        dlogq = terms[0]
        for h in range(1, PIECES):
            dlogq = dlogq + terms[h]
        for h in range(PIECES):
            out[h, rows, :] = (weights[h] * dlogq - terms[h]) / second[h, rows, :]
        return carry

    lax.fori_loop(0, EDGE // 8, one, 0)


def tile_column(pieces, j):
    return jnp.concatenate(
        [pieces[p, PIECE * j : PIECE * (j + 1), :] for p in range(PIECES)], axis=0
    )


def back_lat_kernel(place, pieces, to_lat):
    wide = 2 * RADIUS
    for j in range(COLS // EDGE):
        to_lat[:, EDGE * j : EDGE * (j + 1)] = jnp.where(
            place[0] == 0,
            pieces[PIECES - 1, PIECE * (j + 1) - wide : PIECE * (j + 1), :],
            pieces[0, PIECE * j : PIECE * j + wide, :],
        )


def back_lon_kernel(place, pieces, lat_in, to_even, to_odd):
    to_even[...], to_odd[...] = column_strips(
        2 * RADIUS, tile_column(pieces, 0), tile_column(pieces, COLS // EDGE - 1), lat_in[...],
        place[1],
    )


def back_first_kernel(pieces, slope, share, rh3, rl3, ch, cl, grad_precip, sloped, dx):
    wide = 2 * RADIUS
    dx[0:wide, :] = jnp.zeros((wide, COLS), F32)
    dx[wide + ROWS : TALLER, :] = jnp.zeros((wide, COLS), F32)
    for p in range(PIECES):
        for j in range(COLS // EDGE):
            dx[wide + PIECE * p : wide + PIECE * (p + 1), EDGE * j : EDGE * (j + 1)] = pieces[
                p, PIECE * j : PIECE * (j + 1), :
            ]
    for i in range(3):
        at = BLOCK * i
        rh, rl = split(rows_pass(dx[at : at + BLOCK + 2 * RADIUS, :], rh3, rl3))
        du = jnp.concatenate(
            [
                cols_piece(rh, rl, ch, cl, ((0, 384),), slice(0, 256)),
                cols_piece(rh, rl, ch, cl, ((128, 512),), slice(256, 512)),
                cols_piece(rh, rl, ch, cl, ((384, 512), (0, 128)), slice(512, 640)),
            ],
            axis=1,
        )
        sloped[at : at + BLOCK, :] = slope[at : at + BLOCK, :] * du
        lo, hi = max(at, RADIUS), min(at + BLOCK, RADIUS + ROWS)
        here = slice(lo - RADIUS, hi - RADIUS)
        grad_precip[here, :] = share[here, :] * du[lo - at : hi - at, 0:COLS]


def back_second_kernel(sloped, rh4, rl4, ch, cl, grad_scaling):
    for i in range(4):
        at = EDGE * i
        r = rows_pass(sloped[at : at + EDGE + 2 * RADIUS, :], rh4, rl4)
        grad_scaling[at : at + EDGE, :] = cols_pass(r, ch, cl, False)


def back_halo_kernel(
    place, lat_in, even, odd, slope, share, precip_part, scaling_part,
    rh3, rl3, rh4, rl4, ch, cl, th, tl, bh, bl,
    precip_out, scaling_out, side, column, sloped, precip_edge, scaling_edge, middle, sems,
):
    wide = 2 * RADIUS
    lat, parity = place[0], place[1]
    top = lat == 1
    inner = slice(EDGE, COLS - EDGE)
    last = slice(COLS - EDGE, COLS)
    copies = []

    def sent(src, dst):
        copies.append(pltpu.make_async_copy(src, dst, sems.at[len(copies)]))
        copies[-1].start()

    for part, out in ((precip_part, precip_out), (scaling_part, scaling_out)):
        sent(part.at[wide : ROWS - wide, inner], out.at[wide : ROWS - wide, inner])

    side[...] = jnp.zeros((EDGE, WIDE), F32)
    side[0:wide, :] = jnp.where(parity == 0, even[...], odd[...])
    side[EDGE - wide : EDGE, :] = jnp.where(parity == 0, odd[...], even[...])
    flat = jnp.transpose(side[...])
    column[0:wide, :] = jnp.zeros((wide, EDGE), F32)
    column[wide : wide + ROWS, :] = flat[0:ROWS]
    column[wide + ROWS : TALLER, :] = jnp.zeros((wide, EDGE), F32)

    def band_pass(x):
        xh, xl = split(x)
        above = dot(th[...], xh) + (dot(tl[...], xh) + dot(th[...], xl))
        below = dot(bh[...], xh) + (dot(bl[...], xh) + dot(bh[...], xl))
        return jnp.where(top, above, below)

    beyond = jnp.concatenate([lat_in[...], flat[ROWS : ROWS + wide]], axis=1)
    du = cols_pass(band_pass(beyond), ch, cl, True)
    edge = jnp.where(top, slope[0:wide, :], slope[TALL - wide : TALL, :]) * du
    added = cols_pass(band_pass(edge), ch, cl, False)
    nothing = jnp.zeros((RADIUS, COLS), F32)
    precip_top = jnp.concatenate(
        [jnp.where(top, share[0:RADIUS, :] * du[RADIUS:wide, 0:COLS], 0.0), nothing], axis=0
    )
    precip_end = jnp.concatenate(
        [nothing, jnp.where(top, 0.0, share[ROWS - RADIUS : ROWS, :] * du[0:RADIUS, 0:COLS])],
        axis=0,
    )
    ends = (
        (precip_part, precip_out, precip_top, precip_end),
        (scaling_part, scaling_out, jnp.where(top, added, 0.0), jnp.where(top, 0.0, added)),
    )
    for k, (part, out, first, final) in enumerate(ends):
        middle[2 * k] = part[0:wide, inner] + first[:, inner]
        middle[2 * k + 1] = part[ROWS - wide : ROWS, inner] + final[:, inner]
        sent(middle.at[2 * k], out.at[0:wide, inner])
        sent(middle.at[2 * k + 1], out.at[ROWS - wide : ROWS, inner])

    def finished(edges, out, first, final):
        for k, lanes in enumerate((slice(0, EDGE), last)):
            mine = slice(EDGE * k, EDGE * (k + 1))
            edges[0:wide, mine] += first[:, lanes]
            edges[ROWS - wide : ROWS, mine] += final[:, lanes]
            sent(edges.at[:, mine], out.at[:, lanes])

    for i in range(3):
        at = BLOCK * i
        rh, rl = split(rows_pass(column[at : at + BLOCK + 2 * RADIUS, :], rh3, rl3))
        spots = ((slice(0, EDGE), slice(0, EDGE)), (slice(COLS - EDGE, WIDE), slice(EDGE, 384)))
        for lanes, mine in spots:
            weights_h, weights_l = ch[COLS:WIDE, lanes], cl[COLS:WIDE, lanes]
            du = dot(rh, weights_h) + (dot(rl, weights_h) + dot(rh, weights_l))
            sloped[at : at + BLOCK, mine] = slope[at : at + BLOCK, lanes] * du
            lo, hi = max(at, RADIUS), min(at + BLOCK, RADIUS + ROWS)
            here = slice(lo - RADIUS, hi - RADIUS)
            core = slice(lanes.start, lanes.start + EDGE)
            precip_edge[here, mine.start : mine.start + EDGE] = (
                precip_part[here, core] + share[here, core] * du[lo - at : hi - at, 0:EDGE]
            )
    finished(precip_edge, precip_out, precip_top, precip_end)
    for i in range(4):
        at = EDGE * i
        rh, rl = split(rows_pass(sloped[at : at + EDGE + 2 * RADIUS, :], rh4, rl4))
        here = slice(at, at + EDGE)

        def product(mine, rows, lanes):
            weights_h, weights_l = ch[rows, lanes], cl[rows, lanes]
            return dot(rh[:, mine], weights_h) + (
                dot(rl[:, mine], weights_h) + dot(rh[:, mine], weights_l)
            )

        scaling_edge[here, 0:EDGE] = (
            scaling_part[here, 0:EDGE]
            + product(slice(0, EDGE), slice(0, EDGE), slice(0, EDGE))
            + product(slice(256, 384), slice(COLS, WIDE), slice(0, EDGE))
        )
        scaling_edge[here, EDGE : 2 * EDGE] = scaling_part[here, last] + product(
            slice(EDGE, 384), slice(COLS - EDGE, WIDE), last
        )
    finished(scaling_edge, scaling_out, ends[1][2], ends[1][3])
    for copy in copies:
        copy.wait()


def in_vmem(*shapes):
    return [pltpu.VMEM(shape, F32) for shape in shapes]


def call(
    kernel, args, outs, scratch=(), scalars=1, flops=0, room=4 << 20, name=None, copies=0
):
    size = sum(4 * a.size for a in args) + sum(4 * int(np.prod(o)) for o in outs)
    where = pltpu.HBM if copies else pltpu.VMEM
    return pl.pallas_call(
        kernel,
        out_shape=[pltpu.HBM(o, F32) if copies else jax.ShapeDtypeStruct(o, F32) for o in outs],
        in_specs=[pl.BlockSpec(memory_space=pltpu.SMEM)] * scalars
        + [pl.BlockSpec(memory_space=pltpu.VMEM)] * (len(args) - scalars),
        out_specs=[pl.BlockSpec(memory_space=where)] * len(outs),
        scratch_shapes=in_vmem(*scratch)
        + ([pltpu.SemaphoreType.DMA((copies,))] if copies else []),
        cost_estimate=pl.CostEstimate(flops=flops, bytes_accessed=size, transcendentals=0),
        compiler_params=pltpu.CompilerParams(vmem_limit_bytes=room),
        name=name,
    )(*args)


def lat_swapped(strip):
    return lax.ppermute(strip, "lat", [(0, 1), (1, 0)])


def lon_swapped(to_even, to_odd):
    count = lax.axis_size("lon")
    even = [(i, i ^ 1) for i in range(count)]
    odd = [(i, (((i - 1) % count ^ 1) + 1) % count) for i in range(count)]
    return lax.ppermute(to_even, "lon", even), lax.ppermute(to_odd, "lon", odd)


def hours_swapped(pieces):
    return lax.all_to_all(pieces, HOUR, 0, 0, tiled=True)


def per_device(precip, scaling, hour_weight, cotangent):
    rainfall = precip[0]
    incoming = scaling[0]
    upstream = cotangent[0]
    place = jnp.stack([lax.axis_index("lat"), lax.axis_index("lon") & 1]).astype(jnp.int32)
    band3, band4, around = row_band(BLOCK), row_band(EDGE), col_band()
    bands = (*band3, *band4, *around)
    (packed,) = call(
        pack_kernel, (hour_weight, upstream), ((PIECES, EDGE + 8, EDGE),), name="pack"
    )
    lat_in = lat_swapped(lat_strip(place, incoming, rainfall))
    packed, _ = lax.optimization_barrier((packed, lat_in))
    everyone = hours_swapped(packed)
    even, odd = lon_swapped(
        *call(
            lon_kernel, (place, incoming, rainfall, lat_in), ((STRIP, WIDE), (STRIP, WIDE)),
            name="lon_edges",
        )
    )
    slope, share, second = call(
        forward_kernel,
        (place, incoming, rainfall, lat_in, even, odd, *bands),
        ((TALL, WIDE), (ROWS, COLS), (PIECES, EDGE, EDGE)),
        scratch=(
            (TALLER, WIDE), (TALL, WIDE), (EDGE, WIDE),
            (TALL, WIDE), (ROWS, COLS), (TALL, WIDE), (PIECES, EDGE, EDGE),
        ),
        flops=4 * 10**9,
        room=14 << 20,
        name="forward",
        copies=10,
    )
    second, everyone = lax.optimization_barrier((second, everyone))
    (dsecond,) = call(
        hours_kernel, (hours_swapped(second), everyone), ((PIECES, EDGE, EDGE),), scalars=0,
        name="hours",
    )
    pieces = hours_swapped(dsecond)
    (to_lat,) = call(back_lat_kernel, (place, pieces), ((2 * RADIUS, COLS),), name="back_lat_edges")
    lat_in = lat_swapped(to_lat)
    even, odd = lon_swapped(
        *call(
            back_lon_kernel, (place, pieces, lat_in), ((2 * RADIUS, WIDE), (2 * RADIUS, WIDE)),
            name="back_lon_edges",
        )
    )
    precip_part, sloped = call(
        back_first_kernel,
        (pieces, slope, share, *band3, *around),
        ((ROWS, COLS), (TALL, WIDE)),
        scratch=((TALLER, COLS),),
        scalars=0,
        flops=2 * 10**9,
        room=14 << 20,
        name="back_first",
    )
    (scaling_part,) = call(
        back_second_kernel, (sloped, *band4, *around), ((ROWS, COLS),), scalars=0,
        flops=2 * 10**9, room=14 << 20, name="back_second",
    )
    grad_precip, grad_scaling = call(
        back_halo_kernel,
        (
            place, lat_in, even, odd, slope, share, precip_part, scaling_part, *bands,
            *edge_band(-RADIUS), *edge_band(RADIUS),
        ),
        ((ROWS, COLS), (ROWS, COLS)),
        scratch=(
            (EDGE, WIDE), (TALLER, EDGE), (TALL, 384), (ROWS, 2 * EDGE), (ROWS, 2 * EDGE),
            (4, 2 * RADIUS, 2 * EDGE),
        ),
        flops=10**9,
        room=14 << 20,
        name="back_halo",
        copies=10,
    )
    return (grad_precip[None], grad_scaling[None])


def solution(mesh):
    split_mesh = Mesh(
        mesh.devices.reshape(4, 2, 2, mesh.shape["lat"], mesh.shape["lon"]),
        ("hour_0", "hour_1", "hour_2", "lat", "lon"),
    )
    return jax.shard_map(
        per_device,
        mesh=split_mesh,
        in_specs=(P(HOUR, "lat", "lon"), P(HOUR, "lat", "lon"), P(HOUR), P(HOUR, "lat", "lon")),
        out_specs=(P(HOUR, "lat", "lon"), P(HOUR, "lat", "lon")),
        check_vma=False,
    )
```

```python
import numpy as np
import jax
import jax.numpy as jnp
from jax import lax
from jax.experimental import pallas as pl
from jax.experimental.pallas import tpu as pltpu
from jax.sharding import Mesh
from jax.sharding import PartitionSpec as P

RADIUS = 8
HOUR = ("hour_0", "hour_1", "hour_2")
PHI = 0.8
SPREAD = 50.0

ROWS = 512
COLS = 512
WIDE = 640
EDGE = 128
TALL = ROWS + 2 * RADIUS
TALLER = ROWS + 4 * RADIUS
BLOCK = TALL // 3
PIECES = 16
PIECE = ROWS // PIECES
STRIP = 3 * RADIUS
F32 = jnp.float32
BF16 = jnp.bfloat16


def taps_of(spacing):
    offsets = np.arange(-RADIUS, RADIUS + 1).astype(np.float64)
    total = np.sum(np.exp(-offsets * offsets / SPREAD))
    return np.where(np.abs(spacing) <= RADIUS, np.exp(-spacing * spacing / SPREAD) / total, 0.0)


def halves(matrix):
    matrix = matrix.astype(np.float32)
    high = matrix.astype(jnp.bfloat16)
    low = (matrix - high.astype(np.float32)).astype(jnp.bfloat16)
    return jnp.asarray(high), jnp.asarray(low)


def row_band(size):
    outer = np.arange(size)[:, None]
    inner = np.arange(size + 2 * RADIUS)[None, :]
    return halves(taps_of((inner - outer - RADIUS).astype(np.float64)))


def edge_bands():
    outer = np.arange(2 * RADIUS)[:, None]
    inner = np.arange(2 * RADIUS)[None, :]
    low = taps_of((inner - outer - RADIUS).astype(np.float64))
    high = taps_of((inner - outer + RADIUS).astype(np.float64))
    stacks = np.zeros((2, 48, 48))
    for lat, along in enumerate((high, low)):
        for k, band in enumerate((along, low, high)):
            stacks[lat, 16 * k : 16 * (k + 1), 16 * k : 16 * (k + 1)] = band
    return halves(stacks)


def col_band():
    outer = np.arange(WIDE)[:, None]
    inner = np.arange(WIDE)[None, :]
    spacing = (inner - outer + WIDE // 2) % WIDE - WIDE // 2
    return halves(taps_of(spacing.astype(np.float64)))


def split(x):
    high = x.astype(BF16)
    return high, (x - high.astype(F32)).astype(BF16)


def dot(a, b):
    return jnp.dot(a, b, preferred_element_type=F32)


def rows_pass(x, high, low):
    xh, xl = split(x)
    return dot(high[...], xh) + (dot(low[...], xh) + dot(high[...], xl))


def cols_piece(rh, rl, ch, cl, spans, out):
    total = None
    for lo, hi in spans:
        part = dot(rh[:, lo:hi], ch[lo:hi, out]) + (
            dot(rl[:, lo:hi], ch[lo:hi, out]) + dot(rh[:, lo:hi], cl[lo:hi, out])
        )
        total = part if total is None else total + part
    return total


def cols_pass(r, ch, cl, halo):
    rh, rl = split(r)
    pieces = [
        cols_piece(rh, rl, ch, cl, ((0, 384), (512, 640)), slice(0, 256)),
        cols_piece(rh, rl, ch, cl, ((128, 640),), slice(256, 512)),
    ]
    if halo:
        pieces.append(cols_piece(rh, rl, ch, cl, ((384, 640), (0, 128)), slice(512, 640)))
    return jnp.concatenate(pieces, axis=1)


def valid_part(start, count, lat):
    row = lax.broadcasted_iota(jnp.int32, (count, WIDE), 0) + start
    lane = lax.broadcasted_iota(jnp.int32, (count, WIDE), 1)
    inside = (row >= jnp.where(lat == 0, RADIUS, 0)) & (
        row < jnp.where(lat == 0, TALL, TALL - RADIUS)
    )
    return inside & ((lane < COLS + RADIUS) | (lane >= WIDE - RADIUS))


def my_lat():
    return lax.axis_index("lat")


def my_parity():
    return lax.axis_index("lon") & 1


def fill_edges(ext, reach, rows_in, even, odd, side):
    lat, parity = my_lat(), my_parity()
    side[...] = jnp.zeros((EDGE, WIDE), F32)
    side[0:reach, :] = jnp.where(parity == 0, even, odd)
    side[EDGE - reach : EDGE, :] = jnp.where(parity == 0, odd, even)
    flat = jnp.transpose(side[...])
    corner = flat[ROWS : ROWS + reach]
    ext[reach : reach + ROWS, COLS:WIDE] = flat[0:ROWS]
    ext[0:reach, 0:COLS] = jnp.where(lat == 1, rows_in, 0.0)
    ext[0:reach, COLS:WIDE] = jnp.where(lat == 1, corner, 0.0)
    ext[reach + ROWS : 2 * reach + ROWS, 0:COLS] = jnp.where(lat == 0, rows_in, 0.0)
    ext[reach + ROWS : 2 * reach + ROWS, COLS:WIDE] = jnp.where(lat == 0, corner, 0.0)


def column_strips(reach, first_block, last_block, rows_in, parity):
    spare = jnp.zeros((EDGE - reach, EDGE), F32)
    left = jnp.transpose(jnp.concatenate([first_block, rows_in[:, 0:EDGE], spare], axis=0))
    right = jnp.transpose(
        jnp.concatenate([last_block, rows_in[:, COLS - EDGE : COLS], spare], axis=0)
    )
    left, right = left[0:reach], right[EDGE - reach : EDGE]
    return jnp.where(parity == 0, right, left), jnp.where(parity == 0, left, right)


def lat_kernel(scaling, precip, to_lat, ends, sems):
    lat = my_lat()
    wide, narrow = 2 * RADIUS, RADIUS
    copies = [
        pltpu.make_async_copy(src, dst, sems.at[k])
        for k, (src, dst) in enumerate(
            (
                (scaling.at[0:wide, :], ends.at[0, 0:wide, :]),
                (scaling.at[ROWS - wide : ROWS, :], ends.at[1, 0:wide, :]),
                (precip.at[0:narrow, :], ends.at[0, wide:STRIP, :]),
                (precip.at[ROWS - narrow : ROWS, :], ends.at[1, wide:STRIP, :]),
            )
        )
    ]
    for copy in copies:
        copy.start()
    for copy in copies:
        copy.wait()
    to_lat[...] = jnp.where(lat == 0, ends[1], ends[0])


def in_hbm(x):
    return pltpu.with_memory_space_constraint(x, pltpu.HBM)


def lat_strip(scaling, precip):
    return pl.pallas_call(
        lat_kernel,
        out_shape=jax.ShapeDtypeStruct((STRIP, COLS), F32),
        in_specs=[pl.BlockSpec(memory_space=pltpu.HBM)] * 2,
        out_specs=pl.BlockSpec(memory_space=pltpu.VMEM),
        scratch_shapes=[pltpu.VMEM((2, STRIP, COLS), F32), pltpu.SemaphoreType.DMA((4,))],
        compiler_params=pltpu.CompilerParams(vmem_limit_bytes=2 << 20),
        name="lat_edges",
    )(in_hbm(scaling), in_hbm(precip))


def lon_kernel(scaling, precip, lat_hbm, to_even, to_odd, lat_in, sem):
    pltpu.make_async_copy(lat_hbm, lat_in, sem).start()
    pltpu.make_async_copy(lat_hbm, lat_in, sem).wait()
    wide, narrow = 2 * RADIUS, RADIUS
    to_even[0:wide, :], to_odd[0:wide, :] = column_strips(
        wide, scaling[:, 0:EDGE], scaling[:, COLS - EDGE : COLS], lat_in[0:wide, :], my_parity()
    )
    to_even[wide:STRIP, :], to_odd[wide:STRIP, :] = column_strips(
        narrow, precip[:, 0:EDGE], precip[:, COLS - EDGE : COLS], lat_in[wide:STRIP, :], my_parity()
    )


def pack_kernel(weight, upstream, packed):
    for p in range(PIECES):
        for j in range(COLS // EDGE):
            packed[p, PIECE * j : PIECE * (j + 1), :] = upstream[
                PIECE * p : PIECE * (p + 1), EDGE * j : EDGE * (j + 1)
            ]
        packed[p, EDGE : EDGE + 8, :] = jnp.full((8, EDGE), weight[0], F32)


def forward_kernel(
    scaling, precip, lat_hbm, even, odd, rh3, rl3, rh4, rl4, ch, cl,
    slope_out, share_out, second_out, sx, px, side, slope, share, lifted, second, lat_in, sems,
):
    lat = my_lat()
    wide, narrow = 2 * RADIUS, RADIUS
    fetch = pltpu.make_async_copy(lat_hbm, lat_in, sems.at[10])
    fetch.start()
    sx[wide : wide + ROWS, 0:COLS] = scaling[...]
    px[narrow : narrow + ROWS, 0:COLS] = precip[...]
    fetch.wait()
    fill_edges(sx, wide, lat_in[0:wide, :], even[0:wide, :], odd[0:wide, :], side)
    fill_edges(px, narrow, lat_in[wide:STRIP, :], even[wide:STRIP, :], odd[wide:STRIP, :], side)
    copies = []

    def sent(src, dst):
        copies.append(pltpu.make_async_copy(src, dst, sems.at[len(copies)]))
        copies[-1].start()

    for i in range(3):
        at = BLOCK * i
        r = rows_pass(sx[at : at + BLOCK + 2 * RADIUS, :], rh3, rl3)
        a = cols_pass(r, ch, cl, True)
        rain = px[at : at + BLOCK, :]
        inside = valid_part(at, BLOCK, lat)
        u = jnp.where(inside, jnp.exp(PHI * jnp.log(rain / a)), 0.0)
        lifted[at : at + BLOCK, :] = u
        slope[at : at + BLOCK, :] = jnp.where(inside, -PHI * u / a, 0.0)
        lo, hi = max(at, RADIUS), min(at + BLOCK, RADIUS + ROWS)
        here = slice(lo - RADIUS, hi - RADIUS)
        share[here, :] = PHI * u[lo - at : hi - at, 0:COLS] / rain[lo - at : hi - at, 0:COLS]
        sent(slope.at[at : at + BLOCK, :], slope_out.at[at : at + BLOCK, :])
        sent(share.at[here, :], share_out.at[here, :])
    for i in range(4):
        at = EDGE * i
        r = rows_pass(lifted[at : at + EDGE + 2 * RADIUS, :], rh4, rl4)
        b = cols_pass(r, ch, cl, False)
        for q in range(EDGE // PIECE):
            for j in range(COLS // EDGE):
                second[i * (EDGE // PIECE) + q, PIECE * j : PIECE * (j + 1), :] = b[
                    PIECE * q : PIECE * (q + 1), EDGE * j : EDGE * (j + 1)
                ]
        done = slice(i * (EDGE // PIECE), (i + 1) * (EDGE // PIECE))
        sent(second.at[done], second_out.at[done])
    for copy in copies:
        copy.wait()


def hours_kernel(second, upstream, out):
    def one(at, carry):
        rows = pl.ds(pl.multiple_of(at * 8, 8), 8)
        logs = [jnp.log(second[h, rows, :]) for h in range(PIECES)]
        weights = [upstream[h, EDGE : EDGE + 8, :] for h in range(PIECES)]
        logq = weights[0] * logs[0]
        for h in range(1, PIECES):
            logq = logq + weights[h] * logs[h]
        terms = [
            PHI * upstream[h, rows, :] * jnp.exp(PHI * (logq - logs[h])) for h in range(PIECES)
        ]
        dlogq = terms[0]
        for h in range(1, PIECES):
            dlogq = dlogq + terms[h]
        for h in range(PIECES):
            out[h, rows, :] = (weights[h] * dlogq - terms[h]) / second[h, rows, :]
        return carry

    lax.fori_loop(0, EDGE // 8, one, 0)


def tile_column(pieces, j):
    return jnp.concatenate(
        [pieces[p, PIECE * j : PIECE * (j + 1), :] for p in range(PIECES)], axis=0
    )


def back_lat_kernel(pieces, to_lat):
    wide = 2 * RADIUS
    for j in range(COLS // EDGE):
        to_lat[:, EDGE * j : EDGE * (j + 1)] = jnp.where(
            my_lat() == 0,
            pieces[PIECES - 1, PIECE * (j + 1) - wide : PIECE * (j + 1), :],
            pieces[0, PIECE * j : PIECE * j + wide, :],
        )


def back_lon_kernel(pieces, lat_in, to_even, to_odd):
    to_even[...], to_odd[...] = column_strips(
        2 * RADIUS, tile_column(pieces, 0), tile_column(pieces, COLS // EDGE - 1), lat_in[...],
        my_parity(),
    )


def coefficient_strips(slope, share, slope_edge, share_edge):
    wide = 2 * RADIUS
    top = my_lat() == 1
    nothing = jnp.zeros((RADIUS, COLS), F32)
    first, last = slice(0, EDGE), slice(COLS - EDGE, COLS)

    def turned(block):
        gap = jnp.zeros((WIDE - TALL, EDGE), F32)
        return jnp.transpose(jnp.concatenate([block[RADIUS:TALL], gap, block[0:RADIUS]], axis=0))

    near = lax.broadcasted_iota(jnp.int32, (TALL, EDGE), 1) < EDGE // 2
    tile = turned(jnp.where(near, slope[:, first], slope[:, last]))
    halo = turned(slope[:, COLS:WIDE])
    slope_edge[0:wide, :] = jnp.where(top, slope[0:wide, :], slope[TALL - wide : TALL, :])
    slope_edge[16:24, :] = halo[EDGE - RADIUS : EDGE]
    slope_edge[24:32, :] = tile[0:RADIUS]
    slope_edge[32:40, :] = tile[EDGE - RADIUS : EDGE]
    slope_edge[40:48, :] = halo[0:RADIUS]
    tile = jnp.transpose(jnp.where(near[0:ROWS], share[:, first], share[:, last]))
    share_edge[...] = jnp.zeros((48, WIDE), F32)
    share_edge[0:RADIUS, 0:COLS] = jnp.where(top, nothing, share[ROWS - RADIUS : ROWS, :])
    share_edge[RADIUS:wide, 0:COLS] = jnp.where(top, share[0:RADIUS, :], nothing)
    share_edge[24:32, 0:COLS] = tile[0:RADIUS]
    share_edge[32:40, 0:COLS] = tile[EDGE - RADIUS : EDGE]


def back_first_kernel(
    pieces, slope, share, rh3, rl3, ch, cl, grad_precip, sloped, slope_edge, share_edge, dx
):
    coefficient_strips(slope, share, slope_edge, share_edge)
    wide = 2 * RADIUS
    dx[0:wide, :] = jnp.zeros((wide, COLS), F32)
    dx[wide + ROWS : TALLER, :] = jnp.zeros((wide, COLS), F32)
    for p in range(PIECES):
        for j in range(COLS // EDGE):
            dx[wide + PIECE * p : wide + PIECE * (p + 1), EDGE * j : EDGE * (j + 1)] = pieces[
                p, PIECE * j : PIECE * (j + 1), :
            ]
    for i in range(3):
        at = BLOCK * i
        rh, rl = split(rows_pass(dx[at : at + BLOCK + 2 * RADIUS, :], rh3, rl3))
        du = jnp.concatenate(
            [
                cols_piece(rh, rl, ch, cl, ((0, 384),), slice(0, 256)),
                cols_piece(rh, rl, ch, cl, ((128, 512),), slice(256, 512)),
                cols_piece(rh, rl, ch, cl, ((384, 512), (0, 128)), slice(512, 640)),
            ],
            axis=1,
        )
        sloped[at : at + BLOCK, :] = slope[at : at + BLOCK, :] * du
        lo, hi = max(at, RADIUS), min(at + BLOCK, RADIUS + ROWS)
        here = slice(lo - RADIUS, hi - RADIUS)
        grad_precip[here, :] = share[here, :] * du[lo - at : hi - at, 0:COLS]


def back_second_kernel(sloped, rh4, rl4, ch, cl, grad_scaling):
    for i in range(4):
        at = EDGE * i
        r = rows_pass(sloped[at : at + EDGE + 2 * RADIUS, :], rh4, rl4)
        grad_scaling[at : at + EDGE, :] = cols_pass(r, ch, cl, False)


def around_pass(x):
    taps = taps_of(np.arange(RADIUS + 1).astype(np.float64))
    total = float(taps[0]) * x
    for d in range(1, RADIUS + 1):
        total += float(taps[d]) * (pltpu.roll(x, d, 1) + pltpu.roll(x, WIDE - d, 1))
    return total


def back_halo_kernel(
    lat_in, even, odd, slope_edge, share_edge, precip_part, scaling_part, dh, dl,
    precip_out, scaling_out, strips, square, flat, precip_edge, scaling_edge, middle, sems,
):
    wide = 2 * RADIUS
    lat, parity = my_lat(), my_parity()
    top = lat == 1
    inner = slice(EDGE, COLS - EDGE)
    last = slice(COLS - EDGE, COLS)
    copies = []

    def sent(src, dst):
        copies.append(pltpu.make_async_copy(src, dst, sems.at[len(copies)]))
        copies[-1].start()

    for part, out in ((precip_part, precip_out), (scaling_part, scaling_out)):
        sent(part.at[wide : ROWS - wide, inner], out.at[wide : ROWS - wide, inner])

    right = jnp.where(parity == 0, even[...], odd[...])
    left = jnp.where(parity == 0, odd[...], even[...])
    square[...] = jnp.zeros((EDGE, EDGE), F32)
    square[0:wide, :] = right[:, COLS:WIDE]
    square[EDGE - wide : EDGE, :] = left[:, COLS:WIDE]
    strips[...] = jnp.zeros((48, WIDE), F32)
    strips[0:16, 0:COLS] = lat_in[...]
    strips[0:16, COLS:WIDE] = jnp.transpose(square[...])[0:wide]
    strips[16:32, 0:COLS] = left[:, 0:COLS]
    strips[32:48, 0:COLS] = right[:, 0:COLS]
    band_h, band_l = dh[lat], dl[lat]

    def smoothed(x):
        xh, xl = split(x)
        return around_pass(dot(band_h, xh) + (dot(band_l, xh) + dot(band_h, xl)))

    du = smoothed(strips[...])
    precip_more = share_edge[...] * du
    scaling_more = smoothed(slope_edge[...] * du)
    nothing = jnp.zeros((RADIUS, COLS), F32)
    near = lax.broadcasted_iota(jnp.int32, (ROWS, EDGE), 1) < EDGE // 2

    def finished(k, part, out, edges, reach, low, high, first, final):
        flat[...] = jnp.zeros((EDGE, ROWS), F32)
        flat[0:reach, :] = low
        flat[EDGE - reach : EDGE, :] = high
        turned = jnp.transpose(flat[...])
        middle[2 * k] = part[0:wide, inner] + first[:, inner]
        middle[2 * k + 1] = part[ROWS - wide : ROWS, inner] + final[:, inner]
        sent(middle.at[2 * k], out.at[0:wide, inner])
        sent(middle.at[2 * k + 1], out.at[ROWS - wide : ROWS, inner])
        edges[:, 0:EDGE] = part[:, 0:EDGE] + jnp.where(near, turned, 0.0)
        edges[:, EDGE : 2 * EDGE] = part[:, last] + jnp.where(near, 0.0, turned)
        for q, lanes in enumerate((slice(0, EDGE), last)):
            mine = slice(EDGE * q, EDGE * (q + 1))
            edges[0:wide, mine] += first[:, lanes]
            edges[ROWS - wide : ROWS, mine] += final[:, lanes]
            sent(edges.at[:, mine], out.at[:, lanes])

    finished(
        0, precip_part, precip_out, precip_edge, RADIUS,
        precip_more[24:32, 0:COLS], precip_more[32:40, 0:COLS],
        jnp.concatenate([precip_more[RADIUS:wide, 0:COLS], nothing], axis=0),
        jnp.concatenate([nothing, precip_more[0:RADIUS, 0:COLS]], axis=0),
    )
    added = scaling_more[0:wide, 0:COLS]
    finished(
        1, scaling_part, scaling_out, scaling_edge, wide,
        scaling_more[16:32, 0:COLS], scaling_more[32:48, 0:COLS],
        jnp.where(top, added, 0.0), jnp.where(top, 0.0, added),
    )
    for copy in copies:
        copy.wait()


def in_vmem(*shapes):
    return [pltpu.VMEM(shape, F32) for shape in shapes]


def call(
    kernel, args, outs, scratch=(), scalars=0, flops=0, room=4 << 20, name=None, copies=0,
    far=(), out_hbm=False, single=False,
):
    size = sum(4 * a.size for a in args) + sum(4 * int(np.prod(o)) for o in outs)
    where = pltpu.HBM if out_hbm else pltpu.VMEM
    spaces = [
        pltpu.SMEM if k < scalars else pltpu.HBM if k in far else pltpu.VMEM
        for k in range(len(args))
    ]
    sems = [pltpu.SemaphoreType.DMA((copies,))] if copies else []
    return pl.pallas_call(
        kernel,
        out_shape=[pltpu.HBM(o, F32) if out_hbm else jax.ShapeDtypeStruct(o, F32) for o in outs],
        in_specs=[pl.BlockSpec(memory_space=space) for space in spaces],
        out_specs=[pl.BlockSpec(memory_space=where)] * len(outs),
        scratch_shapes=in_vmem(*scratch) + sems + [pltpu.SemaphoreType.DMA] * single,
        cost_estimate=pl.CostEstimate(flops=flops, bytes_accessed=size, transcendentals=0),
        compiler_params=pltpu.CompilerParams(vmem_limit_bytes=room),
        name=name,
    )(*args)


def lat_swapped(strip):
    return lax.ppermute(strip, "lat", [(0, 1), (1, 0)])


def lon_swapped(to_even, to_odd):
    count = lax.axis_size("lon")
    even = [(i, i ^ 1) for i in range(count)]
    odd = [(i, (((i - 1) % count ^ 1) + 1) % count) for i in range(count)]
    return lax.ppermute(to_even, "lon", even), lax.ppermute(to_odd, "lon", odd)


def hours_swapped(pieces):
    return lax.all_to_all(pieces, HOUR, 0, 0, tiled=True)


def per_device(precip, scaling, hour_weight, cotangent):
    rainfall = precip[0]
    incoming = scaling[0]
    upstream = cotangent[0]
    band3, band4, around = row_band(BLOCK), row_band(EDGE), col_band()
    bands = (*band3, *band4, *around)
    (packed,) = call(
        pack_kernel, (hour_weight, upstream), ((PIECES, EDGE + 8, EDGE),), scalars=1, name="pack"
    )
    lat_in = lat_swapped(lat_strip(incoming, rainfall))
    packed, _ = lax.optimization_barrier((packed, lat_in))
    everyone = hours_swapped(packed)
    even, odd = lon_swapped(
        *call(
            lon_kernel, (incoming, rainfall, in_hbm(lat_in)), ((STRIP, WIDE), (STRIP, WIDE)),
            scratch=((STRIP, COLS),), copies=0, far=(2,), single=True, name="lon_edges",
        )
    )
    slope, share, second = call(
        forward_kernel,
        (incoming, rainfall, in_hbm(lat_in), even, odd, *bands),
        ((TALL, WIDE), (ROWS, COLS), (PIECES, EDGE, EDGE)),
        scratch=(
            (TALLER, WIDE), (TALL, WIDE), (EDGE, WIDE),
            (TALL, WIDE), (ROWS, COLS), (TALL, WIDE), (PIECES, EDGE, EDGE), (STRIP, COLS),
        ),
        flops=4 * 10**9,
        room=14 << 20,
        name="forward",
        copies=11,
        far=(2,),
        out_hbm=True,
    )
    second, everyone = lax.optimization_barrier((second, everyone))
    (dsecond,) = call(
        hours_kernel, (hours_swapped(second), everyone), ((PIECES, EDGE, EDGE),),
        name="hours",
    )
    pieces = hours_swapped(dsecond)
    (to_lat,) = call(back_lat_kernel, (pieces,), ((2 * RADIUS, COLS),), name="back_lat_edges")
    lat_in = lat_swapped(to_lat)
    even, odd = lon_swapped(
        *call(
            back_lon_kernel, (pieces, lat_in), ((2 * RADIUS, WIDE), (2 * RADIUS, WIDE)),
            name="back_lon_edges",
        )
    )
    precip_part, sloped, slope_edge, share_edge = call(
        back_first_kernel,
        (pieces, slope, share, *band3, *around),
        ((ROWS, COLS), (TALL, WIDE), (48, WIDE), (48, WIDE)),
        scratch=((TALLER, COLS),),
        flops=2 * 10**9,
        room=14 << 20,
        name="back_first",
    )
    (scaling_part,) = call(
        back_second_kernel, (sloped, *band4, *around), ((ROWS, COLS),),
        flops=2 * 10**9, room=14 << 20, name="back_second",
    )
    grad_precip, grad_scaling = call(
        back_halo_kernel,
        (lat_in, even, odd, slope_edge, share_edge, precip_part, scaling_part, *edge_bands()),
        ((ROWS, COLS), (ROWS, COLS)),
        scratch=(
            (48, WIDE), (EDGE, EDGE), (EDGE, ROWS), (ROWS, 2 * EDGE), (ROWS, 2 * EDGE),
            (4, 2 * RADIUS, 2 * EDGE),
        ),
        flops=10**9,
        room=14 << 20,
        name="back_halo",
        copies=10,
        out_hbm=True,
    )
    return (grad_precip[None], grad_scaling[None])


def solution(mesh):
    split_mesh = Mesh(
        mesh.devices.reshape(4, 2, 2, mesh.shape["lat"], mesh.shape["lon"]),
        ("hour_0", "hour_1", "hour_2", "lat", "lon"),
    )
    return jax.shard_map(
        per_device,
        mesh=split_mesh,
        in_specs=(P(HOUR, "lat", "lon"), P(HOUR, "lat", "lon"), P(HOUR), P(HOUR, "lat", "lon")),
        out_specs=(P(HOUR, "lat", "lon"), P(HOUR, "lat", "lon")),
        check_vma=False,
    )
```

```python
import numpy as np
import jax
import jax.numpy as jnp
from jax import lax
from jax.experimental import pallas as pl
from jax.experimental.pallas import tpu as pltpu
from jax.sharding import Mesh
from jax.sharding import PartitionSpec as P


RADIUS = 8
HOUR = ("hour_0", "hour_1", "hour_2")
PHI = 0.8
SPREAD = 50.0

ROWS = 512
COLS = 512
WIDE = 640
EDGE = 128
TALL = ROWS + 2 * RADIUS
TALLER = ROWS + 4 * RADIUS
BLOCK = TALL // 3
PIECES = 16
PIECE = ROWS // PIECES
STRIP = 3 * RADIUS
F32 = jnp.float32
BF16 = jnp.bfloat16


def taps_of(spacing):
    offsets = np.arange(-RADIUS, RADIUS + 1).astype(np.float64)
    total = np.sum(np.exp(-offsets * offsets / SPREAD))
    return np.where(np.abs(spacing) <= RADIUS, np.exp(-spacing * spacing / SPREAD) / total, 0.0)


def halves(matrix):
    matrix = matrix.astype(np.float32)
    high = matrix.astype(jnp.bfloat16)
    low = (matrix - high.astype(np.float32)).astype(jnp.bfloat16)
    return jnp.asarray(high), jnp.asarray(low)


def row_band(size):
    outer = np.arange(size)[:, None]
    inner = np.arange(size + 2 * RADIUS)[None, :]
    return halves(taps_of((inner - outer - RADIUS).astype(np.float64)))


def edge_bands():
    outer = np.arange(2 * RADIUS)[:, None]
    inner = np.arange(2 * RADIUS)[None, :]
    low = taps_of((inner - outer - RADIUS).astype(np.float64))
    high = taps_of((inner - outer + RADIUS).astype(np.float64))
    stacks = np.zeros((2, 48, 48))
    for lat, along in enumerate((high, low)):
        for k, band in enumerate((along, low, high)):
            stacks[lat, 16 * k : 16 * (k + 1), 16 * k : 16 * (k + 1)] = band
    return halves(stacks)


def col_band():
    outer = np.arange(WIDE)[:, None]
    inner = np.arange(WIDE)[None, :]
    spacing = (inner - outer + WIDE // 2) % WIDE - WIDE // 2
    return halves(taps_of(spacing.astype(np.float64)))


def split(x):
    high = x.astype(BF16)
    return high, (x - high.astype(F32)).astype(BF16)


def dot(a, b):
    return jnp.dot(a, b, preferred_element_type=F32)


def rows_pass(x, high, low):
    xh, xl = split(x)
    return dot(high[...], xh) + (dot(low[...], xh) + dot(high[...], xl))


def cols_piece(rh, rl, ch, cl, spans, out):
    total = None
    for lo, hi in spans:
        part = dot(rh[:, lo:hi], ch[lo:hi, out]) + (
            dot(rl[:, lo:hi], ch[lo:hi, out]) + dot(rh[:, lo:hi], cl[lo:hi, out])
        )
        total = part if total is None else total + part
    return total


def cols_pass(r, ch, cl, halo):
    rh, rl = split(r)
    pieces = [
        cols_piece(rh, rl, ch, cl, ((0, 384), (512, 640)), slice(0, 256)),
        cols_piece(rh, rl, ch, cl, ((128, 640),), slice(256, 512)),
    ]
    if halo:
        pieces.append(cols_piece(rh, rl, ch, cl, ((384, 640), (0, 128)), slice(512, 640)))
    return jnp.concatenate(pieces, axis=1)


def valid_part(start, count, lat):
    row = lax.broadcasted_iota(jnp.int32, (count, WIDE), 0) + start
    lane = lax.broadcasted_iota(jnp.int32, (count, WIDE), 1)
    inside = (row >= jnp.where(lat == 0, RADIUS, 0)) & (
        row < jnp.where(lat == 0, TALL, TALL - RADIUS)
    )
    return inside & ((lane < COLS + RADIUS) | (lane >= WIDE - RADIUS))


def my_lat():
    return lax.axis_index("lat")


def my_parity():
    return lax.axis_index("lon") & 1


def fill_edges(ext, reach, rows_in, even, odd, side):
    lat, parity = my_lat(), my_parity()
    side[...] = jnp.zeros((EDGE, WIDE), F32)
    side[0:reach, :] = jnp.where(parity == 0, even, odd)
    side[EDGE - reach : EDGE, :] = jnp.where(parity == 0, odd, even)
    flat = jnp.transpose(side[...])
    corner = flat[ROWS : ROWS + reach]
    ext[reach : reach + ROWS, COLS:WIDE] = flat[0:ROWS]
    ext[0:reach, 0:COLS] = jnp.where(lat == 1, rows_in, 0.0)
    ext[0:reach, COLS:WIDE] = jnp.where(lat == 1, corner, 0.0)
    ext[reach + ROWS : 2 * reach + ROWS, 0:COLS] = jnp.where(lat == 0, rows_in, 0.0)
    ext[reach + ROWS : 2 * reach + ROWS, COLS:WIDE] = jnp.where(lat == 0, corner, 0.0)


def column_strips(reach, first_block, last_block, rows_in, parity):
    spare = jnp.zeros((EDGE - reach, EDGE), F32)
    left = jnp.transpose(jnp.concatenate([first_block, rows_in[:, 0:EDGE], spare], axis=0))
    right = jnp.transpose(
        jnp.concatenate([last_block, rows_in[:, COLS - EDGE : COLS], spare], axis=0)
    )
    left, right = left[0:reach], right[EDGE - reach : EDGE]
    return jnp.where(parity == 0, right, left), jnp.where(parity == 0, left, right)


def lat_kernel(scaling, precip, to_lat, ends, sems):
    lat = my_lat()
    wide, narrow = 2 * RADIUS, RADIUS
    copies = [
        pltpu.make_async_copy(src, dst, sems.at[k])
        for k, (src, dst) in enumerate(
            (
                (scaling.at[0:wide, :], ends.at[0, 0:wide, :]),
                (scaling.at[ROWS - wide : ROWS, :], ends.at[1, 0:wide, :]),
                (precip.at[0:narrow, :], ends.at[0, wide:STRIP, :]),
                (precip.at[ROWS - narrow : ROWS, :], ends.at[1, wide:STRIP, :]),
            )
        )
    ]
    for copy in copies:
        copy.start()
    for copy in copies:
        copy.wait()
    to_lat[...] = jnp.where(lat == 0, ends[1], ends[0])


def in_hbm(x):
    return pltpu.with_memory_space_constraint(x, pltpu.HBM)


def lat_strip(scaling, precip):
    return pl.pallas_call(
        lat_kernel,
        out_shape=jax.ShapeDtypeStruct((STRIP, COLS), F32),
        in_specs=[pl.BlockSpec(memory_space=pltpu.HBM)] * 2,
        out_specs=pl.BlockSpec(memory_space=pltpu.VMEM),
        scratch_shapes=[pltpu.VMEM((2, STRIP, COLS), F32), pltpu.SemaphoreType.DMA((4,))],
        compiler_params=pltpu.CompilerParams(vmem_limit_bytes=2 << 20),
        name="lat_edges",
    )(in_hbm(scaling), in_hbm(precip))


def lon_kernel(scaling, precip, lat_in, to_even, to_odd):
    wide, narrow = 2 * RADIUS, RADIUS
    to_even[0:wide, :], to_odd[0:wide, :] = column_strips(
        wide, scaling[:, 0:EDGE], scaling[:, COLS - EDGE : COLS], lat_in[0:wide, :], my_parity()
    )
    to_even[wide:STRIP, :], to_odd[wide:STRIP, :] = column_strips(
        narrow, precip[:, 0:EDGE], precip[:, COLS - EDGE : COLS], lat_in[wide:STRIP, :], my_parity()
    )


def pack_kernel(weight, upstream, packed):
    for p in range(PIECES):
        for j in range(COLS // EDGE):
            packed[p, PIECE * j : PIECE * (j + 1), :] = upstream[
                PIECE * p : PIECE * (p + 1), EDGE * j : EDGE * (j + 1)
            ]
        packed[p, EDGE : EDGE + 8, :] = jnp.full((8, EDGE), weight[0], F32)


def forward_kernel(
    scaling, precip, lat_in, even, odd, rh3, rl3, rh4, rl4, ch, cl,
    slope_out, share_out, second_out, sx, px, side, slope, share, lifted, second, sems,
):
    lat = my_lat()
    wide, narrow = 2 * RADIUS, RADIUS
    sx[wide : wide + ROWS, 0:COLS] = scaling[...]
    px[narrow : narrow + ROWS, 0:COLS] = precip[...]
    fill_edges(sx, wide, lat_in[0:wide, :], even[0:wide, :], odd[0:wide, :], side)
    fill_edges(px, narrow, lat_in[wide:STRIP, :], even[wide:STRIP, :], odd[wide:STRIP, :], side)
    copies = []

    def sent(src, dst):
        copies.append(pltpu.make_async_copy(src, dst, sems.at[len(copies)]))
        copies[-1].start()

    for i in range(3):
        at = BLOCK * i
        r = rows_pass(sx[at : at + BLOCK + 2 * RADIUS, :], rh3, rl3)
        a = cols_pass(r, ch, cl, True)
        rain = px[at : at + BLOCK, :]
        inside = valid_part(at, BLOCK, lat)
        u = jnp.where(inside, jnp.exp(PHI * jnp.log(rain / a)), 0.0)
        lifted[at : at + BLOCK, :] = u
        slope[at : at + BLOCK, :] = jnp.where(inside, -PHI * u / a, 0.0)
        lo, hi = max(at, RADIUS), min(at + BLOCK, RADIUS + ROWS)
        here = slice(lo - RADIUS, hi - RADIUS)
        share[here, :] = PHI * u[lo - at : hi - at, 0:COLS] / rain[lo - at : hi - at, 0:COLS]
        sent(slope.at[at : at + BLOCK, :], slope_out.at[at : at + BLOCK, :])
        sent(share.at[here, :], share_out.at[here, :])
    for i in range(4):
        at = EDGE * i
        r = rows_pass(lifted[at : at + EDGE + 2 * RADIUS, :], rh4, rl4)
        b = cols_pass(r, ch, cl, False)
        for q in range(EDGE // PIECE):
            for j in range(COLS // EDGE):
                second[i * (EDGE // PIECE) + q, PIECE * j : PIECE * (j + 1), :] = b[
                    PIECE * q : PIECE * (q + 1), EDGE * j : EDGE * (j + 1)
                ]
        done = slice(i * (EDGE // PIECE), (i + 1) * (EDGE // PIECE))
        sent(second.at[done], second_out.at[done])
    for copy in copies:
        copy.wait()


def hours_kernel(second, upstream, out):
    def one(at, carry):
        rows = pl.ds(pl.multiple_of(at * 8, 8), 8)
        logs = [jnp.log(second[h, rows, :]) for h in range(PIECES)]
        weights = [upstream[h, EDGE : EDGE + 8, :] for h in range(PIECES)]
        logq = weights[0] * logs[0]
        for h in range(1, PIECES):
            logq = logq + weights[h] * logs[h]
        terms = [
            PHI * upstream[h, rows, :] * jnp.exp(PHI * (logq - logs[h])) for h in range(PIECES)
        ]
        dlogq = terms[0]
        for h in range(1, PIECES):
            dlogq = dlogq + terms[h]
        for h in range(PIECES):
            out[h, rows, :] = (weights[h] * dlogq - terms[h]) / second[h, rows, :]
        return carry

    lax.fori_loop(0, EDGE // 8, one, 0)


def tile_column(pieces, j):
    return jnp.concatenate(
        [pieces[p, PIECE * j : PIECE * (j + 1), :] for p in range(PIECES)], axis=0
    )


def back_lat_kernel(pieces, to_lat):
    wide = 2 * RADIUS
    for j in range(COLS // EDGE):
        to_lat[:, EDGE * j : EDGE * (j + 1)] = jnp.where(
            my_lat() == 0,
            pieces[PIECES - 1, PIECE * (j + 1) - wide : PIECE * (j + 1), :],
            pieces[0, PIECE * j : PIECE * j + wide, :],
        )


def back_lon_kernel(pieces, lat_in, to_even, to_odd):
    to_even[...], to_odd[...] = column_strips(
        2 * RADIUS, tile_column(pieces, 0), tile_column(pieces, COLS // EDGE - 1), lat_in[...],
        my_parity(),
    )


def coefficient_strips(slope, share, slope_edge, share_edge):
    wide = 2 * RADIUS
    top = my_lat() == 1
    nothing = jnp.zeros((RADIUS, COLS), F32)
    first, last = slice(0, EDGE), slice(COLS - EDGE, COLS)

    def turned(block):
        gap = jnp.zeros((WIDE - TALL, EDGE), F32)
        return jnp.transpose(jnp.concatenate([block[RADIUS:TALL], gap, block[0:RADIUS]], axis=0))

    near = lax.broadcasted_iota(jnp.int32, (TALL, EDGE), 1) < EDGE // 2
    tile = turned(jnp.where(near, slope[:, first], slope[:, last]))
    halo = turned(slope[:, COLS:WIDE])
    slope_edge[0:wide, :] = jnp.where(top, slope[0:wide, :], slope[TALL - wide : TALL, :])
    slope_edge[16:24, :] = halo[EDGE - RADIUS : EDGE]
    slope_edge[24:32, :] = tile[0:RADIUS]
    slope_edge[32:40, :] = tile[EDGE - RADIUS : EDGE]
    slope_edge[40:48, :] = halo[0:RADIUS]
    tile = jnp.transpose(jnp.where(near[0:ROWS], share[:, first], share[:, last]))
    share_edge[...] = jnp.zeros((48, WIDE), F32)
    share_edge[0:RADIUS, 0:COLS] = jnp.where(top, nothing, share[ROWS - RADIUS : ROWS, :])
    share_edge[RADIUS:wide, 0:COLS] = jnp.where(top, share[0:RADIUS, :], nothing)
    share_edge[24:32, 0:COLS] = tile[0:RADIUS]
    share_edge[32:40, 0:COLS] = tile[EDGE - RADIUS : EDGE]


def back_first_kernel(
    pieces, slope, share, rh3, rl3, ch, cl, grad_precip, sloped, slope_edge, share_edge, dx
):
    coefficient_strips(slope, share, slope_edge, share_edge)
    wide = 2 * RADIUS
    dx[0:wide, :] = jnp.zeros((wide, COLS), F32)
    dx[wide + ROWS : TALLER, :] = jnp.zeros((wide, COLS), F32)
    for p in range(PIECES):
        for j in range(COLS // EDGE):
            dx[wide + PIECE * p : wide + PIECE * (p + 1), EDGE * j : EDGE * (j + 1)] = pieces[
                p, PIECE * j : PIECE * (j + 1), :
            ]
    for i in range(3):
        at = BLOCK * i
        rh, rl = split(rows_pass(dx[at : at + BLOCK + 2 * RADIUS, :], rh3, rl3))
        du = jnp.concatenate(
            [
                cols_piece(rh, rl, ch, cl, ((0, 384),), slice(0, 256)),
                cols_piece(rh, rl, ch, cl, ((128, 512),), slice(256, 512)),
                cols_piece(rh, rl, ch, cl, ((384, 512), (0, 128)), slice(512, 640)),
            ],
            axis=1,
        )
        sloped[at : at + BLOCK, :] = slope[at : at + BLOCK, :] * du
        lo, hi = max(at, RADIUS), min(at + BLOCK, RADIUS + ROWS)
        here = slice(lo - RADIUS, hi - RADIUS)
        grad_precip[here, :] = share[here, :] * du[lo - at : hi - at, 0:COLS]


def back_second_kernel(sloped, rh4, rl4, ch, cl, grad_scaling):
    for i in range(4):
        at = EDGE * i
        r = rows_pass(sloped[at : at + EDGE + 2 * RADIUS, :], rh4, rl4)
        grad_scaling[at : at + EDGE, :] = cols_pass(r, ch, cl, False)


def around_pass(x):
    taps = taps_of(np.arange(RADIUS + 1).astype(np.float64))
    total = float(taps[0]) * x
    for d in range(1, RADIUS + 1):
        total += float(taps[d]) * (pltpu.roll(x, d, 1) + pltpu.roll(x, WIDE - d, 1))
    return total


def back_halo_kernel(
    lat_in, even, odd, slope_edge, share_edge, precip_part, scaling_part, dh, dl,
    precip_out, scaling_out, strips, square, flat, precip_edge, scaling_edge, middle, sems,
):
    wide = 2 * RADIUS
    lat, parity = my_lat(), my_parity()
    top = lat == 1
    inner = slice(EDGE, COLS - EDGE)
    last = slice(COLS - EDGE, COLS)
    copies = []

    def sent(src, dst):
        copies.append(pltpu.make_async_copy(src, dst, sems.at[len(copies)]))
        copies[-1].start()

    for part, out in ((precip_part, precip_out), (scaling_part, scaling_out)):
        sent(part.at[wide : ROWS - wide, inner], out.at[wide : ROWS - wide, inner])

    right = jnp.where(parity == 0, even[...], odd[...])
    left = jnp.where(parity == 0, odd[...], even[...])
    square[...] = jnp.zeros((EDGE, EDGE), F32)
    square[0:wide, :] = right[:, COLS:WIDE]
    square[EDGE - wide : EDGE, :] = left[:, COLS:WIDE]
    strips[...] = jnp.zeros((48, WIDE), F32)
    strips[0:16, 0:COLS] = lat_in[...]
    strips[0:16, COLS:WIDE] = jnp.transpose(square[...])[0:wide]
    strips[16:32, 0:COLS] = left[:, 0:COLS]
    strips[32:48, 0:COLS] = right[:, 0:COLS]
    band_h, band_l = dh[lat], dl[lat]

    def smoothed(x):
        xh, xl = split(x)
        return around_pass(dot(band_h, xh) + (dot(band_l, xh) + dot(band_h, xl)))

    du = smoothed(strips[...])
    precip_more = share_edge[...] * du
    scaling_more = smoothed(slope_edge[...] * du)
    nothing = jnp.zeros((RADIUS, COLS), F32)
    near = lax.broadcasted_iota(jnp.int32, (ROWS, EDGE), 1) < EDGE // 2

    def finished(k, part, out, edges, reach, low, high, first, final):
        flat[...] = jnp.zeros((EDGE, ROWS), F32)
        flat[0:reach, :] = low
        flat[EDGE - reach : EDGE, :] = high
        turned = jnp.transpose(flat[...])
        middle[2 * k] = part[0:wide, inner] + first[:, inner]
        middle[2 * k + 1] = part[ROWS - wide : ROWS, inner] + final[:, inner]
        sent(middle.at[2 * k], out.at[0:wide, inner])
        sent(middle.at[2 * k + 1], out.at[ROWS - wide : ROWS, inner])
        edges[:, 0:EDGE] = part[:, 0:EDGE] + jnp.where(near, turned, 0.0)
        edges[:, EDGE : 2 * EDGE] = part[:, last] + jnp.where(near, 0.0, turned)
        for q, lanes in enumerate((slice(0, EDGE), last)):
            mine = slice(EDGE * q, EDGE * (q + 1))
            edges[0:wide, mine] += first[:, lanes]
            edges[ROWS - wide : ROWS, mine] += final[:, lanes]
            sent(edges.at[:, mine], out.at[:, lanes])

    finished(
        0, precip_part, precip_out, precip_edge, RADIUS,
        precip_more[24:32, 0:COLS], precip_more[32:40, 0:COLS],
        jnp.concatenate([precip_more[RADIUS:wide, 0:COLS], nothing], axis=0),
        jnp.concatenate([nothing, precip_more[0:RADIUS, 0:COLS]], axis=0),
    )
    added = scaling_more[0:wide, 0:COLS]
    finished(
        1, scaling_part, scaling_out, scaling_edge, wide,
        scaling_more[16:32, 0:COLS], scaling_more[32:48, 0:COLS],
        jnp.where(top, added, 0.0), jnp.where(top, 0.0, added),
    )
    for copy in copies:
        copy.wait()


def in_vmem(*shapes):
    return [pltpu.VMEM(shape, F32) for shape in shapes]


def call(
    kernel, args, outs, scratch=(), scalars=0, flops=0, room=4 << 20, copies=0,
    out_hbm=False,
):
    size = sum(4 * a.size for a in args) + sum(4 * int(np.prod(o)) for o in outs)
    where = pltpu.HBM if out_hbm else pltpu.VMEM
    spaces = [
        pltpu.SMEM if k < scalars else pltpu.VMEM
        for k in range(len(args))
    ]
    sems = [pltpu.SemaphoreType.DMA((copies,))] if copies else []
    return pl.pallas_call(
        kernel,
        out_shape=[pltpu.HBM(o, F32) if out_hbm else jax.ShapeDtypeStruct(o, F32) for o in outs],
        in_specs=[pl.BlockSpec(memory_space=space) for space in spaces],
        out_specs=[pl.BlockSpec(memory_space=where)] * len(outs),
        scratch_shapes=in_vmem(*scratch) + sems,
        cost_estimate=pl.CostEstimate(flops=flops, bytes_accessed=size, transcendentals=0),
        compiler_params=pltpu.CompilerParams(vmem_limit_bytes=room),
    )(*args)


def lat_swapped(strip):
    return lax.ppermute(strip, "lat", [(0, 1), (1, 0)])


def lon_swapped(to_even, to_odd):
    count = lax.axis_size("lon")
    even = [(i, i ^ 1) for i in range(count)]
    odd = [(i, (((i - 1) % count ^ 1) + 1) % count) for i in range(count)]
    return lax.ppermute(to_even, "lon", even), lax.ppermute(to_odd, "lon", odd)


def hours_swapped(pieces):
    return lax.all_to_all(pieces, HOUR, 0, 0, tiled=True)


def per_device(precip, scaling, hour_weight, cotangent):
    rainfall = precip[0]
    incoming = scaling[0]
    upstream = cotangent[0]
    band3, band4, around = row_band(BLOCK), row_band(EDGE), col_band()
    bands = (*band3, *band4, *around)
    to_lat = lat_strip(incoming, rainfall)
    lat_in = lat_swapped(to_lat)
    (packed,) = call(pack_kernel, (hour_weight, upstream), ((PIECES, EDGE + 8, EDGE),), scalars=1)
    everyone = hours_swapped(packed)
    even, odd = lon_swapped(
        *call(lon_kernel, (incoming, rainfall, lat_in), ((STRIP, WIDE), (STRIP, WIDE)))
    )
    slope, share, second = call(
        forward_kernel,
        (incoming, rainfall, lat_in, even, odd, *bands),
        ((TALL, WIDE), (ROWS, COLS), (PIECES, EDGE, EDGE)),
        scratch=(
            (TALLER, WIDE), (TALL, WIDE), (EDGE, WIDE),
            (TALL, WIDE), (ROWS, COLS), (TALL, WIDE), (PIECES, EDGE, EDGE),
        ),
        flops=4 * 10**9,
        room=14 << 20,
        copies=10,
        out_hbm=True,
    )
    second, everyone = lax.optimization_barrier((second, everyone))
    (dsecond,) = call(hours_kernel, (hours_swapped(second), everyone), ((PIECES, EDGE, EDGE),))
    pieces = hours_swapped(dsecond)
    (to_lat,) = call(back_lat_kernel, (pieces,), ((2 * RADIUS, COLS),))
    lat_in = lat_swapped(to_lat)
    even, odd = lon_swapped(
        *call(back_lon_kernel, (pieces, lat_in), ((2 * RADIUS, WIDE), (2 * RADIUS, WIDE)))
    )
    precip_part, sloped, slope_edge, share_edge = call(
        back_first_kernel,
        (pieces, slope, share, *band3, *around),
        ((ROWS, COLS), (TALL, WIDE), (48, WIDE), (48, WIDE)),
        scratch=((TALLER, COLS),),
        flops=2 * 10**9,
        room=14 << 20,
    )
    (scaling_part,) = call(
        back_second_kernel, (sloped, *band4, *around), ((ROWS, COLS),),
        flops=2 * 10**9, room=14 << 20,
    )
    grad_precip, grad_scaling = call(
        back_halo_kernel,
        (lat_in, even, odd, slope_edge, share_edge, precip_part, scaling_part, *edge_bands()),
        ((ROWS, COLS), (ROWS, COLS)),
        scratch=(
            (48, WIDE), (EDGE, EDGE), (EDGE, ROWS), (ROWS, 2 * EDGE), (ROWS, 2 * EDGE),
            (4, 2 * RADIUS, 2 * EDGE),
        ),
        flops=10**9,
        room=14 << 20,
        copies=10,
        out_hbm=True,
    )
    return (grad_precip[None], grad_scaling[None])


def solution(mesh):
    split_mesh = Mesh(
        mesh.devices.reshape(4, 2, 2, mesh.shape["lat"], mesh.shape["lon"]),
        ("hour_0", "hour_1", "hour_2", "lat", "lon"),
    )
    return jax.shard_map(
        per_device,
        mesh=split_mesh,
        in_specs=(P(HOUR, "lat", "lon"), P(HOUR, "lat", "lon"), P(HOUR), P(HOUR, "lat", "lon")),
        out_specs=(P(HOUR, "lat", "lon"), P(HOUR, "lat", "lon")),
        check_vma=False,
    )
```

```python
import numpy as np
import jax
import jax.numpy as jnp
from jax import lax
from jax.experimental import pallas as pl
from jax.experimental.pallas import tpu as pltpu
from jax.sharding import Mesh
from jax.sharding import PartitionSpec as P

RADIUS = 8
HOUR = ("hour_0", "hour_1", "hour_2")
PHI = 0.8
SPREAD = 50.0

ROWS = 512
COLS = 512
WIDE = 640
EDGE = 128
TALL = ROWS + 2 * RADIUS
TALLER = ROWS + 4 * RADIUS
BLOCK = TALL // 3
PIECES = 16
CHIPS = 8
PIECE = ROWS // PIECES
STRIP = 3 * RADIUS
F32 = jnp.float32
BF16 = jnp.bfloat16


def taps_of(spacing):
    offsets = np.arange(-RADIUS, RADIUS + 1).astype(np.float64)
    total = np.sum(np.exp(-offsets * offsets / SPREAD))
    return np.where(np.abs(spacing) <= RADIUS, np.exp(-spacing * spacing / SPREAD) / total, 0.0)


def halves(matrix):
    matrix = matrix.astype(np.float32)
    high = matrix.astype(jnp.bfloat16)
    low = (matrix - high.astype(np.float32)).astype(jnp.bfloat16)
    return jnp.asarray(high), jnp.asarray(low)


def row_band(size):
    outer = np.arange(size)[:, None]
    inner = np.arange(size + 2 * RADIUS)[None, :]
    return halves(taps_of((inner - outer - RADIUS).astype(np.float64)))


def edge_bands():
    outer = np.arange(2 * RADIUS)[:, None]
    inner = np.arange(2 * RADIUS)[None, :]
    low = taps_of((inner - outer - RADIUS).astype(np.float64))
    high = taps_of((inner - outer + RADIUS).astype(np.float64))
    stacks = np.zeros((2, 48, 48))
    for lat, along in enumerate((high, low)):
        for k, band in enumerate((along, low, high)):
            stacks[lat, 16 * k : 16 * (k + 1), 16 * k : 16 * (k + 1)] = band
    return halves(stacks)


def col_band():
    outer = np.arange(WIDE)[:, None]
    inner = np.arange(WIDE)[None, :]
    spacing = (inner - outer + WIDE // 2) % WIDE - WIDE // 2
    return halves(taps_of(spacing.astype(np.float64)))


def split(x):
    high = x.astype(BF16)
    return high, (x - high.astype(F32)).astype(BF16)


def dot(a, b):
    return jnp.dot(a, b, preferred_element_type=F32)


def rows_pass(x, high, low):
    xh, xl = split(x)
    return dot(high[...], xh) + (dot(low[...], xh) + dot(high[...], xl))


def cols_piece(rh, rl, ch, cl, spans, out):
    total = None
    for lo, hi in spans:
        part = dot(rh[:, lo:hi], ch[lo:hi, out]) + (
            dot(rl[:, lo:hi], ch[lo:hi, out]) + dot(rh[:, lo:hi], cl[lo:hi, out])
        )
        total = part if total is None else total + part
    return total


def cols_pass(r, ch, cl, halo):
    rh, rl = split(r)
    pieces = [
        cols_piece(rh, rl, ch, cl, ((0, 384), (512, 640)), slice(0, 256)),
        cols_piece(rh, rl, ch, cl, ((128, 640),), slice(256, 512)),
    ]
    if halo:
        pieces.append(cols_piece(rh, rl, ch, cl, ((384, 640), (0, 128)), slice(512, 640)))
    return jnp.concatenate(pieces, axis=1)


def valid_part(start, count, lat):
    row = lax.broadcasted_iota(jnp.int32, (count, WIDE), 0) + start
    lane = lax.broadcasted_iota(jnp.int32, (count, WIDE), 1)
    inside = (row >= jnp.where(lat == 0, RADIUS, 0)) & (
        row < jnp.where(lat == 0, TALL, TALL - RADIUS)
    )
    return inside & ((lane < COLS + RADIUS) | (lane >= WIDE - RADIUS))


def my_lat():
    return lax.axis_index("lat")


def my_parity():
    return lax.axis_index("lon") & 1


def fill_edges(ext, reach, rows_in, even, odd, side):
    lat, parity = my_lat(), my_parity()
    side[...] = jnp.zeros((EDGE, WIDE), F32)
    side[0:reach, :] = jnp.where(parity == 0, even, odd)
    side[EDGE - reach : EDGE, :] = jnp.where(parity == 0, odd, even)
    flat = jnp.transpose(side[...])
    corner = flat[ROWS : ROWS + reach]
    ext[reach : reach + ROWS, COLS:WIDE] = flat[0:ROWS]
    ext[0:reach, 0:COLS] = jnp.where(lat == 1, rows_in, 0.0)
    ext[0:reach, COLS:WIDE] = jnp.where(lat == 1, corner, 0.0)
    ext[reach + ROWS : 2 * reach + ROWS, 0:COLS] = jnp.where(lat == 0, rows_in, 0.0)
    ext[reach + ROWS : 2 * reach + ROWS, COLS:WIDE] = jnp.where(lat == 0, corner, 0.0)


def column_strips(reach, first_block, last_block, rows_in, parity):
    spare = jnp.zeros((EDGE - reach, EDGE), F32)
    left = jnp.transpose(jnp.concatenate([first_block, rows_in[:, 0:EDGE], spare], axis=0))
    right = jnp.transpose(
        jnp.concatenate([last_block, rows_in[:, COLS - EDGE : COLS], spare], axis=0)
    )
    left, right = left[0:reach], right[EDGE - reach : EDGE]
    return jnp.where(parity == 0, right, left), jnp.where(parity == 0, left, right)


def lat_kernel(scaling, precip, to_lat, sems):
    wide, narrow = 2 * RADIUS, RADIUS
    keep = 1 - my_lat()
    at = pl.multiple_of(keep * (ROWS - wide), 8)
    near = pl.multiple_of(keep * (ROWS - narrow), 8)
    copies = (
        pltpu.make_async_copy(scaling.at[pl.ds(at, wide), :], to_lat.at[0:wide, :], sems.at[0]),
        pltpu.make_async_copy(
            precip.at[pl.ds(near, narrow), :], to_lat.at[wide:STRIP, :], sems.at[1]
        ),
    )
    for copy in copies:
        copy.start()
    for copy in copies:
        copy.wait()


def in_hbm(x):
    return pltpu.with_memory_space_constraint(x, pltpu.HBM)


def lat_strip(scaling, precip):
    return pl.pallas_call(
        lat_kernel,
        out_shape=jax.ShapeDtypeStruct((STRIP, COLS), F32),
        in_specs=[pl.BlockSpec(memory_space=pltpu.HBM)] * 2,
        out_specs=pl.BlockSpec(memory_space=pltpu.VMEM),
        scratch_shapes=[pltpu.SemaphoreType.DMA((2,))],
        compiler_params=pltpu.CompilerParams(vmem_limit_bytes=2 << 20),
        name="lat_edges",
    )(in_hbm(scaling), in_hbm(precip))


def lon_kernel(scaling, precip, lat_in, to_even, to_odd):
    wide, narrow = 2 * RADIUS, RADIUS
    to_even[0:wide, :], to_odd[0:wide, :] = column_strips(
        wide, scaling[:, 0:EDGE], scaling[:, COLS - EDGE : COLS], lat_in[0:wide, :], my_parity()
    )
    to_even[wide:STRIP, :], to_odd[wide:STRIP, :] = column_strips(
        narrow, precip[:, 0:EDGE], precip[:, COLS - EDGE : COLS], lat_in[wide:STRIP, :], my_parity()
    )


def forward_kernel(
    weight, scaling, precip, upstream, lat_in, even, odd, rh3, rl3, rh4, rl4, ch, cl,
    slope, share, second, logs, keep, give, sx, px, side, lifted,
):
    lat = my_lat()
    core = lax.axis_index("hour_2")
    wide, narrow = 2 * RADIUS, RADIUS
    sx[wide : wide + ROWS, 0:COLS] = scaling[...]
    px[narrow : narrow + ROWS, 0:COLS] = precip[...]
    fill_edges(sx, wide, lat_in[0:wide, :], even[0:wide, :], odd[0:wide, :], side)
    fill_edges(px, narrow, lat_in[wide:STRIP, :], even[wide:STRIP, :], odd[wide:STRIP, :], side)
    for i in range(3):
        at = BLOCK * i
        r = rows_pass(sx[at : at + BLOCK + 2 * RADIUS, :], rh3, rl3)
        a = cols_pass(r, ch, cl, True)
        rain = px[at : at + BLOCK, :]
        inside = valid_part(at, BLOCK, lat)
        u = jnp.where(inside, jnp.exp(PHI * jnp.log(rain / a)), 0.0)
        lifted[at : at + BLOCK, :] = u
        slope[at : at + BLOCK, :] = jnp.where(inside, -PHI * u / a, 0.0)
        lo, hi = max(at, RADIUS), min(at + BLOCK, RADIUS + ROWS)
        here = slice(lo - RADIUS, hi - RADIUS)
        share[here, :] = PHI * u[lo - at : hi - at, 0:COLS] / rain[lo - at : hi - at, 0:COLS]
    for i in range(4):
        at = EDGE * i
        r = rows_pass(lifted[at : at + EDGE + 2 * RADIUS, :], rh4, rl4)
        b = cols_pass(r, ch, cl, False)
        logb = jnp.log(b)
        parts = (weight[0] * logb, upstream[at : at + EDGE, :] * jnp.exp(-PHI * logb))
        for j in range(COLS // EDGE):
            lanes = slice(EDGE * j, EDGE * (j + 1))
            for q in range(EDGE // PIECE):
                rows = slice(PIECE * q, PIECE * (q + 1))
                to = slice(PIECE * j, PIECE * (j + 1))
                second[i * (EDGE // PIECE) + q, to, :] = b[rows, lanes]
                logs[i * (EDGE // PIECE) + q, to, :] = logb[rows, lanes]
            for c in range(2):
                first = slice(2 * PIECE * c, 2 * PIECE * c + PIECE)
                other = slice(2 * PIECE * c + PIECE, 2 * PIECE * (c + 1))
                for k, part in enumerate(parts):
                    to = slice(EDGE * k + PIECE * j, EDGE * k + PIECE * (j + 1))
                    x, y = part[first, lanes], part[other, lanes]
                    keep[2 * i + c, to, :] = jnp.where(core == 0, x, y)
                    give[2 * i + c, to, :] = jnp.where(core == 0, y, x)


def pair_kernel(keep, given, out):
    def one(c, carry):
        out[c] = keep[c] + given[c]
        return carry

    lax.fori_loop(0, CHIPS, one, 0)


def owner_kernel(sums, out):
    def total(start):
        x = sums[0, start : start + EDGE, :]
        for c in range(1, CHIPS):
            x = x + sums[c, start : start + EDGE, :]
        return x

    logq = total(0)
    dlogq = PHI * jnp.exp(PHI * logq) * total(EDGE)
    for c in range(CHIPS):
        out[c, 0:EDGE, :] = logq
        out[c, EDGE : 2 * EDGE, :] = dlogq


def db_kernel(weight, mine, theirs, upstream, second, logs, pieces):
    core = lax.axis_index("hour_2")
    for p in range(PIECES):
        here = core == p % 2
        for j in range(COLS // EDGE):
            rows = slice(PIECE * j, PIECE * (j + 1))
            low = slice(EDGE + PIECE * j, EDGE + PIECE * (j + 1))
            logq = jnp.where(here, mine[p // 2, rows, :], theirs[p // 2, rows, :])
            dlogq = jnp.where(here, mine[p // 2, low, :], theirs[p // 2, low, :])
            own = upstream[PIECE * p : PIECE * (p + 1), EDGE * j : EDGE * (j + 1)]
            term = PHI * own * jnp.exp(PHI * (logq - logs[p, rows, :]))
            pieces[p, rows, :] = (weight[0] * dlogq - term) / second[p, rows, :]


def tile_column(pieces, j):
    return jnp.concatenate(
        [pieces[p, PIECE * j : PIECE * (j + 1), :] for p in range(PIECES)], axis=0
    )


def back_lat_kernel(pieces, to_lat):
    wide = 2 * RADIUS
    for j in range(COLS // EDGE):
        to_lat[:, EDGE * j : EDGE * (j + 1)] = jnp.where(
            my_lat() == 0,
            pieces[PIECES - 1, PIECE * (j + 1) - wide : PIECE * (j + 1), :],
            pieces[0, PIECE * j : PIECE * j + wide, :],
        )


def back_lon_kernel(pieces, lat_in, to_even, to_odd):
    to_even[...], to_odd[...] = column_strips(
        2 * RADIUS, tile_column(pieces, 0), tile_column(pieces, COLS // EDGE - 1), lat_in[...],
        my_parity(),
    )


def coefficient_strips(slope, share, slope_edge, share_edge):
    wide = 2 * RADIUS
    top = my_lat() == 1
    nothing = jnp.zeros((RADIUS, COLS), F32)
    first, last = slice(0, EDGE), slice(COLS - EDGE, COLS)

    def turned(block):
        gap = jnp.zeros((WIDE - TALL, EDGE), F32)
        return jnp.transpose(jnp.concatenate([block[RADIUS:TALL], gap, block[0:RADIUS]], axis=0))

    near = lax.broadcasted_iota(jnp.int32, (TALL, EDGE), 1) < EDGE // 2
    tile = turned(jnp.where(near, slope[:, first], slope[:, last]))
    halo = turned(slope[:, COLS:WIDE])
    slope_edge[0:wide, :] = jnp.where(top, slope[0:wide, :], slope[TALL - wide : TALL, :])
    slope_edge[16:24, :] = halo[EDGE - RADIUS : EDGE]
    slope_edge[24:32, :] = tile[0:RADIUS]
    slope_edge[32:40, :] = tile[EDGE - RADIUS : EDGE]
    slope_edge[40:48, :] = halo[0:RADIUS]
    tile = jnp.transpose(jnp.where(near[0:ROWS], share[:, first], share[:, last]))
    share_edge[...] = jnp.zeros((48, WIDE), F32)
    share_edge[0:RADIUS, 0:COLS] = jnp.where(top, nothing, share[ROWS - RADIUS : ROWS, :])
    share_edge[RADIUS:wide, 0:COLS] = jnp.where(top, share[0:RADIUS, :], nothing)
    share_edge[24:32, 0:COLS] = tile[0:RADIUS]
    share_edge[32:40, 0:COLS] = tile[EDGE - RADIUS : EDGE]


def back_first_kernel(
    pieces, slope, share, rh3, rl3, ch, cl, grad_precip, sloped, slope_edge, share_edge, dx
):
    coefficient_strips(slope, share, slope_edge, share_edge)
    wide = 2 * RADIUS
    dx[0:wide, :] = jnp.zeros((wide, COLS), F32)
    dx[wide + ROWS : TALLER, :] = jnp.zeros((wide, COLS), F32)
    for p in range(PIECES):
        for j in range(COLS // EDGE):
            dx[wide + PIECE * p : wide + PIECE * (p + 1), EDGE * j : EDGE * (j + 1)] = pieces[
                p, PIECE * j : PIECE * (j + 1), :
            ]
    for i in range(3):
        at = BLOCK * i
        rh, rl = split(rows_pass(dx[at : at + BLOCK + 2 * RADIUS, :], rh3, rl3))
        du = jnp.concatenate(
            [
                cols_piece(rh, rl, ch, cl, ((0, 384),), slice(0, 256)),
                cols_piece(rh, rl, ch, cl, ((128, 512),), slice(256, 512)),
                cols_piece(rh, rl, ch, cl, ((384, 512), (0, 128)), slice(512, 640)),
            ],
            axis=1,
        )
        sloped[at : at + BLOCK, :] = slope[at : at + BLOCK, :] * du
        lo, hi = max(at, RADIUS), min(at + BLOCK, RADIUS + ROWS)
        here = slice(lo - RADIUS, hi - RADIUS)
        grad_precip[here, :] = share[here, :] * du[lo - at : hi - at, 0:COLS]


def back_second_kernel(sloped, rh4, rl4, ch, cl, grad_scaling):
    for i in range(4):
        at = EDGE * i
        r = rows_pass(sloped[at : at + EDGE + 2 * RADIUS, :], rh4, rl4)
        grad_scaling[at : at + EDGE, :] = cols_pass(r, ch, cl, False)


def around_pass(x):
    taps = taps_of(np.arange(RADIUS + 1).astype(np.float64))
    total = float(taps[0]) * x
    for d in range(1, RADIUS + 1):
        total += float(taps[d]) * (pltpu.roll(x, d, 1) + pltpu.roll(x, WIDE - d, 1))
    return total


def back_halo_kernel(
    lat_in, even, odd, slope_edge, share_edge, precip_part, scaling_part, dh, dl,
    precip_out, scaling_out, strips, square, flat, precip_edge, scaling_edge, middle, sems,
):
    wide = 2 * RADIUS
    lat, parity = my_lat(), my_parity()
    top = lat == 1
    inner = slice(EDGE, COLS - EDGE)
    last = slice(COLS - EDGE, COLS)
    copies = []

    def sent(src, dst):
        copies.append(pltpu.make_async_copy(src, dst, sems.at[len(copies)]))
        copies[-1].start()

    for part, out in ((precip_part, precip_out), (scaling_part, scaling_out)):
        sent(part.at[wide : ROWS - wide, inner], out.at[wide : ROWS - wide, inner])

    right = jnp.where(parity == 0, even[...], odd[...])
    left = jnp.where(parity == 0, odd[...], even[...])
    square[...] = jnp.zeros((EDGE, EDGE), F32)
    square[0:wide, :] = right[:, COLS:WIDE]
    square[EDGE - wide : EDGE, :] = left[:, COLS:WIDE]
    strips[...] = jnp.zeros((48, WIDE), F32)
    strips[0:16, 0:COLS] = lat_in[...]
    strips[0:16, COLS:WIDE] = jnp.transpose(square[...])[0:wide]
    strips[16:32, 0:COLS] = left[:, 0:COLS]
    strips[32:48, 0:COLS] = right[:, 0:COLS]
    band_h, band_l = dh[lat], dl[lat]

    def smoothed(x):
        xh, xl = split(x)
        return around_pass(dot(band_h, xh) + (dot(band_l, xh) + dot(band_h, xl)))

    du = smoothed(strips[...])
    precip_more = share_edge[...] * du
    scaling_more = smoothed(slope_edge[...] * du)
    nothing = jnp.zeros((RADIUS, COLS), F32)
    near = lax.broadcasted_iota(jnp.int32, (ROWS, EDGE), 1) < EDGE // 2

    def finished(k, part, out, edges, reach, low, high, first, final):
        flat[...] = jnp.zeros((EDGE, ROWS), F32)
        flat[0:reach, :] = low
        flat[EDGE - reach : EDGE, :] = high
        turned = jnp.transpose(flat[...])
        middle[2 * k] = part[0:wide, inner] + first[:, inner]
        middle[2 * k + 1] = part[ROWS - wide : ROWS, inner] + final[:, inner]
        sent(middle.at[2 * k], out.at[0:wide, inner])
        sent(middle.at[2 * k + 1], out.at[ROWS - wide : ROWS, inner])
        edges[:, 0:EDGE] = part[:, 0:EDGE] + jnp.where(near, turned, 0.0)
        edges[:, EDGE : 2 * EDGE] = part[:, last] + jnp.where(near, 0.0, turned)
        for q, lanes in enumerate((slice(0, EDGE), last)):
            mine = slice(EDGE * q, EDGE * (q + 1))
            edges[0:wide, mine] += first[:, lanes]
            edges[ROWS - wide : ROWS, mine] += final[:, lanes]
            sent(edges.at[:, mine], out.at[:, lanes])

    finished(
        0, precip_part, precip_out, precip_edge, RADIUS,
        precip_more[24:32, 0:COLS], precip_more[32:40, 0:COLS],
        jnp.concatenate([precip_more[RADIUS:wide, 0:COLS], nothing], axis=0),
        jnp.concatenate([nothing, precip_more[0:RADIUS, 0:COLS]], axis=0),
    )
    added = scaling_more[0:wide, 0:COLS]
    finished(
        1, scaling_part, scaling_out, scaling_edge, wide,
        scaling_more[16:32, 0:COLS], scaling_more[32:48, 0:COLS],
        jnp.where(top, added, 0.0), jnp.where(top, 0.0, added),
    )
    for copy in copies:
        copy.wait()


def in_vmem(*shapes):
    return [pltpu.VMEM(shape, F32) for shape in shapes]


def call(
    kernel, args, outs, scratch=(), scalars=0, flops=0, room=4 << 20, name=None, copies=0,
    out_hbm=False,
):
    size = sum(4 * a.size for a in args) + sum(4 * int(np.prod(o)) for o in outs)
    where = pltpu.HBM if out_hbm else pltpu.VMEM
    spaces = [
        pltpu.SMEM if k < scalars else pltpu.VMEM
        for k in range(len(args))
    ]
    sems = [pltpu.SemaphoreType.DMA((copies,))] if copies else []
    return pl.pallas_call(
        kernel,
        out_shape=[pltpu.HBM(o, F32) if out_hbm else jax.ShapeDtypeStruct(o, F32) for o in outs],
        in_specs=[pl.BlockSpec(memory_space=space) for space in spaces],
        out_specs=[pl.BlockSpec(memory_space=where)] * len(outs),
        scratch_shapes=in_vmem(*scratch) + sems,
        cost_estimate=pl.CostEstimate(flops=flops, bytes_accessed=size, transcendentals=0),
        compiler_params=pltpu.CompilerParams(vmem_limit_bytes=room),
        name=name,
    )(*args)


def lat_swapped(strip):
    return lax.ppermute(strip, "lat", [(0, 1), (1, 0)])


def lon_swapped(to_even, to_odd):
    count = lax.axis_size("lon")
    even = [(i, i ^ 1) for i in range(count)]
    odd = [(i, (((i - 1) % count ^ 1) + 1) % count) for i in range(count)]
    return lax.ppermute(to_even, "lon", even), lax.ppermute(to_odd, "lon", odd)


def chips_swapped(parts):
    return lax.all_to_all(parts, ("hour_0", "hour_1"), 0, 0, tiled=True)


def cores_swapped(parts):
    return lax.ppermute(parts, "hour_2", [(0, 1), (1, 0)])


def per_device(precip, scaling, hour_weight, cotangent):
    rainfall = precip[0]
    incoming = scaling[0]
    upstream = cotangent[0]
    band3, band4, around = row_band(BLOCK), row_band(EDGE), col_band()
    bands = (*band3, *band4, *around)
    to_lat = lat_strip(incoming, rainfall)
    lat_in = lat_swapped(to_lat)
    even, odd = lon_swapped(
        *call(
            lon_kernel, (incoming, rainfall, lat_in), ((STRIP, WIDE), (STRIP, WIDE)),
            name="lon_edges",
        )
    )
    shared = (CHIPS, 2 * EDGE, EDGE)
    whole = (PIECES, EDGE, EDGE)
    slope, share, second, logs, keep, give = call(
        forward_kernel,
        (hour_weight, incoming, rainfall, upstream, lat_in, even, odd, *bands),
        ((TALL, WIDE), (ROWS, COLS), whole, whole, shared, shared),
        scratch=((TALLER, WIDE), (TALL, WIDE), (EDGE, WIDE), (TALL, WIDE)),
        scalars=1,
        flops=4 * 10**9,
        room=14 << 20,
        name="forward",
    )
    (sums,) = call(pair_kernel, (keep, cores_swapped(give)), (shared,), name="pair")
    (owned,) = call(owner_kernel, (chips_swapped(sums),), (shared,), name="owner")
    mine = chips_swapped(owned)
    (pieces,) = call(
        db_kernel, (hour_weight, mine, cores_swapped(mine), upstream, second, logs), (whole,),
        scalars=1, name="db",
    )
    (to_lat,) = call(back_lat_kernel, (pieces,), ((2 * RADIUS, COLS),), name="back_lat_edges")
    lat_in = lat_swapped(to_lat)
    even, odd = lon_swapped(
        *call(
            back_lon_kernel, (pieces, lat_in), ((2 * RADIUS, WIDE), (2 * RADIUS, WIDE)),
            name="back_lon_edges",
        )
    )
    precip_part, sloped, slope_edge, share_edge = call(
        back_first_kernel,
        (pieces, slope, share, *band3, *around),
        ((ROWS, COLS), (TALL, WIDE), (48, WIDE), (48, WIDE)),
        scratch=((TALLER, COLS),),
        flops=2 * 10**9,
        room=14 << 20,
        name="back_first",
    )
    (scaling_part,) = call(
        back_second_kernel, (sloped, *band4, *around), ((ROWS, COLS),),
        flops=2 * 10**9, room=14 << 20, name="back_second",
    )
    grad_precip, grad_scaling = call(
        back_halo_kernel,
        (lat_in, even, odd, slope_edge, share_edge, precip_part, scaling_part, *edge_bands()),
        ((ROWS, COLS), (ROWS, COLS)),
        scratch=(
            (48, WIDE), (EDGE, EDGE), (EDGE, ROWS), (ROWS, 2 * EDGE), (ROWS, 2 * EDGE),
            (4, 2 * RADIUS, 2 * EDGE),
        ),
        flops=10**9,
        room=14 << 20,
        name="back_halo",
        copies=10,
        out_hbm=True,
    )
    return (grad_precip[None], grad_scaling[None])


def solution(mesh):
    split_mesh = Mesh(
        mesh.devices.reshape(4, 2, 2, mesh.shape["lat"], mesh.shape["lon"]),
        ("hour_0", "hour_1", "hour_2", "lat", "lon"),
    )
    return jax.shard_map(
        per_device,
        mesh=split_mesh,
        in_specs=(P(HOUR, "lat", "lon"), P(HOUR, "lat", "lon"), P(HOUR), P(HOUR, "lat", "lon")),
        out_specs=(P(HOUR, "lat", "lon"), P(HOUR, "lat", "lon")),
        check_vma=False,
    )
```

```python
import numpy as np
import jax
import jax.numpy as jnp
from jax import lax
from jax.experimental import pallas as pl
from jax.experimental.pallas import tpu as pltpu
from jax.sharding import Mesh
from jax.sharding import PartitionSpec as P


RADIUS = 8
HOUR = ("hour_0", "hour_1", "hour_2")
PHI = 0.8
SPREAD = 50.0

ROWS = 512
COLS = 512
WIDE = 640
EDGE = 128
TALL = ROWS + 2 * RADIUS
TALLER = ROWS + 4 * RADIUS
BLOCK = TALL // 3
PIECES = 16
CHIPS = 8
ORDER = (5, 7, 3, 1, 4, 2, 6)
PIECE = ROWS // PIECES
STRIP = 3 * RADIUS
F32 = jnp.float32
BF16 = jnp.bfloat16


def taps_of(spacing):
    offsets = np.arange(-RADIUS, RADIUS + 1).astype(np.float64)
    total = np.sum(np.exp(-offsets * offsets / SPREAD))
    return np.where(np.abs(spacing) <= RADIUS, np.exp(-spacing * spacing / SPREAD) / total, 0.0)


def halves(matrix):
    matrix = matrix.astype(np.float32)
    high = matrix.astype(jnp.bfloat16)
    low = (matrix - high.astype(np.float32)).astype(jnp.bfloat16)
    return jnp.asarray(high), jnp.asarray(low)


def row_band(size):
    outer = np.arange(size)[:, None]
    inner = np.arange(size + 2 * RADIUS)[None, :]
    return halves(taps_of((inner - outer - RADIUS).astype(np.float64)))


def edge_bands():
    outer = np.arange(2 * RADIUS)[:, None]
    inner = np.arange(2 * RADIUS)[None, :]
    low = taps_of((inner - outer - RADIUS).astype(np.float64))
    high = taps_of((inner - outer + RADIUS).astype(np.float64))
    stacks = np.zeros((2, 48, 48))
    for lat, along in enumerate((high, low)):
        for k, band in enumerate((along, low, high)):
            stacks[lat, 16 * k : 16 * (k + 1), 16 * k : 16 * (k + 1)] = band
    return halves(stacks)


def col_band():
    outer = np.arange(2 * EDGE)[None, :]
    inner = np.arange(4 * EDGE)[:, None]
    return halves(taps_of((inner - EDGE - outer).astype(np.float64)))


def split(x):
    high = x.astype(BF16)
    return high, (x - high.astype(F32)).astype(BF16)


def dot(a, b):
    return jnp.dot(a, b, preferred_element_type=F32)


def rows_pass(x, high, low):
    xh, xl = split(x)
    return dot(high[...], xh) + (dot(low[...], xh) + dot(high[...], xl))


def cols_piece(rh, rl, ch, cl, spans, count):
    total = None
    for lo, hi, at in spans:
        high, low = ch[at : at + hi - lo, 0:count], cl[at : at + hi - lo, 0:count]
        part = dot(rh[:, lo:hi], high) + (dot(rl[:, lo:hi], high) + dot(rh[:, lo:hi], low))
        total = part if total is None else total + part
    return total


def cols_pass(r, ch, cl, halo):
    rh, rl = split(r)
    pieces = [
        cols_piece(rh, rl, ch, cl, ((512, 640, 0), (0, 384, 128)), 256),
        cols_piece(rh, rl, ch, cl, ((128, 640, 0),), 256),
    ]
    if halo:
        pieces.append(cols_piece(rh, rl, ch, cl, ((384, 640, 0), (0, 128, 256)), 128))
    return jnp.concatenate(pieces, axis=1)


def valid_part(start, count, lat):
    row = lax.broadcasted_iota(jnp.int32, (count, WIDE), 0) + start
    lane = lax.broadcasted_iota(jnp.int32, (count, WIDE), 1)
    inside = (row >= jnp.where(lat == 0, RADIUS, 0)) & (
        row < jnp.where(lat == 0, TALL, TALL - RADIUS)
    )
    return inside & ((lane < COLS + RADIUS) | (lane >= WIDE - RADIUS))


def my_lat():
    return lax.axis_index("lat")


def my_parity():
    return lax.axis_index("lon") & 1


def fill_edges(ext, reach, rows_in, even, odd, side):
    lat, parity = my_lat(), my_parity()
    side[...] = jnp.zeros((EDGE, WIDE), F32)
    side[0:reach, :] = jnp.where(parity == 0, even, odd)
    side[EDGE - reach : EDGE, :] = jnp.where(parity == 0, odd, even)
    flat = jnp.transpose(side[...])
    corner = flat[ROWS : ROWS + reach]
    ext[reach : reach + ROWS, COLS:WIDE] = flat[0:ROWS]
    ext[0:reach, 0:COLS] = jnp.where(lat == 1, rows_in, 0.0)
    ext[0:reach, COLS:WIDE] = jnp.where(lat == 1, corner, 0.0)
    ext[reach + ROWS : 2 * reach + ROWS, 0:COLS] = jnp.where(lat == 0, rows_in, 0.0)
    ext[reach + ROWS : 2 * reach + ROWS, COLS:WIDE] = jnp.where(lat == 0, corner, 0.0)


def column_strips(reach, first_block, last_block, rows_in, parity):
    spare = jnp.zeros((EDGE - reach, EDGE), F32)
    left = jnp.transpose(jnp.concatenate([first_block, rows_in[:, 0:EDGE], spare], axis=0))
    right = jnp.transpose(
        jnp.concatenate([last_block, rows_in[:, COLS - EDGE : COLS], spare], axis=0)
    )
    left, right = left[0:reach], right[EDGE - reach : EDGE]
    return jnp.where(parity == 0, right, left), jnp.where(parity == 0, left, right)


def lat_kernel(scaling, precip, to_lat, sems):
    wide, narrow = 2 * RADIUS, RADIUS
    keep = 1 - my_lat()
    at = pl.multiple_of(keep * (ROWS - wide), 8)
    near = pl.multiple_of(keep * (ROWS - narrow), 8)
    copies = (
        pltpu.make_async_copy(scaling.at[pl.ds(at, wide), :], to_lat.at[0:wide, :], sems.at[0]),
        pltpu.make_async_copy(
            precip.at[pl.ds(near, narrow), :], to_lat.at[wide:STRIP, :], sems.at[1]
        ),
    )
    for copy in copies:
        copy.start()
    for copy in copies:
        copy.wait()


def in_hbm(x):
    return pltpu.with_memory_space_constraint(x, pltpu.HBM)


def lat_strip(scaling, precip):
    return pl.pallas_call(
        lat_kernel,
        out_shape=jax.ShapeDtypeStruct((STRIP, COLS), F32),
        in_specs=[pl.BlockSpec(memory_space=pltpu.HBM)] * 2,
        out_specs=pl.BlockSpec(memory_space=pltpu.VMEM),
        scratch_shapes=[pltpu.SemaphoreType.DMA((2,))],
        compiler_params=pltpu.CompilerParams(vmem_limit_bytes=2 << 20),
        name="lat_edges",
    )(in_hbm(scaling), in_hbm(precip))


def lon_kernel(scaling, precip, lat_in, to_even, to_odd):
    wide, narrow = 2 * RADIUS, RADIUS
    to_even[0:wide, :], to_odd[0:wide, :] = column_strips(
        wide, scaling[:, 0:EDGE], scaling[:, COLS - EDGE : COLS], lat_in[0:wide, :], my_parity()
    )
    to_even[wide:STRIP, :], to_odd[wide:STRIP, :] = column_strips(
        narrow, precip[:, 0:EDGE], precip[:, COLS - EDGE : COLS], lat_in[wide:STRIP, :], my_parity()
    )


def forward_kernel(
    weight, scaling, precip, upstream, lat_in, even, odd, rh3, rl3, rh4, rl4, ch, cl,
    slope, share, second, logs, keep, give, sx, px, side, lifted,
):
    lat = my_lat()
    core = lax.axis_index("hour_2")
    wide, narrow = 2 * RADIUS, RADIUS
    sx[wide : wide + ROWS, 0:COLS] = scaling[...]
    px[narrow : narrow + ROWS, 0:COLS] = precip[...]
    fill_edges(sx, wide, lat_in[0:wide, :], even[0:wide, :], odd[0:wide, :], side)
    fill_edges(px, narrow, lat_in[wide:STRIP, :], even[wide:STRIP, :], odd[wide:STRIP, :], side)
    for i in range(3):
        at = BLOCK * i
        r = rows_pass(sx[at : at + BLOCK + 2 * RADIUS, :], rh3, rl3)
        a = cols_pass(r, ch, cl, True)
        rain = px[at : at + BLOCK, :]
        inside = valid_part(at, BLOCK, lat)
        u = jnp.where(inside, jnp.exp(PHI * jnp.log(rain / a)), 0.0)
        lifted[at : at + BLOCK, :] = u
        slope[at : at + BLOCK, :] = jnp.where(inside, -PHI * u / a, 0.0)
        lo, hi = max(at, RADIUS), min(at + BLOCK, RADIUS + ROWS)
        here = slice(lo - RADIUS, hi - RADIUS)
        share[here, :] = PHI * u[lo - at : hi - at, 0:COLS] / rain[lo - at : hi - at, 0:COLS]
    for i in range(4):
        at = EDGE * i
        r = rows_pass(lifted[at : at + EDGE + 2 * RADIUS, :], rh4, rl4)
        b = cols_pass(r, ch, cl, False)
        logb = jnp.log(b)
        parts = (weight[0] * logb, upstream[at : at + EDGE, :] * jnp.exp(-PHI * logb))
        for j in range(COLS // EDGE):
            lanes = slice(EDGE * j, EDGE * (j + 1))
            for q in range(EDGE // PIECE):
                rows = slice(PIECE * q, PIECE * (q + 1))
                to = slice(PIECE * j, PIECE * (j + 1))
                second[i * (EDGE // PIECE) + q, to, :] = b[rows, lanes]
                logs[i * (EDGE // PIECE) + q, to, :] = logb[rows, lanes]
            for c in range(2):
                first = slice(2 * PIECE * c, 2 * PIECE * c + PIECE)
                other = slice(2 * PIECE * c + PIECE, 2 * PIECE * (c + 1))
                for k, part in enumerate(parts):
                    to = slice(EDGE * k + PIECE * j, EDGE * k + PIECE * (j + 1))
                    x, y = part[first, lanes], part[other, lanes]
                    keep[2 * i + c, to, :] = jnp.where(core == 0, x, y)
                    give[2 * i + c, to, :] = jnp.where(core == 0, y, x)


def my_chip():
    return lax.axis_index("hour_0") * 2 + lax.axis_index("hour_1")


def pair_kernel(keep, given, *outs):
    chip = my_chip()
    for k, out in enumerate(outs):
        out[...] = keep[chip ^ k] + given[chip ^ k]


def owner_kernel(*refs):
    sums, out = refs[:CHIPS], refs[CHIPS]

    def total(start):
        x = sums[0][start : start + EDGE, :]
        for part in sums[1:]:
            x = x + part[start : start + EDGE, :]
        return x

    logq = total(0)
    out[0:EDGE, :] = logq
    out[EDGE : 2 * EDGE, :] = PHI * jnp.exp(PHI * logq) * total(EDGE)


def gather_kernel(*refs):
    chip = my_chip()
    out = refs[CHIPS]
    for k in range(CHIPS):
        out[chip ^ k] = refs[k][...]


def db_kernel(weight, mine, theirs, upstream, second, logs, pieces):
    core = lax.axis_index("hour_2")
    for p in range(PIECES):
        here = core == p % 2
        for j in range(COLS // EDGE):
            rows = slice(PIECE * j, PIECE * (j + 1))
            low = slice(EDGE + PIECE * j, EDGE + PIECE * (j + 1))
            logq = jnp.where(here, mine[p // 2, rows, :], theirs[p // 2, rows, :])
            dlogq = jnp.where(here, mine[p // 2, low, :], theirs[p // 2, low, :])
            own = upstream[PIECE * p : PIECE * (p + 1), EDGE * j : EDGE * (j + 1)]
            term = PHI * own * jnp.exp(PHI * (logq - logs[p, rows, :]))
            pieces[p, rows, :] = (weight[0] * dlogq - term) / second[p, rows, :]


def tile_column(pieces, j):
    return jnp.concatenate(
        [pieces[p, PIECE * j : PIECE * (j + 1), :] for p in range(PIECES)], axis=0
    )


def back_lat_kernel(pieces, to_lat):
    wide = 2 * RADIUS
    for j in range(COLS // EDGE):
        to_lat[:, EDGE * j : EDGE * (j + 1)] = jnp.where(
            my_lat() == 0,
            pieces[PIECES - 1, PIECE * (j + 1) - wide : PIECE * (j + 1), :],
            pieces[0, PIECE * j : PIECE * j + wide, :],
        )


def back_lon_kernel(pieces, lat_in, to_even, to_odd):
    to_even[...], to_odd[...] = column_strips(
        2 * RADIUS, tile_column(pieces, 0), tile_column(pieces, COLS // EDGE - 1), lat_in[...],
        my_parity(),
    )


def coefficient_strips(slope, share, slope_edge, share_edge):
    wide = 2 * RADIUS
    top = my_lat() == 1
    nothing = jnp.zeros((RADIUS, COLS), F32)
    first, last = slice(0, EDGE), slice(COLS - EDGE, COLS)

    def turned(block):
        gap = jnp.zeros((WIDE - TALL, EDGE), F32)
        return jnp.transpose(jnp.concatenate([block[RADIUS:TALL], gap, block[0:RADIUS]], axis=0))

    near = lax.broadcasted_iota(jnp.int32, (TALL, EDGE), 1) < EDGE // 2
    tile = turned(jnp.where(near, slope[:, first], slope[:, last]))
    halo = turned(slope[:, COLS:WIDE])
    slope_edge[0:wide, :] = jnp.where(top, slope[0:wide, :], slope[TALL - wide : TALL, :])
    slope_edge[16:24, :] = halo[EDGE - RADIUS : EDGE]
    slope_edge[24:32, :] = tile[0:RADIUS]
    slope_edge[32:40, :] = tile[EDGE - RADIUS : EDGE]
    slope_edge[40:48, :] = halo[0:RADIUS]
    tile = jnp.transpose(jnp.where(near[0:ROWS], share[:, first], share[:, last]))
    share_edge[...] = jnp.zeros((48, WIDE), F32)
    share_edge[0:RADIUS, 0:COLS] = jnp.where(top, nothing, share[ROWS - RADIUS : ROWS, :])
    share_edge[RADIUS:wide, 0:COLS] = jnp.where(top, share[0:RADIUS, :], nothing)
    share_edge[24:32, 0:COLS] = tile[0:RADIUS]
    share_edge[32:40, 0:COLS] = tile[EDGE - RADIUS : EDGE]


def back_first_kernel(
    pieces, slope, share, rh3, rl3, ch, cl, grad_precip, sloped, slope_edge, share_edge, dx
):
    coefficient_strips(slope, share, slope_edge, share_edge)
    wide = 2 * RADIUS
    dx[0:wide, :] = jnp.zeros((wide, COLS), F32)
    dx[wide + ROWS : TALLER, :] = jnp.zeros((wide, COLS), F32)
    for p in range(PIECES):
        for j in range(COLS // EDGE):
            dx[wide + PIECE * p : wide + PIECE * (p + 1), EDGE * j : EDGE * (j + 1)] = pieces[
                p, PIECE * j : PIECE * (j + 1), :
            ]
    for i in range(3):
        at = BLOCK * i
        rh, rl = split(rows_pass(dx[at : at + BLOCK + 2 * RADIUS, :], rh3, rl3))
        du = jnp.concatenate(
            [
                cols_piece(rh, rl, ch, cl, ((0, 384, 128),), 256),
                cols_piece(rh, rl, ch, cl, ((128, 512, 0),), 256),
                cols_piece(rh, rl, ch, cl, ((384, 512, 0), (0, 128, 256)), 128),
            ],
            axis=1,
        )
        sloped[at : at + BLOCK, :] = slope[at : at + BLOCK, :] * du
        lo, hi = max(at, RADIUS), min(at + BLOCK, RADIUS + ROWS)
        here = slice(lo - RADIUS, hi - RADIUS)
        grad_precip[here, :] = share[here, :] * du[lo - at : hi - at, 0:COLS]


def back_second_kernel(sloped, rh4, rl4, ch, cl, grad_scaling):
    for i in range(4):
        at = EDGE * i
        r = rows_pass(sloped[at : at + EDGE + 2 * RADIUS, :], rh4, rl4)
        grad_scaling[at : at + EDGE, :] = cols_pass(r, ch, cl, False)


def around_pass(x):
    taps = taps_of(np.arange(RADIUS + 1).astype(np.float64))
    total = float(taps[0]) * x
    for d in range(1, RADIUS + 1):
        total += float(taps[d]) * (pltpu.roll(x, d, 1) + pltpu.roll(x, WIDE - d, 1))
    return total


def back_halo_kernel(
    lat_in, even, odd, slope_edge, share_edge, precip_part, scaling_part, dh, dl,
    precip_out, scaling_out, strips, square, flat, precip_edge, scaling_edge, middle, sems,
):
    wide = 2 * RADIUS
    lat, parity = my_lat(), my_parity()
    top = lat == 1
    inner = slice(EDGE, COLS - EDGE)
    last = slice(COLS - EDGE, COLS)
    copies = []

    def sent(src, dst):
        copies.append(pltpu.make_async_copy(src, dst, sems.at[len(copies)]))
        copies[-1].start()

    for part, out in ((precip_part, precip_out), (scaling_part, scaling_out)):
        sent(part.at[wide : ROWS - wide, inner], out.at[wide : ROWS - wide, inner])

    right = jnp.where(parity == 0, even[...], odd[...])
    left = jnp.where(parity == 0, odd[...], even[...])
    square[...] = jnp.zeros((EDGE, EDGE), F32)
    square[0:wide, :] = right[:, COLS:WIDE]
    square[EDGE - wide : EDGE, :] = left[:, COLS:WIDE]
    strips[...] = jnp.zeros((48, WIDE), F32)
    strips[0:16, 0:COLS] = lat_in[...]
    strips[0:16, COLS:WIDE] = jnp.transpose(square[...])[0:wide]
    strips[16:32, 0:COLS] = left[:, 0:COLS]
    strips[32:48, 0:COLS] = right[:, 0:COLS]
    band_h, band_l = dh[lat], dl[lat]

    def smoothed(x):
        xh, xl = split(x)
        return around_pass(dot(band_h, xh) + (dot(band_l, xh) + dot(band_h, xl)))

    du = smoothed(strips[...])
    precip_more = share_edge[...] * du
    scaling_more = smoothed(slope_edge[...] * du)
    nothing = jnp.zeros((RADIUS, COLS), F32)
    near = lax.broadcasted_iota(jnp.int32, (ROWS, EDGE), 1) < EDGE // 2

    def finished(k, part, out, edges, reach, low, high, first, final):
        flat[...] = jnp.zeros((EDGE, ROWS), F32)
        flat[0:reach, :] = low
        flat[EDGE - reach : EDGE, :] = high
        turned = jnp.transpose(flat[...])
        middle[2 * k] = part[0:wide, inner] + first[:, inner]
        middle[2 * k + 1] = part[ROWS - wide : ROWS, inner] + final[:, inner]
        sent(middle.at[2 * k], out.at[0:wide, inner])
        sent(middle.at[2 * k + 1], out.at[ROWS - wide : ROWS, inner])
        edges[:, 0:EDGE] = part[:, 0:EDGE] + jnp.where(near, turned, 0.0)
        edges[:, EDGE : 2 * EDGE] = part[:, last] + jnp.where(near, 0.0, turned)
        for q, lanes in enumerate((slice(0, EDGE), last)):
            mine = slice(EDGE * q, EDGE * (q + 1))
            edges[0:wide, mine] += first[:, lanes]
            edges[ROWS - wide : ROWS, mine] += final[:, lanes]
            sent(edges.at[:, mine], out.at[:, lanes])

    finished(
        0, precip_part, precip_out, precip_edge, RADIUS,
        precip_more[24:32, 0:COLS], precip_more[32:40, 0:COLS],
        jnp.concatenate([precip_more[RADIUS:wide, 0:COLS], nothing], axis=0),
        jnp.concatenate([nothing, precip_more[0:RADIUS, 0:COLS]], axis=0),
    )
    added = scaling_more[0:wide, 0:COLS]
    finished(
        1, scaling_part, scaling_out, scaling_edge, wide,
        scaling_more[16:32, 0:COLS], scaling_more[32:48, 0:COLS],
        jnp.where(top, added, 0.0), jnp.where(top, 0.0, added),
    )
    for copy in copies:
        copy.wait()


def in_vmem(*shapes):
    return [pltpu.VMEM(shape, F32) for shape in shapes]


def call(
    kernel, args, outs, scratch=(), scalars=0, flops=0, room=4 << 20, copies=0,
    out_hbm=False,
):
    size = sum(4 * a.size for a in args) + sum(4 * int(np.prod(o)) for o in outs)
    where = pltpu.HBM if out_hbm else pltpu.VMEM
    spaces = [
        pltpu.SMEM if k < scalars else pltpu.VMEM
        for k in range(len(args))
    ]
    sems = [pltpu.SemaphoreType.DMA((copies,))] if copies else []
    return pl.pallas_call(
        kernel,
        out_shape=[pltpu.HBM(o, F32) if out_hbm else jax.ShapeDtypeStruct(o, F32) for o in outs],
        in_specs=[pl.BlockSpec(memory_space=space) for space in spaces],
        out_specs=[pl.BlockSpec(memory_space=where)] * len(outs),
        scratch_shapes=in_vmem(*scratch) + sems,
        cost_estimate=pl.CostEstimate(flops=flops, bytes_accessed=size, transcendentals=0),
        compiler_params=pltpu.CompilerParams(vmem_limit_bytes=room),
    )(*args)


def lat_swapped(strip):
    return lax.ppermute(strip, "lat", [(0, 1), (1, 0)])


def lon_swapped(to_even, to_odd):
    count = lax.axis_size("lon")
    even = [(i, i ^ 1) for i in range(count)]
    odd = [(i, (((i - 1) % count ^ 1) + 1) % count) for i in range(count)]
    return lax.ppermute(to_even, "lon", even), lax.ppermute(to_odd, "lon", odd)


def chips_swapped(parts):
    moved = {0: parts[0]}
    for k in ORDER:
        pairs = [(i, i ^ k) for i in range(CHIPS)]
        moved[k] = lax.ppermute(parts[k], ("hour_0", "hour_1"), pairs)
    return [moved[k] for k in range(CHIPS)]


def cores_swapped(parts):
    return lax.ppermute(parts, "hour_2", [(0, 1), (1, 0)])


def per_device(precip, scaling, hour_weight, cotangent):
    rainfall = precip[0]
    incoming = scaling[0]
    upstream = cotangent[0]
    band3, band4, around = row_band(BLOCK), row_band(EDGE), col_band()
    bands = (*band3, *band4, *around)
    to_lat = lat_strip(incoming, rainfall)
    lat_in = lat_swapped(to_lat)
    even, odd = lon_swapped(
        *call(lon_kernel, (incoming, rainfall, lat_in), ((STRIP, WIDE), (STRIP, WIDE)))
    )
    shared = (CHIPS, 2 * EDGE, EDGE)
    whole = (PIECES, EDGE, EDGE)
    slope, share, second, logs, keep, give = call(
        forward_kernel,
        (hour_weight, incoming, rainfall, upstream, lat_in, even, odd, *bands),
        ((TALL, WIDE), (ROWS, COLS), whole, whole, shared, shared),
        scratch=((TALLER, WIDE), (TALL, WIDE), (EDGE, WIDE), (TALL, WIDE)),
        scalars=1,
        flops=4 * 10**9,
        room=14 << 20,
    )
    one = shared[1:]
    sums = call(pair_kernel, (keep, cores_swapped(give)), (one,) * CHIPS)
    (owned,) = call(owner_kernel, chips_swapped(sums), (one,))
    (mine,) = call(gather_kernel, chips_swapped([owned] * CHIPS), (shared,))
    (pieces,) = call(
        db_kernel, (hour_weight, mine, cores_swapped(mine), upstream, second, logs), (whole,),
        scalars=1,
    )
    (to_lat,) = call(back_lat_kernel, (pieces,), ((2 * RADIUS, COLS),))
    lat_in = lat_swapped(to_lat)
    even, odd = lon_swapped(
        *call(back_lon_kernel, (pieces, lat_in), ((2 * RADIUS, WIDE), (2 * RADIUS, WIDE)))
    )
    precip_part, sloped, slope_edge, share_edge = call(
        back_first_kernel,
        (pieces, slope, share, *band3, *around),
        ((ROWS, COLS), (TALL, WIDE), (48, WIDE), (48, WIDE)),
        scratch=((TALLER, COLS),),
        flops=2 * 10**9,
        room=14 << 20,
    )
    (scaling_part,) = call(
        back_second_kernel, (sloped, *band4, *around), ((ROWS, COLS),),
        flops=2 * 10**9, room=14 << 20,
    )
    grad_precip, grad_scaling = call(
        back_halo_kernel,
        (lat_in, even, odd, slope_edge, share_edge, precip_part, scaling_part, *edge_bands()),
        ((ROWS, COLS), (ROWS, COLS)),
        scratch=(
            (48, WIDE), (EDGE, EDGE), (EDGE, ROWS), (ROWS, 2 * EDGE), (ROWS, 2 * EDGE),
            (4, 2 * RADIUS, 2 * EDGE),
        ),
        flops=10**9,
        room=14 << 20,
        copies=10,
        out_hbm=True,
    )
    return (grad_precip[None], grad_scaling[None])


def solution(mesh):
    split_mesh = Mesh(
        mesh.devices.reshape(4, 2, 2, mesh.shape["lat"], mesh.shape["lon"]),
        ("hour_0", "hour_1", "hour_2", "lat", "lon"),
    )
    return jax.shard_map(
        per_device,
        mesh=split_mesh,
        in_specs=(P(HOUR, "lat", "lon"), P(HOUR, "lat", "lon"), P(HOUR), P(HOUR, "lat", "lon")),
        out_specs=(P(HOUR, "lat", "lon"), P(HOUR, "lat", "lon")),
        check_vma=False,
    )
```

```python
import numpy as np
import jax
import jax.numpy as jnp
from jax import lax
from jax.experimental import pallas as pl
from jax.experimental.pallas import tpu as pltpu
from jax.sharding import Mesh
from jax.sharding import PartitionSpec as P


RADIUS = 8
HOUR = ("hour_0", "hour_1", "hour_2")
PHI = 0.8
SPREAD = 50.0

ROWS = 512
COLS = 512
WIDE = 640
EDGE = 128
TALL = ROWS + 2 * RADIUS
TALLER = ROWS + 4 * RADIUS
BLOCK = TALL // 3
PIECES = 16
CHIPS = 8
PIECE = ROWS // PIECES
STRIP = 3 * RADIUS
F32 = jnp.float32
BF16 = jnp.bfloat16


def taps_of(spacing):
    offsets = np.arange(-RADIUS, RADIUS + 1).astype(np.float64)
    total = np.sum(np.exp(-offsets * offsets / SPREAD))
    return np.where(np.abs(spacing) <= RADIUS, np.exp(-spacing * spacing / SPREAD) / total, 0.0)


def halves(matrix):
    matrix = matrix.astype(np.float32)
    high = matrix.astype(jnp.bfloat16)
    low = (matrix - high.astype(np.float32)).astype(jnp.bfloat16)
    return jnp.asarray(high), jnp.asarray(low)


def row_band(size):
    outer = np.arange(size)[:, None]
    inner = np.arange(size + 2 * RADIUS)[None, :]
    return halves(taps_of((inner - outer - RADIUS).astype(np.float64)))


def edge_bands():
    outer = np.arange(2 * RADIUS)[:, None]
    inner = np.arange(2 * RADIUS)[None, :]
    low = taps_of((inner - outer - RADIUS).astype(np.float64))
    high = taps_of((inner - outer + RADIUS).astype(np.float64))
    stacks = np.zeros((2, 48, 48))
    for lat, along in enumerate((high, low)):
        for k, band in enumerate((along, low, high)):
            stacks[lat, 16 * k : 16 * (k + 1), 16 * k : 16 * (k + 1)] = band
    return halves(stacks)


def col_band():
    outer = np.arange(2 * EDGE)[None, :]
    inner = np.arange(4 * EDGE)[:, None]
    return halves(taps_of((inner - EDGE - outer).astype(np.float64)))


def split(x):
    high = x.astype(BF16)
    return high, (x - high.astype(F32)).astype(BF16)


def dot(a, b):
    return jnp.dot(a, b, preferred_element_type=F32)


def rows_pass(x, high, low):
    xh, xl = split(x)
    return dot(high[...], xh) + (dot(low[...], xh) + dot(high[...], xl))


def cols_piece(rh, rl, ch, cl, spans, count):
    total = None
    for lo, hi, at in spans:
        high, low = ch[at : at + hi - lo, 0:count], cl[at : at + hi - lo, 0:count]
        part = dot(rh[:, lo:hi], high) + (dot(rl[:, lo:hi], high) + dot(rh[:, lo:hi], low))
        total = part if total is None else total + part
    return total


def cols_pass(r, ch, cl, halo):
    rh, rl = split(r)
    pieces = [
        cols_piece(rh, rl, ch, cl, ((512, 640, 0), (0, 384, 128)), 256),
        cols_piece(rh, rl, ch, cl, ((128, 640, 0),), 256),
    ]
    if halo:
        pieces.append(cols_piece(rh, rl, ch, cl, ((384, 640, 0), (0, 128, 256)), 128))
    return jnp.concatenate(pieces, axis=1)


def valid_part(start, count, lat):
    row = lax.broadcasted_iota(jnp.int32, (count, WIDE), 0) + start
    lane = lax.broadcasted_iota(jnp.int32, (count, WIDE), 1)
    inside = (row >= jnp.where(lat == 0, RADIUS, 0)) & (
        row < jnp.where(lat == 0, TALL, TALL - RADIUS)
    )
    return inside & ((lane < COLS + RADIUS) | (lane >= WIDE - RADIUS))


def my_lat():
    return lax.axis_index("lat")


def my_parity():
    return lax.axis_index("lon") & 1


def fill_edges(ext, reach, rows_in, even, odd, side):
    lat, parity = my_lat(), my_parity()
    side[...] = jnp.zeros((EDGE, WIDE), F32)
    side[0:reach, :] = jnp.where(parity == 0, even, odd)
    side[EDGE - reach : EDGE, :] = jnp.where(parity == 0, odd, even)
    flat = jnp.transpose(side[...])
    corner = flat[ROWS : ROWS + reach]
    ext[reach : reach + ROWS, COLS:WIDE] = flat[0:ROWS]
    ext[0:reach, 0:COLS] = jnp.where(lat == 1, rows_in, 0.0)
    ext[0:reach, COLS:WIDE] = jnp.where(lat == 1, corner, 0.0)
    ext[reach + ROWS : 2 * reach + ROWS, 0:COLS] = jnp.where(lat == 0, rows_in, 0.0)
    ext[reach + ROWS : 2 * reach + ROWS, COLS:WIDE] = jnp.where(lat == 0, corner, 0.0)


def column_strips(reach, first_block, last_block, rows_in, parity):
    spare = jnp.zeros((EDGE - reach, EDGE), F32)
    left = jnp.transpose(jnp.concatenate([first_block, rows_in[:, 0:EDGE], spare], axis=0))
    right = jnp.transpose(
        jnp.concatenate([last_block, rows_in[:, COLS - EDGE : COLS], spare], axis=0)
    )
    left, right = left[0:reach], right[EDGE - reach : EDGE]
    return jnp.where(parity == 0, right, left), jnp.where(parity == 0, left, right)


def lat_kernel(scaling, precip, to_lat, sems):
    wide, narrow = 2 * RADIUS, RADIUS
    keep = 1 - my_lat()
    at = pl.multiple_of(keep * (ROWS - wide), 8)
    near = pl.multiple_of(keep * (ROWS - narrow), 8)
    copies = (
        pltpu.make_async_copy(scaling.at[pl.ds(at, wide), :], to_lat.at[0:wide, :], sems.at[0]),
        pltpu.make_async_copy(
            precip.at[pl.ds(near, narrow), :], to_lat.at[wide:STRIP, :], sems.at[1]
        ),
    )
    for copy in copies:
        copy.start()
    for copy in copies:
        copy.wait()


def in_hbm(x):
    return pltpu.with_memory_space_constraint(x, pltpu.HBM)


def lat_strip(scaling, precip):
    return pl.pallas_call(
        lat_kernel,
        out_shape=jax.ShapeDtypeStruct((STRIP, COLS), F32),
        in_specs=[pl.BlockSpec(memory_space=pltpu.HBM)] * 2,
        out_specs=pl.BlockSpec(memory_space=pltpu.VMEM),
        scratch_shapes=[pltpu.SemaphoreType.DMA((2,))],
        compiler_params=pltpu.CompilerParams(vmem_limit_bytes=2 << 20),
        name="lat_edges",
    )(in_hbm(scaling), in_hbm(precip))


def lon_kernel(scaling, precip, lat_in, to_even, to_odd):
    wide, narrow = 2 * RADIUS, RADIUS
    to_even[0:wide, :], to_odd[0:wide, :] = column_strips(
        wide, scaling[:, 0:EDGE], scaling[:, COLS - EDGE : COLS], lat_in[0:wide, :], my_parity()
    )
    to_even[wide:STRIP, :], to_odd[wide:STRIP, :] = column_strips(
        narrow, precip[:, 0:EDGE], precip[:, COLS - EDGE : COLS], lat_in[wide:STRIP, :], my_parity()
    )


def forward_kernel(
    weight, scaling, precip, upstream, lat_in, even, odd, rh3, rl3, rh4, rl4, ch, cl,
    slope, share, second, logs, keep_even, keep_odd, give_even, give_odd, sx, px, side, lifted,
):
    lat = my_lat()
    core = lax.axis_index("hour_2")
    far, near = lax.axis_index("hour_0"), lax.axis_index("hour_1")
    wide, narrow = 2 * RADIUS, RADIUS
    sx[wide : wide + ROWS, 0:COLS] = scaling[...]
    px[narrow : narrow + ROWS, 0:COLS] = precip[...]
    fill_edges(sx, wide, lat_in[0:wide, :], even[0:wide, :], odd[0:wide, :], side)
    fill_edges(px, narrow, lat_in[wide:STRIP, :], even[wide:STRIP, :], odd[wide:STRIP, :], side)
    for i in range(3):
        at = BLOCK * i
        r = rows_pass(sx[at : at + BLOCK + 2 * RADIUS, :], rh3, rl3)
        a = cols_pass(r, ch, cl, True)
        rain = px[at : at + BLOCK, :]
        inside = valid_part(at, BLOCK, lat)
        u = jnp.where(inside, jnp.exp(PHI * jnp.log(rain / a)), 0.0)
        lifted[at : at + BLOCK, :] = u
        slope[at : at + BLOCK, :] = jnp.where(inside, -PHI * u / a, 0.0)
        lo, hi = max(at, RADIUS), min(at + BLOCK, RADIUS + ROWS)
        here = slice(lo - RADIUS, hi - RADIUS)
        share[here, :] = PHI * u[lo - at : hi - at, 0:COLS] / rain[lo - at : hi - at, 0:COLS]
    for i in range(4):
        at = EDGE * i
        r = rows_pass(lifted[at : at + EDGE + 2 * RADIUS, :], rh4, rl4)
        b = cols_pass(r, ch, cl, False)
        logb = jnp.log(b)
        parts = (weight[0] * logb, upstream[at : at + EDGE, :] * jnp.exp(-PHI * logb))
        for j in range(COLS // EDGE):
            lanes = slice(EDGE * j, EDGE * (j + 1))
            for q in range(EDGE // PIECE):
                rows = slice(PIECE * q, PIECE * (q + 1))
                to = slice(PIECE * j, PIECE * (j + 1))
                second[i * (EDGE // PIECE) + q, to, :] = b[rows, lanes]
                logs[i * (EDGE // PIECE) + q, to, :] = logb[rows, lanes]
            for k, part in enumerate(parts):
                to = slice(EDGE * k + PIECE * j, EDGE * k + PIECE * (j + 1))
                four = [part[PIECE * q : PIECE * (q + 1), lanes] for q in range(4)]
                stay = [jnp.where(core == 0, four[2 * c], four[2 * c + 1]) for c in range(2)]
                leave = [jnp.where(core == 0, four[2 * c + 1], four[2 * c]) for c in range(2)]
                keep_even[i ^ far, to, :] = jnp.where(near == 0, stay[0], stay[1])
                keep_odd[i ^ far, to, :] = jnp.where(near == 0, stay[1], stay[0])
                give_even[i ^ far, to, :] = jnp.where(near == 0, leave[0], leave[1])
                give_odd[i ^ far, to, :] = jnp.where(near == 0, leave[1], leave[0])


def pair_kernel(keep, given, *outs):
    for k, out in enumerate(outs):
        out[...] = keep[k] + given[k]


def owner_kernel(*refs):
    sums, out = refs[:CHIPS], refs[CHIPS]

    def total(start):
        x = sums[0][start : start + EDGE, :]
        for part in sums[1:]:
            x = x + part[start : start + EDGE, :]
        return x

    logq = total(0)
    out[0:EDGE, :] = logq
    out[EDGE : 2 * EDGE, :] = PHI * jnp.exp(PHI * logq) * total(EDGE)


def gather_kernel(*refs):
    for k in range(CHIPS // 2):
        refs[-1][k] = refs[k][...]


def db_kernel(
    weight, even, odd, their_even, their_odd, upstream, second, logs, pieces
):
    core = lax.axis_index("hour_2")
    far, near = lax.axis_index("hour_0"), lax.axis_index("hour_1")
    for i in range(CHIPS // 2):
        for own in range(2):
            here = core == own
            for j in range(COLS // EDGE):
                rows = slice(PIECE * j, PIECE * (j + 1))
                low = slice(EDGE + PIECE * j, EDGE + PIECE * (j + 1))
                found = [
                    [
                        jnp.where(here, mine[i ^ far, part, :], theirs[i ^ far, part, :])
                        for part in (rows, low)
                    ]
                    for mine, theirs in ((even, their_even), (odd, their_odd))
                ]
                for c in range(2):
                    logq, dlogq = (
                        jnp.where(near == c, same, other) for same, other in zip(*found)
                    )
                    p = 4 * i + 2 * c + own
                    value = upstream[PIECE * p : PIECE * (p + 1), EDGE * j : EDGE * (j + 1)]
                    term = PHI * value * jnp.exp(PHI * (logq - logs[p, rows, :]))
                    pieces[p, rows, :] = (weight[0] * dlogq - term) / second[p, rows, :]


def tile_column(pieces, j):
    return jnp.concatenate(
        [pieces[p, PIECE * j : PIECE * (j + 1), :] for p in range(PIECES)], axis=0
    )


def back_lat_kernel(pieces, to_lat):
    wide = 2 * RADIUS
    for j in range(COLS // EDGE):
        to_lat[:, EDGE * j : EDGE * (j + 1)] = jnp.where(
            my_lat() == 0,
            pieces[PIECES - 1, PIECE * (j + 1) - wide : PIECE * (j + 1), :],
            pieces[0, PIECE * j : PIECE * j + wide, :],
        )


def back_lon_kernel(pieces, lat_in, to_even, to_odd):
    to_even[...], to_odd[...] = column_strips(
        2 * RADIUS, tile_column(pieces, 0), tile_column(pieces, COLS // EDGE - 1), lat_in[...],
        my_parity(),
    )


def coefficient_strips(slope, share, slope_edge, share_edge):
    wide = 2 * RADIUS
    top = my_lat() == 1
    nothing = jnp.zeros((RADIUS, COLS), F32)
    first, last = slice(0, EDGE), slice(COLS - EDGE, COLS)

    def turned(block):
        gap = jnp.zeros((WIDE - TALL, EDGE), F32)
        return jnp.transpose(jnp.concatenate([block[RADIUS:TALL], gap, block[0:RADIUS]], axis=0))

    near = lax.broadcasted_iota(jnp.int32, (TALL, EDGE), 1) < EDGE // 2
    tile = turned(jnp.where(near, slope[:, first], slope[:, last]))
    halo = turned(slope[:, COLS:WIDE])
    slope_edge[0:wide, :] = jnp.where(top, slope[0:wide, :], slope[TALL - wide : TALL, :])
    slope_edge[16:24, :] = halo[EDGE - RADIUS : EDGE]
    slope_edge[24:32, :] = tile[0:RADIUS]
    slope_edge[32:40, :] = tile[EDGE - RADIUS : EDGE]
    slope_edge[40:48, :] = halo[0:RADIUS]
    tile = jnp.transpose(jnp.where(near[0:ROWS], share[:, first], share[:, last]))
    share_edge[...] = jnp.zeros((48, WIDE), F32)
    share_edge[0:RADIUS, 0:COLS] = jnp.where(top, nothing, share[ROWS - RADIUS : ROWS, :])
    share_edge[RADIUS:wide, 0:COLS] = jnp.where(top, share[0:RADIUS, :], nothing)
    share_edge[24:32, 0:COLS] = tile[0:RADIUS]
    share_edge[32:40, 0:COLS] = tile[EDGE - RADIUS : EDGE]


def back_first_kernel(
    pieces, slope, share, rh3, rl3, ch, cl, grad_precip, sloped, slope_edge, share_edge, dx
):
    coefficient_strips(slope, share, slope_edge, share_edge)
    wide = 2 * RADIUS
    dx[0:wide, :] = jnp.zeros((wide, COLS), F32)
    dx[wide + ROWS : TALLER, :] = jnp.zeros((wide, COLS), F32)
    for p in range(PIECES):
        for j in range(COLS // EDGE):
            dx[wide + PIECE * p : wide + PIECE * (p + 1), EDGE * j : EDGE * (j + 1)] = pieces[
                p, PIECE * j : PIECE * (j + 1), :
            ]
    for i in range(3):
        at = BLOCK * i
        rh, rl = split(rows_pass(dx[at : at + BLOCK + 2 * RADIUS, :], rh3, rl3))
        du = jnp.concatenate(
            [
                cols_piece(rh, rl, ch, cl, ((0, 384, 128),), 256),
                cols_piece(rh, rl, ch, cl, ((128, 512, 0),), 256),
                cols_piece(rh, rl, ch, cl, ((384, 512, 0), (0, 128, 256)), 128),
            ],
            axis=1,
        )
        sloped[at : at + BLOCK, :] = slope[at : at + BLOCK, :] * du
        lo, hi = max(at, RADIUS), min(at + BLOCK, RADIUS + ROWS)
        here = slice(lo - RADIUS, hi - RADIUS)
        grad_precip[here, :] = share[here, :] * du[lo - at : hi - at, 0:COLS]


def back_second_kernel(sloped, rh4, rl4, ch, cl, grad_scaling):
    for i in range(4):
        at = EDGE * i
        r = rows_pass(sloped[at : at + EDGE + 2 * RADIUS, :], rh4, rl4)
        grad_scaling[at : at + EDGE, :] = cols_pass(r, ch, cl, False)


def around_pass(x):
    taps = taps_of(np.arange(RADIUS + 1).astype(np.float64))
    total = float(taps[0]) * x
    for d in range(1, RADIUS + 1):
        total += float(taps[d]) * (pltpu.roll(x, d, 1) + pltpu.roll(x, WIDE - d, 1))
    return total


def back_halo_kernel(
    lat_in, even, odd, slope_edge, share_edge, precip_part, scaling_part, dh, dl,
    precip_out, scaling_out, strips, square, flat, precip_edge, scaling_edge, middle, sems,
):
    wide = 2 * RADIUS
    lat, parity = my_lat(), my_parity()
    top = lat == 1
    inner = slice(EDGE, COLS - EDGE)
    last = slice(COLS - EDGE, COLS)
    copies = []

    def sent(src, dst):
        copies.append(pltpu.make_async_copy(src, dst, sems.at[len(copies)]))
        copies[-1].start()

    for part, out in ((precip_part, precip_out), (scaling_part, scaling_out)):
        sent(part.at[wide : ROWS - wide, inner], out.at[wide : ROWS - wide, inner])

    right = jnp.where(parity == 0, even[...], odd[...])
    left = jnp.where(parity == 0, odd[...], even[...])
    square[...] = jnp.zeros((EDGE, EDGE), F32)
    square[0:wide, :] = right[:, COLS:WIDE]
    square[EDGE - wide : EDGE, :] = left[:, COLS:WIDE]
    strips[...] = jnp.zeros((48, WIDE), F32)
    strips[0:16, 0:COLS] = lat_in[...]
    strips[0:16, COLS:WIDE] = jnp.transpose(square[...])[0:wide]
    strips[16:32, 0:COLS] = left[:, 0:COLS]
    strips[32:48, 0:COLS] = right[:, 0:COLS]
    band_h, band_l = dh[lat], dl[lat]

    def smoothed(x):
        xh, xl = split(x)
        return around_pass(dot(band_h, xh) + (dot(band_l, xh) + dot(band_h, xl)))

    du = smoothed(strips[...])
    precip_more = share_edge[...] * du
    scaling_more = smoothed(slope_edge[...] * du)
    nothing = jnp.zeros((RADIUS, COLS), F32)
    near = lax.broadcasted_iota(jnp.int32, (ROWS, EDGE), 1) < EDGE // 2

    def finished(k, part, out, edges, reach, low, high, first, final):
        flat[...] = jnp.zeros((EDGE, ROWS), F32)
        flat[0:reach, :] = low
        flat[EDGE - reach : EDGE, :] = high
        turned = jnp.transpose(flat[...])
        middle[2 * k] = part[0:wide, inner] + first[:, inner]
        middle[2 * k + 1] = part[ROWS - wide : ROWS, inner] + final[:, inner]
        sent(middle.at[2 * k], out.at[0:wide, inner])
        sent(middle.at[2 * k + 1], out.at[ROWS - wide : ROWS, inner])
        edges[:, 0:EDGE] = part[:, 0:EDGE] + jnp.where(near, turned, 0.0)
        edges[:, EDGE : 2 * EDGE] = part[:, last] + jnp.where(near, 0.0, turned)
        for q, lanes in enumerate((slice(0, EDGE), last)):
            mine = slice(EDGE * q, EDGE * (q + 1))
            edges[0:wide, mine] += first[:, lanes]
            edges[ROWS - wide : ROWS, mine] += final[:, lanes]
            sent(edges.at[:, mine], out.at[:, lanes])

    finished(
        0, precip_part, precip_out, precip_edge, RADIUS,
        precip_more[24:32, 0:COLS], precip_more[32:40, 0:COLS],
        jnp.concatenate([precip_more[RADIUS:wide, 0:COLS], nothing], axis=0),
        jnp.concatenate([nothing, precip_more[0:RADIUS, 0:COLS]], axis=0),
    )
    added = scaling_more[0:wide, 0:COLS]
    finished(
        1, scaling_part, scaling_out, scaling_edge, wide,
        scaling_more[16:32, 0:COLS], scaling_more[32:48, 0:COLS],
        jnp.where(top, added, 0.0), jnp.where(top, 0.0, added),
    )
    for copy in copies:
        copy.wait()


def in_vmem(*shapes):
    return [pltpu.VMEM(shape, F32) for shape in shapes]


def call(
    kernel, args, outs, scratch=(), scalars=0, flops=0, room=4 << 20, copies=0,
    out_hbm=False,
):
    size = sum(4 * a.size for a in args) + sum(4 * int(np.prod(o)) for o in outs)
    where = pltpu.HBM if out_hbm else pltpu.VMEM
    spaces = [
        pltpu.SMEM if k < scalars else pltpu.VMEM
        for k in range(len(args))
    ]
    sems = [pltpu.SemaphoreType.DMA((copies,))] if copies else []
    return pl.pallas_call(
        kernel,
        out_shape=[pltpu.HBM(o, F32) if out_hbm else jax.ShapeDtypeStruct(o, F32) for o in outs],
        in_specs=[pl.BlockSpec(memory_space=space) for space in spaces],
        out_specs=[pl.BlockSpec(memory_space=where)] * len(outs),
        scratch_shapes=in_vmem(*scratch) + sems,
        cost_estimate=pl.CostEstimate(flops=flops, bytes_accessed=size, transcendentals=0),
        compiler_params=pltpu.CompilerParams(vmem_limit_bytes=room),
    )(*args)


def lat_swapped(strip):
    return lax.ppermute(strip, "lat", [(0, 1), (1, 0)])


def lon_swapped(to_even, to_odd):
    count = lax.axis_size("lon")
    even = [(i, i ^ 1) for i in range(count)]
    odd = [(i, (((i - 1) % count ^ 1) + 1) % count) for i in range(count)]
    return lax.ppermute(to_even, "lon", even), lax.ppermute(to_odd, "lon", odd)


def chip_swapped(part, k):
    if k == 0:
        return part
    pairs = [(i, i ^ k) for i in range(CHIPS)]
    return lax.ppermute(part, ("hour_0", "hour_1"), pairs)


def cores_swapped(parts):
    return lax.ppermute(parts, "hour_2", [(0, 1), (1, 0)])


def per_device(precip, scaling, hour_weight, cotangent):
    rainfall = precip[0]
    incoming = scaling[0]
    upstream = cotangent[0]
    band3, band4, around = row_band(BLOCK), row_band(EDGE), col_band()
    bands = (*band3, *band4, *around)
    to_lat = lat_strip(incoming, rainfall)
    lat_in = lat_swapped(to_lat)
    even, odd = lon_swapped(
        *call(lon_kernel, (incoming, rainfall, lat_in), ((STRIP, WIDE), (STRIP, WIDE)))
    )
    half = (CHIPS // 2, 2 * EDGE, EDGE)
    whole = (PIECES, EDGE, EDGE)
    slope, share, second, logs, keep_even, keep_odd, give_even, give_odd = call(
        forward_kernel,
        (hour_weight, incoming, rainfall, upstream, lat_in, even, odd, *bands),
        ((TALL, WIDE), (ROWS, COLS), whole, whole, half, half, half, half),
        scratch=((TALLER, WIDE), (TALL, WIDE), (EDGE, WIDE), (TALL, WIDE)),
        scalars=1,
        flops=4 * 10**9,
        room=14 << 20,
    )
    given_odd = cores_swapped(give_odd)
    given_even = cores_swapped(give_even)
    arrived = []
    for keep, given, first in ((keep_odd, given_odd, 1), (keep_even, given_even, 0)):
        sums = call(pair_kernel, (keep, given), (half[1:],) * (CHIPS // 2))
        arrived += [chip_swapped(part, 2 * k + first) for k, part in enumerate(sums)]
    (owned,) = call(owner_kernel, tuple(arrived), (half[1:],))

    def collected(first, *after):
        parts = [chip_swapped(owned, 2 * k + first) for k in range(CHIPS // 2)]
        return call(gather_kernel, (*parts, *after), (half,))[0]

    odd_part = collected(1)
    their_odd = cores_swapped(odd_part)
    even_part = collected(0, odd_part)
    their_even = cores_swapped(even_part)
    (pieces,) = call(
        db_kernel,
        (hour_weight, even_part, odd_part, their_even, their_odd, upstream, second, logs),
        (whole,),
        scalars=1,
    )
    (to_lat,) = call(back_lat_kernel, (pieces,), ((2 * RADIUS, COLS),))
    lat_in = lat_swapped(to_lat)
    even, odd = lon_swapped(
        *call(back_lon_kernel, (pieces, lat_in), ((2 * RADIUS, WIDE), (2 * RADIUS, WIDE)))
    )
    precip_part, sloped, slope_edge, share_edge = call(
        back_first_kernel,
        (pieces, slope, share, *band3, *around),
        ((ROWS, COLS), (TALL, WIDE), (48, WIDE), (48, WIDE)),
        scratch=((TALLER, COLS),),
        flops=2 * 10**9,
        room=14 << 20,
    )
    (scaling_part,) = call(
        back_second_kernel, (sloped, *band4, *around), ((ROWS, COLS),),
        flops=2 * 10**9, room=14 << 20,
    )
    grad_precip, grad_scaling = call(
        back_halo_kernel,
        (lat_in, even, odd, slope_edge, share_edge, precip_part, scaling_part, *edge_bands()),
        ((ROWS, COLS), (ROWS, COLS)),
        scratch=(
            (48, WIDE), (EDGE, EDGE), (EDGE, ROWS), (ROWS, 2 * EDGE), (ROWS, 2 * EDGE),
            (4, 2 * RADIUS, 2 * EDGE),
        ),
        flops=10**9,
        room=14 << 20,
        copies=10,
        out_hbm=True,
    )
    return (grad_precip[None], grad_scaling[None])


def solution(mesh):
    split_mesh = Mesh(
        mesh.devices.reshape(4, 2, 2, mesh.shape["lat"], mesh.shape["lon"]),
        ("hour_0", "hour_1", "hour_2", "lat", "lon"),
    )
    return jax.shard_map(
        per_device,
        mesh=split_mesh,
        in_specs=(P(HOUR, "lat", "lon"), P(HOUR, "lat", "lon"), P(HOUR), P(HOUR, "lat", "lon")),
        out_specs=(P(HOUR, "lat", "lon"), P(HOUR, "lat", "lon")),
        check_vma=False,
    )
```

```python
import numpy as np
import jax
import jax.numpy as jnp
from jax import lax
from jax.experimental import pallas as pl
from jax.experimental.pallas import tpu as pltpu
from jax.sharding import Mesh
from jax.sharding import PartitionSpec as P


RADIUS = 8
HOUR = ("hour_0", "hour_1", "hour_2")
PHI = 0.8
SPREAD = 50.0

ROWS = 512
COLS = 512
WIDE = 640
EDGE = 128
TALL = ROWS + 2 * RADIUS
TALLER = ROWS + 4 * RADIUS
BLOCK = TALL // 3
PIECES = 16
CHIPS = 8
PIECE = ROWS // PIECES
STRIP = 3 * RADIUS
F32 = jnp.float32
BF16 = jnp.bfloat16


def taps_of(spacing):
    offsets = np.arange(-RADIUS, RADIUS + 1).astype(np.float64)
    total = np.sum(np.exp(-offsets * offsets / SPREAD))
    return np.where(np.abs(spacing) <= RADIUS, np.exp(-spacing * spacing / SPREAD) / total, 0.0)


def halves(matrix):
    matrix = matrix.astype(np.float32)
    high = matrix.astype(jnp.bfloat16)
    low = (matrix - high.astype(np.float32)).astype(jnp.bfloat16)
    return jnp.asarray(high), jnp.asarray(low)


def row_band(size):
    outer = np.arange(size)[:, None]
    inner = np.arange(size + 2 * RADIUS)[None, :]
    return jnp.concatenate(halves(taps_of((inner - outer - RADIUS).astype(np.float64))), axis=0)


def edge_bands():
    outer = np.arange(2 * RADIUS)[:, None]
    inner = np.arange(2 * RADIUS)[None, :]
    low = taps_of((inner - outer - RADIUS).astype(np.float64))
    high = taps_of((inner - outer + RADIUS).astype(np.float64))
    stacks = np.zeros((2, 48, 48))
    for lat, along in enumerate((high, low)):
        for k, band in enumerate((along, low, high)):
            stacks[lat, 16 * k : 16 * (k + 1), 16 * k : 16 * (k + 1)] = band
    return halves(stacks)


def col_band():
    outer = np.arange(2 * EDGE)[None, :]
    inner = np.arange(4 * EDGE)[:, None]
    return halves(taps_of((inner - EDGE - outer).astype(np.float64)))


def split(x):
    high = x.astype(BF16)
    return high, (x - high.astype(F32)).astype(BF16)


def dot(a, b):
    return jnp.dot(a, b, preferred_element_type=F32)


def rows_pass(x, both):
    xh, xl = split(x)
    rows = both.shape[0] // 2
    twice = dot(both[...], xh)
    return twice[0:rows] + (twice[rows:] + dot(both[0:rows, :], xl))


def cols_piece(rh, rl, ch, cl, spans, count):
    total = None
    for lo, hi, at in spans:
        high, low = ch[at : at + hi - lo, 0:count], cl[at : at + hi - lo, 0:count]
        rows = rh.shape[0]
        twice = dot(jnp.concatenate([rh[:, lo:hi], rl[:, lo:hi]], axis=0), high)
        part = twice[0:rows] + (twice[rows:] + dot(rh[:, lo:hi], low))
        total = part if total is None else total + part
    return total


def cols_pass(r, ch, cl, halo):
    rh, rl = split(r)
    pieces = [
        cols_piece(rh, rl, ch, cl, ((512, 640, 0), (0, 384, 128)), 256),
        cols_piece(rh, rl, ch, cl, ((128, 640, 0),), 256),
    ]
    if halo:
        pieces.append(cols_piece(rh, rl, ch, cl, ((384, 640, 0), (0, 128, 256)), 128))
    return jnp.concatenate(pieces, axis=1)


def valid_part(start, count, lat):
    row = lax.broadcasted_iota(jnp.int32, (count, WIDE), 0) + start
    lane = lax.broadcasted_iota(jnp.int32, (count, WIDE), 1)
    inside = (row >= jnp.where(lat == 0, RADIUS, 0)) & (
        row < jnp.where(lat == 0, TALL, TALL - RADIUS)
    )
    return inside & ((lane < COLS + RADIUS) | (lane >= WIDE - RADIUS))


def my_lat():
    return lax.axis_index("lat")


def my_parity():
    return lax.axis_index("lon") & 1


def fill_edges(ext, reach, rows_in, even, odd, side):
    lat, parity = my_lat(), my_parity()
    side[...] = jnp.zeros((EDGE, WIDE), F32)
    side[0:reach, :] = jnp.where(parity == 0, even, odd)
    side[EDGE - reach : EDGE, :] = jnp.where(parity == 0, odd, even)
    flat = jnp.transpose(side[...])
    corner = flat[ROWS : ROWS + reach]
    ext[reach : reach + ROWS, COLS:WIDE] = flat[0:ROWS]
    ext[0:reach, 0:COLS] = jnp.where(lat == 1, rows_in, 0.0)
    ext[0:reach, COLS:WIDE] = jnp.where(lat == 1, corner, 0.0)
    ext[reach + ROWS : 2 * reach + ROWS, 0:COLS] = jnp.where(lat == 0, rows_in, 0.0)
    ext[reach + ROWS : 2 * reach + ROWS, COLS:WIDE] = jnp.where(lat == 0, corner, 0.0)


def column_strips(reach, first_block, last_block, rows_in, parity):
    spare = jnp.zeros((EDGE - reach, EDGE), F32)
    left = jnp.transpose(jnp.concatenate([first_block, rows_in[:, 0:EDGE], spare], axis=0))
    right = jnp.transpose(
        jnp.concatenate([last_block, rows_in[:, COLS - EDGE : COLS], spare], axis=0)
    )
    left, right = left[0:reach], right[EDGE - reach : EDGE]
    return jnp.where(parity == 0, right, left), jnp.where(parity == 0, left, right)


def lat_kernel(scaling, precip, to_lat, sems):
    wide, narrow = 2 * RADIUS, RADIUS
    keep = 1 - my_lat()
    at = pl.multiple_of(keep * (ROWS - wide), 8)
    near = pl.multiple_of(keep * (ROWS - narrow), 8)
    copies = (
        pltpu.make_async_copy(scaling.at[pl.ds(at, wide), :], to_lat.at[0:wide, :], sems.at[0]),
        pltpu.make_async_copy(
            precip.at[pl.ds(near, narrow), :], to_lat.at[wide:STRIP, :], sems.at[1]
        ),
    )
    for copy in copies:
        copy.start()
    for copy in copies:
        copy.wait()


def in_hbm(x):
    return pltpu.with_memory_space_constraint(x, pltpu.HBM)


def lat_strip(scaling, precip):
    return pl.pallas_call(
        lat_kernel,
        out_shape=jax.ShapeDtypeStruct((STRIP, COLS), F32),
        in_specs=[pl.BlockSpec(memory_space=pltpu.HBM)] * 2,
        out_specs=pl.BlockSpec(memory_space=pltpu.VMEM),
        scratch_shapes=[pltpu.SemaphoreType.DMA((2,))],
        compiler_params=pltpu.CompilerParams(vmem_limit_bytes=2 << 20),
        name="lat_edges",
    )(in_hbm(scaling), in_hbm(precip))


def lon_kernel(scaling, precip, lat_in, to_even, to_odd):
    wide, narrow = 2 * RADIUS, RADIUS
    to_even[0:wide, :], to_odd[0:wide, :] = column_strips(
        wide, scaling[:, 0:EDGE], scaling[:, COLS - EDGE : COLS], lat_in[0:wide, :], my_parity()
    )
    to_even[wide:STRIP, :], to_odd[wide:STRIP, :] = column_strips(
        narrow, precip[:, 0:EDGE], precip[:, COLS - EDGE : COLS], lat_in[wide:STRIP, :], my_parity()
    )


def forward_kernel(
    scaling, precip, lat_in, even, odd, both3, ch, cl, slope, share, lifted, sx, px, side
):
    lat = my_lat()
    wide, narrow = 2 * RADIUS, RADIUS
    sx[wide : wide + ROWS, 0:COLS] = scaling[...]
    px[narrow : narrow + ROWS, 0:COLS] = precip[...]
    fill_edges(sx, wide, lat_in[0:wide, :], even[0:wide, :], odd[0:wide, :], side)
    fill_edges(px, narrow, lat_in[wide:STRIP, :], even[wide:STRIP, :], odd[wide:STRIP, :], side)
    for i in range(3):
        at = BLOCK * i
        r = rows_pass(sx[at : at + BLOCK + 2 * RADIUS, :], both3)
        a = cols_pass(r, ch, cl, True)
        rain = px[at : at + BLOCK, :]
        inside = valid_part(at, BLOCK, lat)
        u = jnp.where(inside, jnp.exp(PHI * jnp.log(rain / a)), 0.0)
        lifted[at : at + BLOCK, :] = u
        slope[at : at + BLOCK, :] = jnp.where(inside, -PHI * u / a, 0.0)
        lo, hi = max(at, RADIUS), min(at + BLOCK, RADIUS + ROWS)
        here = slice(lo - RADIUS, hi - RADIUS)
        share[here, :] = PHI * u[lo - at : hi - at, 0:COLS] / rain[lo - at : hi - at, 0:COLS]


def half_start(flip):
    near = lax.axis_index("hour_1")
    return pl.multiple_of(((1 - near) if flip else near) * (ROWS // 2), ROWS // 2)


def log_kernel(flip, weight, lifted, upstream, both4, ch, cl, second, logs, keep, give):
    core, far = lax.axis_index("hour_2"), lax.axis_index("hour_0")
    for i in range(2):
        at = half_start(flip) + EDGE * i
        r = rows_pass(lifted[pl.ds(at, EDGE + 2 * RADIUS), :], both4)
        b = cols_pass(r, ch, cl, False)
        logb = jnp.log(b)
        parts = (
            weight[0] * logb, upstream[pl.ds(at, EDGE), :] * jnp.exp(-PHI * logb)
        )
        for j in range(COLS // EDGE):
            lanes = slice(EDGE * j, EDGE * (j + 1))
            four = [slice(PIECE * q, PIECE * (q + 1)) for q in range(4)]
            for q, rows in enumerate(four):
                to = slice(PIECE * j, PIECE * (j + 1))
                second[4 * i + q, to, :] = b[rows, lanes]
                logs[4 * i + q, to, :] = logb[rows, lanes]
            for k, part in enumerate(parts):
                to = slice(EDGE * k + PIECE * j, EDGE * k + PIECE * (j + 1))
                for c in range(2):
                    x, y = part[four[2 * c], lanes], part[four[2 * c + 1], lanes]
                    keep[(2 * i + c) ^ far, to, :] = jnp.where(core == 0, x, y)
                    give[(2 * i + c) ^ far, to, :] = jnp.where(core == 0, y, x)


def pair_kernel(keep, given, *outs):
    for k, out in enumerate(outs):
        out[...] = keep[k] + given[k]


def owner_kernel(*refs):
    sums, out = refs[:CHIPS], refs[CHIPS]

    def total(start):
        x = sums[0][start : start + EDGE, :]
        for part in sums[1:]:
            x = x + part[start : start + EDGE, :]
        return x

    logq = total(0)
    out[0:EDGE, :] = logq
    out[EDGE : 2 * EDGE, :] = PHI * jnp.exp(PHI * logq) * total(EDGE)


def gather_kernel(*refs):
    for k in range(CHIPS // 2):
        refs[-1][k] = refs[k][...]


def db_kernel(
    weight, even, odd, their_even, their_odd, upstream, second_even, second_odd, logs_even,
    logs_odd, pieces,
):
    core, far = lax.axis_index("hour_2"), lax.axis_index("hour_0")
    for flip, mine, theirs, second, logs in (
        (False, even, their_even, second_even, logs_even),
        (True, odd, their_odd, second_odd, logs_odd),
    ):
        start = half_start(flip)
        first = start // PIECE
        for n in range(PIECES // 2):
            here, slot = core == n % 2, (n // 2) ^ far
            for j in range(COLS // EDGE):
                rows = slice(PIECE * j, PIECE * (j + 1))
                low = slice(EDGE + PIECE * j, EDGE + PIECE * (j + 1))
                logq = jnp.where(here, mine[slot, rows, :], theirs[slot, rows, :])
                dlogq = jnp.where(here, mine[slot, low, :], theirs[slot, low, :])
                value = upstream[pl.ds(start + PIECE * n, PIECE), EDGE * j : EDGE * (j + 1)]
                term = PHI * value * jnp.exp(PHI * (logq - logs[n, rows, :]))
                pieces[first + n, rows, :] = (weight[0] * dlogq - term) / second[n, rows, :]


def tile_column(pieces, j):
    return jnp.concatenate(
        [pieces[p, PIECE * j : PIECE * (j + 1), :] for p in range(PIECES)], axis=0
    )


def back_lat_kernel(pieces, to_lat):
    wide = 2 * RADIUS
    for j in range(COLS // EDGE):
        to_lat[:, EDGE * j : EDGE * (j + 1)] = jnp.where(
            my_lat() == 0,
            pieces[PIECES - 1, PIECE * (j + 1) - wide : PIECE * (j + 1), :],
            pieces[0, PIECE * j : PIECE * j + wide, :],
        )


def back_lon_kernel(pieces, lat_in, to_even, to_odd):
    to_even[...], to_odd[...] = column_strips(
        2 * RADIUS, tile_column(pieces, 0), tile_column(pieces, COLS // EDGE - 1), lat_in[...],
        my_parity(),
    )


def coefficient_strips(slope, share, slope_edge, share_edge):
    wide = 2 * RADIUS
    top = my_lat() == 1
    nothing = jnp.zeros((RADIUS, COLS), F32)
    first, last = slice(0, EDGE), slice(COLS - EDGE, COLS)

    def turned(block):
        gap = jnp.zeros((WIDE - TALL, EDGE), F32)
        return jnp.transpose(jnp.concatenate([block[RADIUS:TALL], gap, block[0:RADIUS]], axis=0))

    near = lax.broadcasted_iota(jnp.int32, (TALL, EDGE), 1) < EDGE // 2
    tile = turned(jnp.where(near, slope[:, first], slope[:, last]))
    halo = turned(slope[:, COLS:WIDE])
    slope_edge[0:wide, :] = jnp.where(top, slope[0:wide, :], slope[TALL - wide : TALL, :])
    slope_edge[16:24, :] = halo[EDGE - RADIUS : EDGE]
    slope_edge[24:32, :] = tile[0:RADIUS]
    slope_edge[32:40, :] = tile[EDGE - RADIUS : EDGE]
    slope_edge[40:48, :] = halo[0:RADIUS]
    tile = jnp.transpose(jnp.where(near[0:ROWS], share[:, first], share[:, last]))
    share_edge[...] = jnp.zeros((48, WIDE), F32)
    share_edge[0:RADIUS, 0:COLS] = jnp.where(top, nothing, share[ROWS - RADIUS : ROWS, :])
    share_edge[RADIUS:wide, 0:COLS] = jnp.where(top, share[0:RADIUS, :], nothing)
    share_edge[24:32, 0:COLS] = tile[0:RADIUS]
    share_edge[32:40, 0:COLS] = tile[EDGE - RADIUS : EDGE]


def back_first_kernel(
    pieces, slope, share, both3, ch, cl, grad_precip, sloped, slope_edge, share_edge, dx
):
    coefficient_strips(slope, share, slope_edge, share_edge)
    wide = 2 * RADIUS
    dx[0:wide, :] = jnp.zeros((wide, COLS), F32)
    dx[wide + ROWS : TALLER, :] = jnp.zeros((wide, COLS), F32)
    for p in range(PIECES):
        for j in range(COLS // EDGE):
            dx[wide + PIECE * p : wide + PIECE * (p + 1), EDGE * j : EDGE * (j + 1)] = pieces[
                p, PIECE * j : PIECE * (j + 1), :
            ]
    for i in range(3):
        at = BLOCK * i
        rh, rl = split(rows_pass(dx[at : at + BLOCK + 2 * RADIUS, :], both3))
        du = jnp.concatenate(
            [
                cols_piece(rh, rl, ch, cl, ((0, 384, 128),), 256),
                cols_piece(rh, rl, ch, cl, ((128, 512, 0),), 256),
                cols_piece(rh, rl, ch, cl, ((384, 512, 0), (0, 128, 256)), 128),
            ],
            axis=1,
        )
        sloped[at : at + BLOCK, :] = slope[at : at + BLOCK, :] * du
        lo, hi = max(at, RADIUS), min(at + BLOCK, RADIUS + ROWS)
        here = slice(lo - RADIUS, hi - RADIUS)
        grad_precip[here, :] = share[here, :] * du[lo - at : hi - at, 0:COLS]


def back_second_kernel(sloped, both4, ch, cl, grad_scaling):
    for i in range(4):
        at = EDGE * i
        r = rows_pass(sloped[at : at + EDGE + 2 * RADIUS, :], both4)
        grad_scaling[at : at + EDGE, :] = cols_pass(r, ch, cl, False)


def around_pass(x):
    taps = taps_of(np.arange(RADIUS + 1).astype(np.float64))
    total = float(taps[0]) * x
    for d in range(1, RADIUS + 1):
        total += float(taps[d]) * (pltpu.roll(x, d, 1) + pltpu.roll(x, WIDE - d, 1))
    return total


def back_halo_kernel(
    lat_in, even, odd, slope_edge, share_edge, precip_part, scaling_part, dh, dl,
    precip_out, scaling_out, strips, square, flat, precip_edge, scaling_edge, middle, sems,
):
    wide = 2 * RADIUS
    lat, parity = my_lat(), my_parity()
    top = lat == 1
    inner = slice(EDGE, COLS - EDGE)
    last = slice(COLS - EDGE, COLS)
    copies = []

    def sent(src, dst):
        copies.append(pltpu.make_async_copy(src, dst, sems.at[len(copies)]))
        copies[-1].start()

    for part, out in ((precip_part, precip_out), (scaling_part, scaling_out)):
        sent(part.at[wide : ROWS - wide, inner], out.at[wide : ROWS - wide, inner])

    right = jnp.where(parity == 0, even[...], odd[...])
    left = jnp.where(parity == 0, odd[...], even[...])
    square[...] = jnp.zeros((EDGE, EDGE), F32)
    square[0:wide, :] = right[:, COLS:WIDE]
    square[EDGE - wide : EDGE, :] = left[:, COLS:WIDE]
    strips[...] = jnp.zeros((48, WIDE), F32)
    strips[0:16, 0:COLS] = lat_in[...]
    strips[0:16, COLS:WIDE] = jnp.transpose(square[...])[0:wide]
    strips[16:32, 0:COLS] = left[:, 0:COLS]
    strips[32:48, 0:COLS] = right[:, 0:COLS]
    band_h, band_l = dh[lat], dl[lat]

    def smoothed(x):
        xh, xl = split(x)
        return around_pass(dot(band_h, xh) + (dot(band_l, xh) + dot(band_h, xl)))

    du = smoothed(strips[...])
    precip_more = share_edge[...] * du
    scaling_more = smoothed(slope_edge[...] * du)
    nothing = jnp.zeros((RADIUS, COLS), F32)
    near = lax.broadcasted_iota(jnp.int32, (ROWS, EDGE), 1) < EDGE // 2

    def finished(k, part, out, edges, reach, low, high, first, final):
        flat[...] = jnp.zeros((EDGE, ROWS), F32)
        flat[0:reach, :] = low
        flat[EDGE - reach : EDGE, :] = high
        turned = jnp.transpose(flat[...])
        middle[2 * k] = part[0:wide, inner] + first[:, inner]
        middle[2 * k + 1] = part[ROWS - wide : ROWS, inner] + final[:, inner]
        sent(middle.at[2 * k], out.at[0:wide, inner])
        sent(middle.at[2 * k + 1], out.at[ROWS - wide : ROWS, inner])
        edges[:, 0:EDGE] = part[:, 0:EDGE] + jnp.where(near, turned, 0.0)
        edges[:, EDGE : 2 * EDGE] = part[:, last] + jnp.where(near, 0.0, turned)
        for q, lanes in enumerate((slice(0, EDGE), last)):
            mine = slice(EDGE * q, EDGE * (q + 1))
            edges[0:wide, mine] += first[:, lanes]
            edges[ROWS - wide : ROWS, mine] += final[:, lanes]
            sent(edges.at[:, mine], out.at[:, lanes])

    finished(
        0, precip_part, precip_out, precip_edge, RADIUS,
        precip_more[24:32, 0:COLS], precip_more[32:40, 0:COLS],
        jnp.concatenate([precip_more[RADIUS:wide, 0:COLS], nothing], axis=0),
        jnp.concatenate([nothing, precip_more[0:RADIUS, 0:COLS]], axis=0),
    )
    added = scaling_more[0:wide, 0:COLS]
    finished(
        1, scaling_part, scaling_out, scaling_edge, wide,
        scaling_more[16:32, 0:COLS], scaling_more[32:48, 0:COLS],
        jnp.where(top, added, 0.0), jnp.where(top, 0.0, added),
    )
    for copy in copies:
        copy.wait()


def in_vmem(*shapes):
    return [pltpu.VMEM(shape, F32) for shape in shapes]


def call(
    kernel, args, outs, scratch=(), scalars=0, flops=0, room=4 << 20, copies=0,
    out_hbm=False,
):
    size = sum(4 * a.size for a in args) + sum(4 * int(np.prod(o)) for o in outs)
    where = pltpu.HBM if out_hbm else pltpu.VMEM
    spaces = [
        pltpu.SMEM if k < scalars else pltpu.VMEM
        for k in range(len(args))
    ]
    sems = [pltpu.SemaphoreType.DMA((copies,))] if copies else []
    return pl.pallas_call(
        kernel,
        out_shape=[pltpu.HBM(o, F32) if out_hbm else jax.ShapeDtypeStruct(o, F32) for o in outs],
        in_specs=[pl.BlockSpec(memory_space=space) for space in spaces],
        out_specs=[pl.BlockSpec(memory_space=where)] * len(outs),
        scratch_shapes=in_vmem(*scratch) + sems,
        cost_estimate=pl.CostEstimate(flops=flops, bytes_accessed=size, transcendentals=0),
        compiler_params=pltpu.CompilerParams(vmem_limit_bytes=room),
    )(*args)


def lat_swapped(strip):
    return lax.ppermute(strip, "lat", [(0, 1), (1, 0)])


def lon_swapped(to_even, to_odd):
    count = lax.axis_size("lon")
    even = [(i, i ^ 1) for i in range(count)]
    odd = [(i, (((i - 1) % count ^ 1) + 1) % count) for i in range(count)]
    return lax.ppermute(to_even, "lon", even), lax.ppermute(to_odd, "lon", odd)


def chip_swapped(part, k):
    if k == 0:
        return part
    pairs = [(i, i ^ k) for i in range(CHIPS)]
    return lax.ppermute(part, ("hour_0", "hour_1"), pairs)


def cores_swapped(parts):
    return lax.ppermute(parts, "hour_2", [(0, 1), (1, 0)])


def per_device(precip, scaling, hour_weight, cotangent):
    rainfall = precip[0]
    incoming = scaling[0]
    upstream = cotangent[0]
    band3, band4, around = row_band(BLOCK), row_band(EDGE), col_band()
    to_lat = lat_strip(incoming, rainfall)
    lat_in = lat_swapped(to_lat)
    even, odd = lon_swapped(
        *call(lon_kernel, (incoming, rainfall, lat_in), ((STRIP, WIDE), (STRIP, WIDE)))
    )
    half = (CHIPS // 2, 2 * EDGE, EDGE)
    whole, part = (PIECES, EDGE, EDGE), (PIECES // 2, EDGE, EDGE)
    slope, share, lifted = call(
        forward_kernel,
        (incoming, rainfall, lat_in, even, odd, band3, *around),
        ((TALL, WIDE), (ROWS, COLS), (TALL, WIDE)),
        scratch=((TALLER, WIDE), (TALL, WIDE), (EDGE, WIDE)),
        flops=2 * 10**9,
        room=14 << 20,
    )

    def logged(flip, *after):
        return call(
            lambda *refs: log_kernel(flip, *refs[: 6], *refs[6 + len(after) :]),
            (hour_weight, lifted, upstream, band4, *around, *after),
            (part, part, half, half),
            scalars=1,
            flops=10**9,
            room=14 << 20,
        )

    second_odd, logs_odd, keep_odd, give_odd = logged(True)
    given_odd = cores_swapped(give_odd)
    second_even, logs_even, keep_even, give_even = logged(False, keep_odd)
    given_even = cores_swapped(give_even)
    arrived = []
    for keep, given, first in ((keep_odd, given_odd, 1), (keep_even, given_even, 0)):
        sums = call(pair_kernel, (keep, given), (half[1:],) * (CHIPS // 2))
        arrived += [chip_swapped(part, 2 * k + first) for k, part in enumerate(sums)]
    (owned,) = call(owner_kernel, tuple(arrived), (half[1:],))

    def collected(first, *after):
        parts = [chip_swapped(owned, 2 * k + first) for k in range(CHIPS // 2)]
        return call(gather_kernel, (*parts, *after), (half,))[0]

    odd_part = collected(1)
    their_odd = cores_swapped(odd_part)
    even_part = collected(0, odd_part)
    their_even = cores_swapped(even_part)
    (pieces,) = call(
        db_kernel,
        (
            hour_weight, even_part, odd_part, their_even, their_odd, upstream, second_even,
            second_odd, logs_even, logs_odd,
        ),
        (whole,),
        scalars=1,
    )
    (to_lat,) = call(back_lat_kernel, (pieces,), ((2 * RADIUS, COLS),))
    lat_in = lat_swapped(to_lat)
    even, odd = lon_swapped(
        *call(back_lon_kernel, (pieces, lat_in), ((2 * RADIUS, WIDE), (2 * RADIUS, WIDE)))
    )
    precip_part, sloped, slope_edge, share_edge = call(
        back_first_kernel,
        (pieces, slope, share, band3, *around),
        ((ROWS, COLS), (TALL, WIDE), (48, WIDE), (48, WIDE)),
        scratch=((TALLER, COLS),),
        flops=2 * 10**9,
        room=14 << 20,
    )
    (scaling_part,) = call(
        back_second_kernel, (sloped, band4, *around), ((ROWS, COLS),),
        flops=2 * 10**9, room=14 << 20,
    )
    grad_precip, grad_scaling = call(
        back_halo_kernel,
        (lat_in, even, odd, slope_edge, share_edge, precip_part, scaling_part, *edge_bands()),
        ((ROWS, COLS), (ROWS, COLS)),
        scratch=(
            (48, WIDE), (EDGE, EDGE), (EDGE, ROWS), (ROWS, 2 * EDGE), (ROWS, 2 * EDGE),
            (4, 2 * RADIUS, 2 * EDGE),
        ),
        flops=10**9,
        room=14 << 20,
        copies=10,
        out_hbm=True,
    )
    return (grad_precip[None], grad_scaling[None])


def solution(mesh):
    split_mesh = Mesh(
        mesh.devices.reshape(4, 2, 2, mesh.shape["lat"], mesh.shape["lon"]),
        ("hour_0", "hour_1", "hour_2", "lat", "lon"),
    )
    return jax.shard_map(
        per_device,
        mesh=split_mesh,
        in_specs=(P(HOUR, "lat", "lon"), P(HOUR, "lat", "lon"), P(HOUR), P(HOUR, "lat", "lon")),
        out_specs=(P(HOUR, "lat", "lon"), P(HOUR, "lat", "lon")),
        check_vma=False,
    )
```

```python
import numpy as np
import jax
import jax.numpy as jnp
from jax import lax
from jax.experimental import pallas as pl
from jax.experimental.pallas import tpu as pltpu
from jax.sharding import Mesh
from jax.sharding import PartitionSpec as P


RADIUS = 8
HOUR = ("hour_0", "hour_1", "hour_2")
PHI = 0.8
SPREAD = 50.0

ROWS = 512
COLS = 512
WIDE = 640
EDGE = 128
TALL = ROWS + 2 * RADIUS
TALLER = ROWS + 4 * RADIUS
BLOCK = TALL // 3
PIECES = 16
CHIPS = 8
PIECE = ROWS // PIECES
STRIP = 3 * RADIUS
F32 = jnp.float32
BF16 = jnp.bfloat16


def taps_of(spacing):
    offsets = np.arange(-RADIUS, RADIUS + 1).astype(np.float64)
    total = np.sum(np.exp(-offsets * offsets / SPREAD))
    return np.where(np.abs(spacing) <= RADIUS, np.exp(-spacing * spacing / SPREAD) / total, 0.0)


def halves(matrix):
    matrix = matrix.astype(np.float32)
    high = matrix.astype(jnp.bfloat16)
    low = (matrix - high.astype(np.float32)).astype(jnp.bfloat16)
    return jnp.asarray(high), jnp.asarray(low)


def row_band(size):
    outer = np.arange(size)[:, None]
    inner = np.arange(size + 2 * RADIUS)[None, :]
    return jnp.concatenate(halves(taps_of((inner - outer - RADIUS).astype(np.float64))), axis=0)


def edge_bands():
    outer = np.arange(2 * RADIUS)[:, None]
    inner = np.arange(2 * RADIUS)[None, :]
    low = taps_of((inner - outer - RADIUS).astype(np.float64))
    high = taps_of((inner - outer + RADIUS).astype(np.float64))
    stacks = np.zeros((2, 48, 48))
    for lat, along in enumerate((high, low)):
        for k, band in enumerate((along, low, high)):
            stacks[lat, 16 * k : 16 * (k + 1), 16 * k : 16 * (k + 1)] = band
    return halves(stacks)


def col_band():
    outer = np.arange(2 * EDGE)[None, :]
    inner = np.arange(4 * EDGE)[:, None]
    return halves(taps_of((inner - EDGE - outer).astype(np.float64)))


def split(x):
    high = x.astype(BF16)
    return high, (x - high.astype(F32)).astype(BF16)


def dot(a, b):
    return jnp.dot(a, b, preferred_element_type=F32)


def rows_pass(x, both):
    xh, xl = split(x)
    rows = both.shape[0] // 2
    twice = dot(both[...], xh)
    return twice[0:rows] + (twice[rows:] + dot(both[0:rows, :], xl))


def cols_piece(rh, rl, ch, cl, spans, count):
    total = None
    for lo, hi, at in spans:
        high, low = ch[at : at + hi - lo, 0:count], cl[at : at + hi - lo, 0:count]
        rows = rh.shape[0]
        twice = dot(jnp.concatenate([rh[:, lo:hi], rl[:, lo:hi]], axis=0), high)
        part = twice[0:rows] + (twice[rows:] + dot(rh[:, lo:hi], low))
        total = part if total is None else total + part
    return total


def cols_pass(r, ch, cl, halo):
    rh, rl = split(r)
    pieces = [
        cols_piece(rh, rl, ch, cl, ((512, 640, 0), (0, 384, 128)), 256),
        cols_piece(rh, rl, ch, cl, ((128, 640, 0),), 256),
    ]
    if halo:
        pieces.append(cols_piece(rh, rl, ch, cl, ((384, 640, 0), (0, 128, 256)), 128))
    return jnp.concatenate(pieces, axis=1)


def valid_part(start, count, lat):
    row = lax.broadcasted_iota(jnp.int32, (count, WIDE), 0) + start
    lane = lax.broadcasted_iota(jnp.int32, (count, WIDE), 1)
    inside = (row >= jnp.where(lat == 0, RADIUS, 0)) & (
        row < jnp.where(lat == 0, TALL, TALL - RADIUS)
    )
    return inside & ((lane < COLS + RADIUS) | (lane >= WIDE - RADIUS))


def my_lat():
    return lax.axis_index("lat")


def my_parity():
    return lax.axis_index("lon") & 1


def fill_edges(ext, reach, rows_in, even, odd, side):
    lat, parity = my_lat(), my_parity()
    side[...] = jnp.zeros((EDGE, WIDE), F32)
    side[0:reach, :] = jnp.where(parity == 0, even, odd)
    side[EDGE - reach : EDGE, :] = jnp.where(parity == 0, odd, even)
    flat = jnp.transpose(side[...])
    corner = flat[ROWS : ROWS + reach]
    ext[reach : reach + ROWS, COLS:WIDE] = flat[0:ROWS]
    ext[0:reach, 0:COLS] = jnp.where(lat == 1, rows_in, 0.0)
    ext[0:reach, COLS:WIDE] = jnp.where(lat == 1, corner, 0.0)
    ext[reach + ROWS : 2 * reach + ROWS, 0:COLS] = jnp.where(lat == 0, rows_in, 0.0)
    ext[reach + ROWS : 2 * reach + ROWS, COLS:WIDE] = jnp.where(lat == 0, corner, 0.0)


def column_strips(reach, first_block, last_block, rows_in, parity):
    spare = jnp.zeros((EDGE - reach, EDGE), F32)
    left = jnp.transpose(jnp.concatenate([first_block, rows_in[:, 0:EDGE], spare], axis=0))
    right = jnp.transpose(
        jnp.concatenate([last_block, rows_in[:, COLS - EDGE : COLS], spare], axis=0)
    )
    left, right = left[0:reach], right[EDGE - reach : EDGE]
    return jnp.where(parity == 0, right, left), jnp.where(parity == 0, left, right)


def lat_kernel(scaling, precip, to_lat, sems):
    wide, narrow = 2 * RADIUS, RADIUS
    keep = 1 - my_lat()
    at = pl.multiple_of(keep * (ROWS - wide), 8)
    near = pl.multiple_of(keep * (ROWS - narrow), 8)
    copies = (
        pltpu.make_async_copy(scaling.at[pl.ds(at, wide), :], to_lat.at[0:wide, :], sems.at[0]),
        pltpu.make_async_copy(
            precip.at[pl.ds(near, narrow), :], to_lat.at[wide:STRIP, :], sems.at[1]
        ),
    )
    for copy in copies:
        copy.start()
    for copy in copies:
        copy.wait()


def in_hbm(x):
    return pltpu.with_memory_space_constraint(x, pltpu.HBM)


def lat_strip(scaling, precip):
    return pl.pallas_call(
        lat_kernel,
        out_shape=jax.ShapeDtypeStruct((STRIP, COLS), F32),
        in_specs=[pl.BlockSpec(memory_space=pltpu.HBM)] * 2,
        out_specs=pl.BlockSpec(memory_space=pltpu.VMEM),
        scratch_shapes=[pltpu.SemaphoreType.DMA((2,))],
        compiler_params=pltpu.CompilerParams(vmem_limit_bytes=2 << 20),
        name="lat_edges",
    )(in_hbm(scaling), in_hbm(precip))


def lon_kernel(scaling, precip, lat_in, to_even, to_odd):
    wide, narrow = 2 * RADIUS, RADIUS
    to_even[0:wide, :], to_odd[0:wide, :] = column_strips(
        wide, scaling[:, 0:EDGE], scaling[:, COLS - EDGE : COLS], lat_in[0:wide, :], my_parity()
    )
    to_even[wide:STRIP, :], to_odd[wide:STRIP, :] = column_strips(
        narrow, precip[:, 0:EDGE], precip[:, COLS - EDGE : COLS], lat_in[wide:STRIP, :], my_parity()
    )


def forward_kernel(
    scaling, precip, lat_in, even, odd, both3, ch, cl, first, lifted, sx, px, side
):
    lat = my_lat()
    wide, narrow = 2 * RADIUS, RADIUS
    sx[wide : wide + ROWS, 0:COLS] = scaling[...]
    px[narrow : narrow + ROWS, 0:COLS] = precip[...]
    fill_edges(sx, wide, lat_in[0:wide, :], even[0:wide, :], odd[0:wide, :], side)
    fill_edges(px, narrow, lat_in[wide:STRIP, :], even[wide:STRIP, :], odd[wide:STRIP, :], side)
    for i in range(3):
        at = BLOCK * i
        r = rows_pass(sx[at : at + BLOCK + 2 * RADIUS, :], both3)
        a = cols_pass(r, ch, cl, True)
        first[at : at + BLOCK, :] = a
        lifted[at : at + BLOCK, :] = jnp.where(
            valid_part(at, BLOCK, lat), jnp.exp(PHI * jnp.log(px[at : at + BLOCK, :] / a)), 0.0
        )


def half_start(flip):
    near = lax.axis_index("hour_1")
    return pl.multiple_of(((1 - near) if flip else near) * (ROWS // 2), ROWS // 2)


def log_kernel(flip, weight, lifted, upstream, both4, ch, cl, second, scaled, keep, give):
    core, far = lax.axis_index("hour_2"), lax.axis_index("hour_0")
    for i in range(2):
        at = half_start(flip) + EDGE * i
        r = rows_pass(lifted[pl.ds(at, EDGE + 2 * RADIUS), :], both4)
        b = cols_pass(r, ch, cl, False)
        logb = jnp.log(b)
        parts = (
            weight[0] * logb, upstream[pl.ds(at, EDGE), :] * jnp.exp(-PHI * logb)
        )
        for j in range(COLS // EDGE):
            lanes = slice(EDGE * j, EDGE * (j + 1))
            four = [slice(PIECE * q, PIECE * (q + 1)) for q in range(4)]
            for q, rows in enumerate(four):
                to = slice(PIECE * j, PIECE * (j + 1))
                second[4 * i + q, to, :] = b[rows, lanes]
                scaled[4 * i + q, to, :] = parts[1][rows, lanes]
            for k, part in enumerate(parts):
                to = slice(EDGE * k + PIECE * j, EDGE * k + PIECE * (j + 1))
                for c in range(2):
                    x, y = part[four[2 * c], lanes], part[four[2 * c + 1], lanes]
                    keep[(2 * i + c) ^ far, to, :] = jnp.where(core == 0, x, y)
                    give[(2 * i + c) ^ far, to, :] = jnp.where(core == 0, y, x)


def pair_kernel(keep, given, *outs):
    for k, out in enumerate(outs):
        out[...] = keep[k] + given[k]


def owner_kernel(*refs):
    sums, out = refs[:CHIPS], refs[CHIPS]

    def total(start):
        x = sums[0][start : start + EDGE, :]
        for part in sums[1:]:
            x = x + part[start : start + EDGE, :]
        return x

    level = jnp.exp(PHI * total(0))
    out[0:EDGE, :] = level
    out[EDGE : 2 * EDGE, :] = PHI * level * total(EDGE)


def gather_kernel(*refs):
    for k in range(CHIPS // 2):
        refs[-1][k] = refs[k][...]


def db_kernel(
    even, odd, their_even, their_odd, rise_even, rise_odd, fall_even, fall_odd, pieces
):
    core, far = lax.axis_index("hour_2"), lax.axis_index("hour_0")
    for flip, mine, theirs, rise, fall in (
        (False, even, their_even, rise_even, fall_even),
        (True, odd, their_odd, rise_odd, fall_odd),
    ):
        first = half_start(flip) // PIECE
        for n in range(PIECES // 2):
            here, slot = core == n % 2, (n // 2) ^ far
            level = jnp.where(here, mine[slot, 0:EDGE, :], theirs[slot, 0:EDGE, :])
            dlogq = jnp.where(
                here, mine[slot, EDGE : 2 * EDGE, :], theirs[slot, EDGE : 2 * EDGE, :]
            )
            pieces[first + n] = rise[n] * dlogq - fall[n] * level


def tile_column(pieces, j):
    return jnp.concatenate(
        [pieces[p, PIECE * j : PIECE * (j + 1), :] for p in range(PIECES)], axis=0
    )


def back_lat_kernel(pieces, to_lat):
    wide = 2 * RADIUS
    for j in range(COLS // EDGE):
        to_lat[:, EDGE * j : EDGE * (j + 1)] = jnp.where(
            my_lat() == 0,
            pieces[PIECES - 1, PIECE * (j + 1) - wide : PIECE * (j + 1), :],
            pieces[0, PIECE * j : PIECE * j + wide, :],
        )


def back_lon_kernel(pieces, lat_in, to_even, to_odd):
    to_even[...], to_odd[...] = column_strips(
        2 * RADIUS, tile_column(pieces, 0), tile_column(pieces, COLS // EDGE - 1), lat_in[...],
        my_parity(),
    )


def coefficient_strips(slope, share, slope_edge, share_edge):
    wide = 2 * RADIUS
    top = my_lat() == 1
    nothing = jnp.zeros((RADIUS, COLS), F32)
    first, last = slice(0, EDGE), slice(COLS - EDGE, COLS)

    def turned(block):
        gap = jnp.zeros((WIDE - TALL, EDGE), F32)
        return jnp.transpose(jnp.concatenate([block[RADIUS:TALL], gap, block[0:RADIUS]], axis=0))

    near = lax.broadcasted_iota(jnp.int32, (TALL, EDGE), 1) < EDGE // 2
    tile = turned(jnp.where(near, slope[:, first], slope[:, last]))
    halo = turned(slope[:, COLS:WIDE])
    slope_edge[0:wide, :] = jnp.where(top, slope[0:wide, :], slope[TALL - wide : TALL, :])
    slope_edge[16:24, :] = halo[EDGE - RADIUS : EDGE]
    slope_edge[24:32, :] = tile[0:RADIUS]
    slope_edge[32:40, :] = tile[EDGE - RADIUS : EDGE]
    slope_edge[40:48, :] = halo[0:RADIUS]
    tile = jnp.transpose(jnp.where(near[0:ROWS], share[:, first], share[:, last]))
    share_edge[...] = jnp.zeros((48, WIDE), F32)
    share_edge[0:RADIUS, 0:COLS] = jnp.where(top, nothing, share[ROWS - RADIUS : ROWS, :])
    share_edge[RADIUS:wide, 0:COLS] = jnp.where(top, share[0:RADIUS, :], nothing)
    share_edge[24:32, 0:COLS] = tile[0:RADIUS]
    share_edge[32:40, 0:COLS] = tile[EDGE - RADIUS : EDGE]


def prepare_kernel(
    weight, first, lifted, precip, second_even, second_odd, scaled_even, scaled_odd,
    slope, share, slope_edge, share_edge, rise_even, rise_odd, fall_even, fall_odd,
):
    lat = my_lat()
    for i in range(3):
        rows = slice(BLOCK * i, BLOCK * (i + 1))
        slope[rows, :] = jnp.where(
            valid_part(BLOCK * i, BLOCK, lat), -PHI * lifted[rows, :] / first[rows, :], 0.0
        )
    share[...] = PHI * lifted[RADIUS : RADIUS + ROWS, 0:COLS] / precip[...]
    coefficient_strips(slope, share, slope_edge, share_edge)
    for second, scaled, rise, fall in (
        (second_even, scaled_even, rise_even, fall_even),
        (second_odd, scaled_odd, rise_odd, fall_odd),
    ):
        inverse = 1.0 / second[...]
        rise[...] = weight[0] * inverse
        fall[...] = PHI * scaled[...] * inverse


def back_first_kernel(
    pieces, slope, share, both3, ch, cl, grad_precip, sloped, dx
):
    wide = 2 * RADIUS
    dx[0:wide, :] = jnp.zeros((wide, COLS), F32)
    dx[wide + ROWS : TALLER, :] = jnp.zeros((wide, COLS), F32)
    for p in range(PIECES):
        for j in range(COLS // EDGE):
            dx[wide + PIECE * p : wide + PIECE * (p + 1), EDGE * j : EDGE * (j + 1)] = pieces[
                p, PIECE * j : PIECE * (j + 1), :
            ]
    for i in range(3):
        at = BLOCK * i
        rh, rl = split(rows_pass(dx[at : at + BLOCK + 2 * RADIUS, :], both3))
        du = jnp.concatenate(
            [
                cols_piece(rh, rl, ch, cl, ((0, 384, 128),), 256),
                cols_piece(rh, rl, ch, cl, ((128, 512, 0),), 256),
                cols_piece(rh, rl, ch, cl, ((384, 512, 0), (0, 128, 256)), 128),
            ],
            axis=1,
        )
        sloped[at : at + BLOCK, :] = slope[at : at + BLOCK, :] * du
        lo, hi = max(at, RADIUS), min(at + BLOCK, RADIUS + ROWS)
        here = slice(lo - RADIUS, hi - RADIUS)
        grad_precip[here, :] = share[here, :] * du[lo - at : hi - at, 0:COLS]


def back_second_kernel(sloped, both4, ch, cl, grad_scaling):
    for i in range(4):
        at = EDGE * i
        r = rows_pass(sloped[at : at + EDGE + 2 * RADIUS, :], both4)
        grad_scaling[at : at + EDGE, :] = cols_pass(r, ch, cl, False)


def around_pass(x):
    taps = taps_of(np.arange(RADIUS + 1).astype(np.float64))
    total = float(taps[0]) * x
    for d in range(1, RADIUS + 1):
        total += float(taps[d]) * (pltpu.roll(x, d, 1) + pltpu.roll(x, WIDE - d, 1))
    return total


def back_halo_kernel(
    lat_in, even, odd, slope_edge, share_edge, precip_part, scaling_part, dh, dl,
    precip_out, scaling_out, strips, square, flat, precip_edge, scaling_edge, middle, sems,
):
    wide = 2 * RADIUS
    lat, parity = my_lat(), my_parity()
    top = lat == 1
    inner = slice(EDGE, COLS - EDGE)
    last = slice(COLS - EDGE, COLS)
    copies = []

    def sent(src, dst):
        copies.append(pltpu.make_async_copy(src, dst, sems.at[len(copies)]))
        copies[-1].start()

    for part, out in ((precip_part, precip_out), (scaling_part, scaling_out)):
        sent(part.at[wide : ROWS - wide, inner], out.at[wide : ROWS - wide, inner])

    right = jnp.where(parity == 0, even[...], odd[...])
    left = jnp.where(parity == 0, odd[...], even[...])
    square[...] = jnp.zeros((EDGE, EDGE), F32)
    square[0:wide, :] = right[:, COLS:WIDE]
    square[EDGE - wide : EDGE, :] = left[:, COLS:WIDE]
    strips[...] = jnp.zeros((48, WIDE), F32)
    strips[0:16, 0:COLS] = lat_in[...]
    strips[0:16, COLS:WIDE] = jnp.transpose(square[...])[0:wide]
    strips[16:32, 0:COLS] = left[:, 0:COLS]
    strips[32:48, 0:COLS] = right[:, 0:COLS]
    band_h, band_l = dh[lat], dl[lat]

    def smoothed(x):
        xh, xl = split(x)
        return around_pass(dot(band_h, xh) + (dot(band_l, xh) + dot(band_h, xl)))

    du = smoothed(strips[...])
    precip_more = share_edge[...] * du
    scaling_more = smoothed(slope_edge[...] * du)
    nothing = jnp.zeros((RADIUS, COLS), F32)
    near = lax.broadcasted_iota(jnp.int32, (ROWS, EDGE), 1) < EDGE // 2

    def finished(k, part, out, edges, reach, low, high, first, final):
        flat[...] = jnp.zeros((EDGE, ROWS), F32)
        flat[0:reach, :] = low
        flat[EDGE - reach : EDGE, :] = high
        turned = jnp.transpose(flat[...])
        middle[2 * k] = part[0:wide, inner] + first[:, inner]
        middle[2 * k + 1] = part[ROWS - wide : ROWS, inner] + final[:, inner]
        sent(middle.at[2 * k], out.at[0:wide, inner])
        sent(middle.at[2 * k + 1], out.at[ROWS - wide : ROWS, inner])
        edges[:, 0:EDGE] = part[:, 0:EDGE] + jnp.where(near, turned, 0.0)
        edges[:, EDGE : 2 * EDGE] = part[:, last] + jnp.where(near, 0.0, turned)
        for q, lanes in enumerate((slice(0, EDGE), last)):
            mine = slice(EDGE * q, EDGE * (q + 1))
            edges[0:wide, mine] += first[:, lanes]
            edges[ROWS - wide : ROWS, mine] += final[:, lanes]
            sent(edges.at[:, mine], out.at[:, lanes])

    finished(
        0, precip_part, precip_out, precip_edge, RADIUS,
        precip_more[24:32, 0:COLS], precip_more[32:40, 0:COLS],
        jnp.concatenate([precip_more[RADIUS:wide, 0:COLS], nothing], axis=0),
        jnp.concatenate([nothing, precip_more[0:RADIUS, 0:COLS]], axis=0),
    )
    added = scaling_more[0:wide, 0:COLS]
    finished(
        1, scaling_part, scaling_out, scaling_edge, wide,
        scaling_more[16:32, 0:COLS], scaling_more[32:48, 0:COLS],
        jnp.where(top, added, 0.0), jnp.where(top, 0.0, added),
    )
    for copy in copies:
        copy.wait()


def in_vmem(*shapes):
    return [pltpu.VMEM(shape, F32) for shape in shapes]


def call(
    kernel, args, outs, scratch=(), scalars=0, flops=0, room=4 << 20, copies=0,
    out_hbm=False,
):
    size = sum(4 * a.size for a in args) + sum(4 * int(np.prod(o)) for o in outs)
    where = pltpu.HBM if out_hbm else pltpu.VMEM
    spaces = [
        pltpu.SMEM if k < scalars else pltpu.VMEM
        for k in range(len(args))
    ]
    sems = [pltpu.SemaphoreType.DMA((copies,))] if copies else []
    return pl.pallas_call(
        kernel,
        out_shape=[pltpu.HBM(o, F32) if out_hbm else jax.ShapeDtypeStruct(o, F32) for o in outs],
        in_specs=[pl.BlockSpec(memory_space=space) for space in spaces],
        out_specs=[pl.BlockSpec(memory_space=where)] * len(outs),
        scratch_shapes=in_vmem(*scratch) + sems,
        cost_estimate=pl.CostEstimate(flops=flops, bytes_accessed=size, transcendentals=0),
        compiler_params=pltpu.CompilerParams(vmem_limit_bytes=room),
    )(*args)


def lat_swapped(strip):
    return lax.ppermute(strip, "lat", [(0, 1), (1, 0)])


def lon_swapped(to_even, to_odd):
    count = lax.axis_size("lon")
    even = [(i, i ^ 1) for i in range(count)]
    odd = [(i, (((i - 1) % count ^ 1) + 1) % count) for i in range(count)]
    return lax.ppermute(to_even, "lon", even), lax.ppermute(to_odd, "lon", odd)


def chip_swapped(part, k):
    if k == 0:
        return part
    pairs = [(i, i ^ k) for i in range(CHIPS)]
    return lax.ppermute(part, ("hour_0", "hour_1"), pairs)


def cores_swapped(parts):
    return lax.ppermute(parts, "hour_2", [(0, 1), (1, 0)])


def per_device(precip, scaling, hour_weight, cotangent):
    rainfall = precip[0]
    incoming = scaling[0]
    upstream = cotangent[0]
    band3, band4, around = row_band(BLOCK), row_band(EDGE), col_band()
    to_lat = lat_strip(incoming, rainfall)
    lat_in = lat_swapped(to_lat)
    even, odd = lon_swapped(
        *call(lon_kernel, (incoming, rainfall, lat_in), ((STRIP, WIDE), (STRIP, WIDE)))
    )
    half = (CHIPS // 2, 2 * EDGE, EDGE)
    whole, part = (PIECES, EDGE, EDGE), (PIECES // 2, EDGE, EDGE)
    smooth, lifted = call(
        forward_kernel,
        (incoming, rainfall, lat_in, even, odd, band3, *around),
        ((TALL, WIDE), (TALL, WIDE)),
        scratch=((TALLER, WIDE), (TALL, WIDE), (EDGE, WIDE)),
        flops=2 * 10**9,
        room=14 << 20,
    )

    def logged(flip, *after):
        return call(
            lambda *refs: log_kernel(flip, *refs[: 6], *refs[6 + len(after) :]),
            (hour_weight, lifted, upstream, band4, *around, *after),
            (part, part, half, half),
            scalars=1,
            flops=10**9,
            room=14 << 20,
        )

    second_odd, scaled_odd, keep_odd, give_odd = logged(True)
    given_odd = cores_swapped(give_odd)
    second_even, scaled_even, keep_even, give_even = logged(False, keep_odd)
    given_even = cores_swapped(give_even)
    arrived = []
    for keep, given, first in ((keep_odd, given_odd, 1), (keep_even, given_even, 0)):
        sums = call(pair_kernel, (keep, given), (half[1:],) * (CHIPS // 2))
        arrived += [chip_swapped(part, 2 * k + first) for k, part in enumerate(sums)]
    slope, share, slope_edge, share_edge, *factors = call(
        prepare_kernel,
        (
            hour_weight, smooth, lifted, rainfall, second_even, second_odd, scaled_even,
            scaled_odd,
        ),
        ((TALL, WIDE), (ROWS, COLS), (48, WIDE), (48, WIDE), part, part, part, part),
        scalars=1,
        room=14 << 20,
    )
    (owned,) = call(owner_kernel, tuple(arrived), (half[1:],))

    def collected(first, *after):
        parts = [chip_swapped(owned, 2 * k + first) for k in range(CHIPS // 2)]
        return call(gather_kernel, (*parts, *after), (half,))[0]

    odd_part = collected(1)
    their_odd = cores_swapped(odd_part)
    even_part = collected(0, odd_part)
    their_even = cores_swapped(even_part)
    (pieces,) = call(db_kernel, (even_part, odd_part, their_even, their_odd, *factors), (whole,))
    (to_lat,) = call(back_lat_kernel, (pieces,), ((2 * RADIUS, COLS),))
    lat_in = lat_swapped(to_lat)
    even, odd = lon_swapped(
        *call(back_lon_kernel, (pieces, lat_in), ((2 * RADIUS, WIDE), (2 * RADIUS, WIDE)))
    )
    precip_part, sloped = call(
        back_first_kernel,
        (pieces, slope, share, band3, *around),
        ((ROWS, COLS), (TALL, WIDE)),
        scratch=((TALLER, COLS),),
        flops=2 * 10**9,
        room=14 << 20,
    )
    (scaling_part,) = call(
        back_second_kernel, (sloped, band4, *around), ((ROWS, COLS),),
        flops=2 * 10**9, room=14 << 20,
    )
    grad_precip, grad_scaling = call(
        back_halo_kernel,
        (lat_in, even, odd, slope_edge, share_edge, precip_part, scaling_part, *edge_bands()),
        ((ROWS, COLS), (ROWS, COLS)),
        scratch=(
            (48, WIDE), (EDGE, EDGE), (EDGE, ROWS), (ROWS, 2 * EDGE), (ROWS, 2 * EDGE),
            (4, 2 * RADIUS, 2 * EDGE),
        ),
        flops=10**9,
        room=14 << 20,
        copies=10,
        out_hbm=True,
    )
    return (grad_precip[None], grad_scaling[None])


def solution(mesh):
    split_mesh = Mesh(
        mesh.devices.reshape(4, 2, 2, mesh.shape["lat"], mesh.shape["lon"]),
        ("hour_0", "hour_1", "hour_2", "lat", "lon"),
    )
    return jax.shard_map(
        per_device,
        mesh=split_mesh,
        in_specs=(P(HOUR, "lat", "lon"), P(HOUR, "lat", "lon"), P(HOUR), P(HOUR, "lat", "lon")),
        out_specs=(P(HOUR, "lat", "lon"), P(HOUR, "lat", "lon")),
        check_vma=False,
    )
```

```python
import numpy as np
import jax
import jax.numpy as jnp
from jax import lax
from jax.experimental import pallas as pl
from jax.experimental.pallas import tpu as pltpu
from jax.sharding import Mesh
from jax.sharding import PartitionSpec as P


RADIUS = 8
HOUR = ("hour_0", "hour_1", "hour_2")
PHI = 0.8
SPREAD = 50.0

ROWS = 512
COLS = 512
WIDE = 640
EDGE = 128
TALL = ROWS + 2 * RADIUS
TALLER = ROWS + 4 * RADIUS
BLOCK = TALL // 3
PIECES = 16
CHIPS = 8
PIECE = ROWS // PIECES
STRIP = 3 * RADIUS
F32 = jnp.float32
BF16 = jnp.bfloat16


def taps_of(spacing):
    offsets = np.arange(-RADIUS, RADIUS + 1).astype(np.float64)
    total = np.sum(np.exp(-offsets * offsets / SPREAD))
    return np.where(np.abs(spacing) <= RADIUS, np.exp(-spacing * spacing / SPREAD) / total, 0.0)


def halves(matrix):
    matrix = matrix.astype(np.float32)
    high = matrix.astype(jnp.bfloat16)
    low = (matrix - high.astype(np.float32)).astype(jnp.bfloat16)
    return jnp.asarray(high), jnp.asarray(low)


def row_band(size):
    outer = np.arange(size)[:, None]
    inner = np.arange(size + 2 * RADIUS)[None, :]
    return jnp.concatenate(halves(taps_of((inner - outer - RADIUS).astype(np.float64))), axis=0)


def edge_bands():
    outer = np.arange(2 * RADIUS)[:, None]
    inner = np.arange(2 * RADIUS)[None, :]
    low = taps_of((inner - outer - RADIUS).astype(np.float64))
    high = taps_of((inner - outer + RADIUS).astype(np.float64))
    stacks = np.zeros((2, 48, 48))
    for lat, along in enumerate((high, low)):
        for k, band in enumerate((along, low, high)):
            stacks[lat, 16 * k : 16 * (k + 1), 16 * k : 16 * (k + 1)] = band
    return halves(stacks)


def col_band():
    outer = np.arange(2 * EDGE)[None, :]
    inner = np.arange(4 * EDGE)[:, None]
    return halves(taps_of((inner - EDGE - outer).astype(np.float64)))


def split(x):
    high = x.astype(BF16)
    return high, (x - high.astype(F32)).astype(BF16)


def dot(a, b):
    return jnp.dot(a, b, preferred_element_type=F32)


def rows_pass(x, both):
    xh, xl = split(x)
    rows = both.shape[0] // 2
    twice = dot(both[...], xh)
    return twice[0:rows] + (twice[rows:] + dot(both[0:rows, :], xl))


def cols_piece(rh, rl, ch, cl, spans, count):
    total = None
    for lo, hi, at in spans:
        high, low = ch[at : at + hi - lo, 0:count], cl[at : at + hi - lo, 0:count]
        rows = rh.shape[0]
        twice = dot(jnp.concatenate([rh[:, lo:hi], rl[:, lo:hi]], axis=0), high)
        part = twice[0:rows] + (twice[rows:] + dot(rh[:, lo:hi], low))
        total = part if total is None else total + part
    return total


def cols_pass(r, ch, cl, halo):
    rh, rl = split(r)
    pieces = [
        cols_piece(rh, rl, ch, cl, ((512, 640, 0), (0, 384, 128)), 256),
        cols_piece(rh, rl, ch, cl, ((128, 640, 0),), 256),
    ]
    if halo:
        pieces.append(cols_piece(rh, rl, ch, cl, ((384, 640, 0), (0, 128, 256)), 128))
    return jnp.concatenate(pieces, axis=1)


def valid_part(start, count, lat):
    row = lax.broadcasted_iota(jnp.int32, (count, WIDE), 0) + start
    lane = lax.broadcasted_iota(jnp.int32, (count, WIDE), 1)
    inside = (row >= jnp.where(lat == 0, RADIUS, 0)) & (
        row < jnp.where(lat == 0, TALL, TALL - RADIUS)
    )
    return inside & ((lane < COLS + RADIUS) | (lane >= WIDE - RADIUS))


def my_lat():
    return lax.axis_index("lat")


def my_parity():
    return lax.axis_index("lon") & 1


def fill_edges(ext, reach, rows_in, even, odd, side):
    lat, parity = my_lat(), my_parity()
    side[...] = jnp.zeros((EDGE, WIDE), F32)
    side[0:reach, :] = jnp.where(parity == 0, even, odd)
    side[EDGE - reach : EDGE, :] = jnp.where(parity == 0, odd, even)
    flat = jnp.transpose(side[...])
    corner = flat[ROWS : ROWS + reach]
    ext[reach : reach + ROWS, COLS:WIDE] = flat[0:ROWS]
    ext[0:reach, 0:COLS] = jnp.where(lat == 1, rows_in, 0.0)
    ext[0:reach, COLS:WIDE] = jnp.where(lat == 1, corner, 0.0)
    ext[reach + ROWS : 2 * reach + ROWS, 0:COLS] = jnp.where(lat == 0, rows_in, 0.0)
    ext[reach + ROWS : 2 * reach + ROWS, COLS:WIDE] = jnp.where(lat == 0, corner, 0.0)


def column_strips(reach, first_block, last_block, rows_in, parity):
    spare = jnp.zeros((EDGE - reach, EDGE), F32)
    left = jnp.transpose(jnp.concatenate([first_block, rows_in[:, 0:EDGE], spare], axis=0))
    right = jnp.transpose(
        jnp.concatenate([last_block, rows_in[:, COLS - EDGE : COLS], spare], axis=0)
    )
    left, right = left[0:reach], right[EDGE - reach : EDGE]
    return jnp.where(parity == 0, right, left), jnp.where(parity == 0, left, right)


def lat_kernel(scaling, precip, to_lat, sems):
    wide, narrow = 2 * RADIUS, RADIUS
    keep = 1 - my_lat()
    at = pl.multiple_of(keep * (ROWS - wide), 8)
    near = pl.multiple_of(keep * (ROWS - narrow), 8)
    copies = (
        pltpu.make_async_copy(scaling.at[pl.ds(at, wide), :], to_lat.at[0:wide, :], sems.at[0]),
        pltpu.make_async_copy(
            precip.at[pl.ds(near, narrow), :], to_lat.at[wide:STRIP, :], sems.at[1]
        ),
    )
    for copy in copies:
        copy.start()
    for copy in copies:
        copy.wait()


def in_hbm(x):
    return pltpu.with_memory_space_constraint(x, pltpu.HBM)


def lat_strip(scaling, precip):
    return pl.pallas_call(
        lat_kernel,
        out_shape=jax.ShapeDtypeStruct((STRIP, COLS), F32),
        in_specs=[pl.BlockSpec(memory_space=pltpu.HBM)] * 2,
        out_specs=pl.BlockSpec(memory_space=pltpu.VMEM),
        scratch_shapes=[pltpu.SemaphoreType.DMA((2,))],
        compiler_params=pltpu.CompilerParams(vmem_limit_bytes=2 << 20),
        name="lat_edges",
    )(in_hbm(scaling), in_hbm(precip))


def lon_kernel(scaling, precip, lat_in, to_even, to_odd):
    wide, narrow = 2 * RADIUS, RADIUS
    to_even[0:wide, :], to_odd[0:wide, :] = column_strips(
        wide, scaling[:, 0:EDGE], scaling[:, COLS - EDGE : COLS], lat_in[0:wide, :], my_parity()
    )
    to_even[wide:STRIP, :], to_odd[wide:STRIP, :] = column_strips(
        narrow, precip[:, 0:EDGE], precip[:, COLS - EDGE : COLS], lat_in[wide:STRIP, :], my_parity()
    )


def around_pass(x):
    taps = taps_of(np.arange(RADIUS + 1).astype(np.float64))
    total = float(taps[0]) * x
    for d in range(1, RADIUS + 1):
        total += float(taps[d]) * (pltpu.roll(x, d, 1) + pltpu.roll(x, WIDE - d, 1))
    return total


def smoothed(x, bands):
    xh, xl = split(x)
    return around_pass(dot(bands[0], xh) + (dot(bands[1], xh) + dot(bands[0], xl)))


def fill_strips(strips, square, lat_in, even, odd):
    wide, parity = 2 * RADIUS, my_parity()
    right = jnp.where(parity == 0, even, odd)
    left = jnp.where(parity == 0, odd, even)
    square[...] = jnp.zeros((EDGE, EDGE), F32)
    square[0:wide, :] = right[:, COLS:WIDE]
    square[EDGE - wide : EDGE, :] = left[:, COLS:WIDE]
    strips[...] = jnp.zeros((48, WIDE), F32)
    strips[0:16, 0:COLS] = lat_in
    strips[0:16, COLS:WIDE] = jnp.transpose(square[...])[0:wide]
    strips[16:32, 0:COLS] = left[:, 0:COLS]
    strips[32:48, 0:COLS] = right[:, 0:COLS]


def tile_pass(x, both3, ch, cl):
    rh, rl = split(rows_pass(x, both3))
    return jnp.concatenate(
        [
            cols_piece(rh, rl, ch, cl, ((0, 384, 128),), 256),
            cols_piece(rh, rl, ch, cl, ((128, 512, 0),), 256),
            cols_piece(rh, rl, ch, cl, ((384, 512, 0), (0, 128, 256)), 128),
        ],
        axis=1,
    )


def front_kernel(scaling, both3, ch, cl, partial, sx):
    wide = 2 * RADIUS
    sx[0:wide, :] = jnp.zeros((wide, COLS), F32)
    sx[wide + ROWS : TALLER, :] = jnp.zeros((wide, COLS), F32)
    sx[wide : wide + ROWS, :] = scaling[...]
    for i in range(3):
        at = BLOCK * i
        partial[at : at + BLOCK, :] = tile_pass(sx[at : at + BLOCK + wide, :], both3, ch, cl)


def forward_kernel(
    partial, precip, lat_in, even, odd, dh, dl, first, lifted, px, side, strips, square,
    tile_more, halo_more,
):
    lat = my_lat()
    top = lat == 1
    wide, narrow = 2 * RADIUS, RADIUS
    px[narrow : narrow + ROWS, 0:COLS] = precip[...]
    fill_edges(px, narrow, lat_in[wide:STRIP, :], even[wide:STRIP, :], odd[wide:STRIP, :], side)
    fill_strips(strips, square, lat_in[0:wide, :], even[0:wide, :], odd[0:wide, :])
    more = smoothed(strips[...], (dh[lat], dl[lat]))
    for target, low, high in ((tile_more, 24, 32), (halo_more, 40, 16)):
        side[...] = jnp.zeros((EDGE, WIDE), F32)
        side[0:narrow, :] = more[low : low + narrow]
        side[EDGE - narrow : EDGE, :] = more[high : high + narrow]
        turned = jnp.transpose(side[...])
        target[narrow:TALL, :] = turned[0 : TALL - narrow]
        target[0:narrow, :] = turned[WIDE - narrow : WIDE]
    close = lax.broadcasted_iota(jnp.int32, (BLOCK, EDGE), 1) < EDGE // 2
    for i in range(3):
        rows = slice(BLOCK * i, BLOCK * (i + 1))
        extra = tile_more[rows, :]
        a = jnp.concatenate(
            [
                partial[rows, 0:EDGE] + jnp.where(close, extra, 0.0),
                partial[rows, EDGE : COLS - EDGE],
                partial[rows, COLS - EDGE : COLS] + jnp.where(close, 0.0, extra),
                partial[rows, COLS:WIDE] + halo_more[rows, :],
            ],
            axis=1,
        )
        if i == 0:
            a = jnp.concatenate([a[0:wide] + jnp.where(top, more[0:wide], 0.0), a[wide:]], axis=0)
        if i == 2:
            end = BLOCK - wide
            a = jnp.concatenate([a[0:end], a[end:] + jnp.where(top, 0.0, more[0:wide])], axis=0)
        first[rows, :] = a
        lifted[rows, :] = jnp.where(
            valid_part(BLOCK * i, BLOCK, lat), jnp.exp(PHI * jnp.log(px[rows, :] / a)), 0.0
        )


def half_start(flip):
    near = lax.axis_index("hour_1")
    return pl.multiple_of(((1 - near) if flip else near) * (ROWS // 2), ROWS // 2)


def log_kernel(flip, weight, lifted, upstream, both4, ch, cl, second, scaled, keep, give):
    core, far = lax.axis_index("hour_2"), lax.axis_index("hour_0")
    for i in range(2):
        at = half_start(flip) + EDGE * i
        r = rows_pass(lifted[pl.ds(at, EDGE + 2 * RADIUS), :], both4)
        b = cols_pass(r, ch, cl, False)
        logb = jnp.log(b)
        parts = (
            weight[0] * logb, upstream[pl.ds(at, EDGE), :] * jnp.exp(-PHI * logb)
        )
        for j in range(COLS // EDGE):
            lanes = slice(EDGE * j, EDGE * (j + 1))
            four = [slice(PIECE * q, PIECE * (q + 1)) for q in range(4)]
            for q, rows in enumerate(four):
                to = slice(PIECE * j, PIECE * (j + 1))
                second[4 * i + q, to, :] = b[rows, lanes]
                scaled[4 * i + q, to, :] = parts[1][rows, lanes]
            for k, part in enumerate(parts):
                to = slice(EDGE * k + PIECE * j, EDGE * k + PIECE * (j + 1))
                for c in range(2):
                    x, y = part[four[2 * c], lanes], part[four[2 * c + 1], lanes]
                    keep[(2 * i + c) ^ far, to, :] = jnp.where(core == 0, x, y)
                    give[(2 * i + c) ^ far, to, :] = jnp.where(core == 0, y, x)


def pair_kernel(keep, given, *outs):
    for k, out in enumerate(outs):
        out[...] = keep[k] + given[k]


def owner_kernel(*refs):
    sums, out = refs[:CHIPS], refs[CHIPS]

    def total(start):
        x = sums[0][start : start + EDGE, :]
        for part in sums[1:]:
            x = x + part[start : start + EDGE, :]
        return x

    level = jnp.exp(PHI * total(0))
    out[0:EDGE, :] = level
    out[EDGE : 2 * EDGE, :] = PHI * level * total(EDGE)


def gather_kernel(*refs):
    for k in range(CHIPS // 2):
        refs[-1][k] = refs[k][...]


def db_kernel(
    even, odd, their_even, their_odd, rise_even, rise_odd, fall_even, fall_odd, pieces
):
    core, far = lax.axis_index("hour_2"), lax.axis_index("hour_0")
    for flip, mine, theirs, rise, fall in (
        (False, even, their_even, rise_even, fall_even),
        (True, odd, their_odd, rise_odd, fall_odd),
    ):
        first = half_start(flip) // PIECE
        for n in range(PIECES // 2):
            here, slot = core == n % 2, (n // 2) ^ far
            level = jnp.where(here, mine[slot, 0:EDGE, :], theirs[slot, 0:EDGE, :])
            dlogq = jnp.where(
                here, mine[slot, EDGE : 2 * EDGE, :], theirs[slot, EDGE : 2 * EDGE, :]
            )
            pieces[first + n] = rise[n] * dlogq - fall[n] * level


def tile_column(pieces, j):
    return jnp.concatenate(
        [pieces[p, PIECE * j : PIECE * (j + 1), :] for p in range(PIECES)], axis=0
    )


def back_lat_kernel(pieces, to_lat):
    wide = 2 * RADIUS
    for j in range(COLS // EDGE):
        to_lat[:, EDGE * j : EDGE * (j + 1)] = jnp.where(
            my_lat() == 0,
            pieces[PIECES - 1, PIECE * (j + 1) - wide : PIECE * (j + 1), :],
            pieces[0, PIECE * j : PIECE * j + wide, :],
        )


def back_lon_kernel(pieces, lat_in, to_even, to_odd):
    to_even[...], to_odd[...] = column_strips(
        2 * RADIUS, tile_column(pieces, 0), tile_column(pieces, COLS // EDGE - 1), lat_in[...],
        my_parity(),
    )


def coefficient_strips(slope, share, slope_edge, share_edge):
    wide = 2 * RADIUS
    top = my_lat() == 1
    nothing = jnp.zeros((RADIUS, COLS), F32)
    first, last = slice(0, EDGE), slice(COLS - EDGE, COLS)

    def turned(block):
        gap = jnp.zeros((WIDE - TALL, EDGE), F32)
        return jnp.transpose(jnp.concatenate([block[RADIUS:TALL], gap, block[0:RADIUS]], axis=0))

    near = lax.broadcasted_iota(jnp.int32, (TALL, EDGE), 1) < EDGE // 2
    tile = turned(jnp.where(near, slope[:, first], slope[:, last]))
    halo = turned(slope[:, COLS:WIDE])
    slope_edge[0:wide, :] = jnp.where(top, slope[0:wide, :], slope[TALL - wide : TALL, :])
    slope_edge[16:24, :] = halo[EDGE - RADIUS : EDGE]
    slope_edge[24:32, :] = tile[0:RADIUS]
    slope_edge[32:40, :] = tile[EDGE - RADIUS : EDGE]
    slope_edge[40:48, :] = halo[0:RADIUS]
    tile = jnp.transpose(jnp.where(near[0:ROWS], share[:, first], share[:, last]))
    share_edge[...] = jnp.zeros((48, WIDE), F32)
    share_edge[0:RADIUS, 0:COLS] = jnp.where(top, nothing, share[ROWS - RADIUS : ROWS, :])
    share_edge[RADIUS:wide, 0:COLS] = jnp.where(top, share[0:RADIUS, :], nothing)
    share_edge[24:32, 0:COLS] = tile[0:RADIUS]
    share_edge[32:40, 0:COLS] = tile[EDGE - RADIUS : EDGE]


def prepare_kernel(
    weight, first, lifted, precip, second_even, second_odd, scaled_even, scaled_odd,
    slope, share, slope_edge, share_edge, rise_even, rise_odd, fall_even, fall_odd,
):
    lat = my_lat()
    for i in range(3):
        rows = slice(BLOCK * i, BLOCK * (i + 1))
        slope[rows, :] = jnp.where(
            valid_part(BLOCK * i, BLOCK, lat), -PHI * lifted[rows, :] / first[rows, :], 0.0
        )
    share[...] = PHI * lifted[RADIUS : RADIUS + ROWS, 0:COLS] / precip[...]
    coefficient_strips(slope, share, slope_edge, share_edge)
    for second, scaled, rise, fall in (
        (second_even, scaled_even, rise_even, fall_even),
        (second_odd, scaled_odd, rise_odd, fall_odd),
    ):
        inverse = 1.0 / second[...]
        rise[...] = weight[0] * inverse
        fall[...] = PHI * scaled[...] * inverse


def back_first_kernel(
    pieces, slope, share, both3, ch, cl, grad_precip, sloped, dx
):
    wide = 2 * RADIUS
    dx[0:wide, :] = jnp.zeros((wide, COLS), F32)
    dx[wide + ROWS : TALLER, :] = jnp.zeros((wide, COLS), F32)
    for p in range(PIECES):
        for j in range(COLS // EDGE):
            dx[wide + PIECE * p : wide + PIECE * (p + 1), EDGE * j : EDGE * (j + 1)] = pieces[
                p, PIECE * j : PIECE * (j + 1), :
            ]
    for i in range(3):
        at = BLOCK * i
        du = tile_pass(dx[at : at + BLOCK + 2 * RADIUS, :], both3, ch, cl)
        sloped[at : at + BLOCK, :] = slope[at : at + BLOCK, :] * du
        lo, hi = max(at, RADIUS), min(at + BLOCK, RADIUS + ROWS)
        here = slice(lo - RADIUS, hi - RADIUS)
        grad_precip[here, :] = share[here, :] * du[lo - at : hi - at, 0:COLS]


def back_second_kernel(sloped, both4, ch, cl, grad_scaling):
    for i in range(4):
        at = EDGE * i
        r = rows_pass(sloped[at : at + EDGE + 2 * RADIUS, :], both4)
        grad_scaling[at : at + EDGE, :] = cols_pass(r, ch, cl, False)


def back_halo_kernel(
    lat_in, even, odd, slope_edge, share_edge, precip_part, scaling_part, dh, dl,
    precip_out, scaling_out, strips, square, flat, precip_edge, scaling_edge, middle, sems,
):
    wide = 2 * RADIUS
    lat = my_lat()
    top = lat == 1
    inner = slice(EDGE, COLS - EDGE)
    last = slice(COLS - EDGE, COLS)
    copies = []

    def sent(src, dst):
        copies.append(pltpu.make_async_copy(src, dst, sems.at[len(copies)]))
        copies[-1].start()

    for part, out in ((precip_part, precip_out), (scaling_part, scaling_out)):
        sent(part.at[wide : ROWS - wide, inner], out.at[wide : ROWS - wide, inner])

    fill_strips(strips, square, lat_in[...], even[...], odd[...])
    bands = dh[lat], dl[lat]
    du = smoothed(strips[...], bands)
    precip_more = share_edge[...] * du
    scaling_more = smoothed(slope_edge[...] * du, bands)
    nothing = jnp.zeros((RADIUS, COLS), F32)
    near = lax.broadcasted_iota(jnp.int32, (ROWS, EDGE), 1) < EDGE // 2

    def finished(k, part, out, edges, reach, low, high, first, final):
        flat[...] = jnp.zeros((EDGE, ROWS), F32)
        flat[0:reach, :] = low
        flat[EDGE - reach : EDGE, :] = high
        turned = jnp.transpose(flat[...])
        middle[2 * k] = part[0:wide, inner] + first[:, inner]
        middle[2 * k + 1] = part[ROWS - wide : ROWS, inner] + final[:, inner]
        sent(middle.at[2 * k], out.at[0:wide, inner])
        sent(middle.at[2 * k + 1], out.at[ROWS - wide : ROWS, inner])
        edges[:, 0:EDGE] = part[:, 0:EDGE] + jnp.where(near, turned, 0.0)
        edges[:, EDGE : 2 * EDGE] = part[:, last] + jnp.where(near, 0.0, turned)
        for q, lanes in enumerate((slice(0, EDGE), last)):
            mine = slice(EDGE * q, EDGE * (q + 1))
            edges[0:wide, mine] += first[:, lanes]
            edges[ROWS - wide : ROWS, mine] += final[:, lanes]
            sent(edges.at[:, mine], out.at[:, lanes])

    finished(
        0, precip_part, precip_out, precip_edge, RADIUS,
        precip_more[24:32, 0:COLS], precip_more[32:40, 0:COLS],
        jnp.concatenate([precip_more[RADIUS:wide, 0:COLS], nothing], axis=0),
        jnp.concatenate([nothing, precip_more[0:RADIUS, 0:COLS]], axis=0),
    )
    added = scaling_more[0:wide, 0:COLS]
    finished(
        1, scaling_part, scaling_out, scaling_edge, wide,
        scaling_more[16:32, 0:COLS], scaling_more[32:48, 0:COLS],
        jnp.where(top, added, 0.0), jnp.where(top, 0.0, added),
    )
    for copy in copies:
        copy.wait()


def in_vmem(*shapes):
    return [pltpu.VMEM(shape, F32) for shape in shapes]


def call(
    kernel, args, outs, scratch=(), scalars=0, flops=0, room=4 << 20, copies=0,
    out_hbm=False,
):
    size = sum(4 * a.size for a in args) + sum(4 * int(np.prod(o)) for o in outs)
    where = pltpu.HBM if out_hbm else pltpu.VMEM
    spaces = [
        pltpu.SMEM if k < scalars else pltpu.VMEM
        for k in range(len(args))
    ]
    sems = [pltpu.SemaphoreType.DMA((copies,))] if copies else []
    return pl.pallas_call(
        kernel,
        out_shape=[pltpu.HBM(o, F32) if out_hbm else jax.ShapeDtypeStruct(o, F32) for o in outs],
        in_specs=[pl.BlockSpec(memory_space=space) for space in spaces],
        out_specs=[pl.BlockSpec(memory_space=where)] * len(outs),
        scratch_shapes=in_vmem(*scratch) + sems,
        cost_estimate=pl.CostEstimate(flops=flops, bytes_accessed=size, transcendentals=0),
        compiler_params=pltpu.CompilerParams(vmem_limit_bytes=room),
    )(*args)


def lat_swapped(strip):
    return lax.ppermute(strip, "lat", [(0, 1), (1, 0)])


def lon_swapped(to_even, to_odd):
    count = lax.axis_size("lon")
    even = [(i, i ^ 1) for i in range(count)]
    odd = [(i, (((i - 1) % count ^ 1) + 1) % count) for i in range(count)]
    return lax.ppermute(to_even, "lon", even), lax.ppermute(to_odd, "lon", odd)


def chip_swapped(part, k):
    if k == 0:
        return part
    pairs = [(i, i ^ k) for i in range(CHIPS)]
    return lax.ppermute(part, ("hour_0", "hour_1"), pairs)


def cores_swapped(parts):
    return lax.ppermute(parts, "hour_2", [(0, 1), (1, 0)])


def per_device(precip, scaling, hour_weight, cotangent):
    rainfall = precip[0]
    incoming = scaling[0]
    upstream = cotangent[0]
    band3, band4, around = row_band(BLOCK), row_band(EDGE), col_band()
    to_lat = lat_strip(incoming, rainfall)
    lat_in = lat_swapped(to_lat)
    (partial,) = call(
        front_kernel, (incoming, band3, *around), ((TALL, WIDE),),
        scratch=((TALLER, COLS),), flops=2 * 10**9, room=14 << 20,
    )
    even, odd = lon_swapped(
        *call(lon_kernel, (incoming, rainfall, lat_in), ((STRIP, WIDE), (STRIP, WIDE)))
    )
    half = (CHIPS // 2, 2 * EDGE, EDGE)
    whole, part = (PIECES, EDGE, EDGE), (PIECES // 2, EDGE, EDGE)
    smooth, lifted = call(
        forward_kernel,
        (partial, rainfall, lat_in, even, odd, *edge_bands()),
        ((TALL, WIDE), (TALL, WIDE)),
        scratch=(
            (TALL, WIDE), (EDGE, WIDE), (48, WIDE), (EDGE, EDGE), (TALL, EDGE), (TALL, EDGE),
        ),
        flops=5 * 10**8,
        room=14 << 20,
    )

    def logged(flip, *after):
        return call(
            lambda *refs: log_kernel(flip, *refs[: 6], *refs[6 + len(after) :]),
            (hour_weight, lifted, upstream, band4, *around, *after),
            (part, part, half, half),
            scalars=1,
            flops=10**9,
            room=14 << 20,
        )

    second_odd, scaled_odd, keep_odd, give_odd = logged(True)
    given_odd = cores_swapped(give_odd)
    second_even, scaled_even, keep_even, give_even = logged(False, keep_odd)
    given_even = cores_swapped(give_even)
    arrived = []
    for keep, given, first in ((keep_odd, given_odd, 1), (keep_even, given_even, 0)):
        sums = call(pair_kernel, (keep, given), (half[1:],) * (CHIPS // 2))
        arrived += [chip_swapped(part, 2 * k + first) for k, part in enumerate(sums)]
    slope, share, slope_edge, share_edge, *factors = call(
        prepare_kernel,
        (
            hour_weight, smooth, lifted, rainfall, second_even, second_odd, scaled_even,
            scaled_odd,
        ),
        ((TALL, WIDE), (ROWS, COLS), (48, WIDE), (48, WIDE), part, part, part, part),
        scalars=1,
        room=14 << 20,
    )
    (owned,) = call(owner_kernel, tuple(arrived), (half[1:],))

    def collected(first, *after):
        parts = [chip_swapped(owned, 2 * k + first) for k in range(CHIPS // 2)]
        return call(gather_kernel, (*parts, *after), (half,))[0]

    odd_part = collected(1)
    their_odd = cores_swapped(odd_part)
    even_part = collected(0, odd_part)
    their_even = cores_swapped(even_part)
    (pieces,) = call(db_kernel, (even_part, odd_part, their_even, their_odd, *factors), (whole,))
    (to_lat,) = call(back_lat_kernel, (pieces,), ((2 * RADIUS, COLS),))
    lat_in = lat_swapped(to_lat)
    even, odd = lon_swapped(
        *call(back_lon_kernel, (pieces, lat_in), ((2 * RADIUS, WIDE), (2 * RADIUS, WIDE)))
    )
    precip_part, sloped = call(
        back_first_kernel,
        (pieces, slope, share, band3, *around),
        ((ROWS, COLS), (TALL, WIDE)),
        scratch=((TALLER, COLS),),
        flops=2 * 10**9,
        room=14 << 20,
    )
    (scaling_part,) = call(
        back_second_kernel, (sloped, band4, *around), ((ROWS, COLS),),
        flops=2 * 10**9, room=14 << 20,
    )
    grad_precip, grad_scaling = call(
        back_halo_kernel,
        (lat_in, even, odd, slope_edge, share_edge, precip_part, scaling_part, *edge_bands()),
        ((ROWS, COLS), (ROWS, COLS)),
        scratch=(
            (48, WIDE), (EDGE, EDGE), (EDGE, ROWS), (ROWS, 2 * EDGE), (ROWS, 2 * EDGE),
            (4, 2 * RADIUS, 2 * EDGE),
        ),
        flops=10**9,
        room=14 << 20,
        copies=10,
        out_hbm=True,
    )
    return (grad_precip[None], grad_scaling[None])


def solution(mesh):
    split_mesh = Mesh(
        mesh.devices.reshape(4, 2, 2, mesh.shape["lat"], mesh.shape["lon"]),
        ("hour_0", "hour_1", "hour_2", "lat", "lon"),
    )
    return jax.shard_map(
        per_device,
        mesh=split_mesh,
        in_specs=(P(HOUR, "lat", "lon"), P(HOUR, "lat", "lon"), P(HOUR), P(HOUR, "lat", "lon")),
        out_specs=(P(HOUR, "lat", "lon"), P(HOUR, "lat", "lon")),
        check_vma=False,
    )
```
